32 devices in a mesh: groups: 2 (over y), lon: 4 (over z), lat: 2 (over x), sub: 2 (over core).
Axes of the slice: x: 2, y: 2, z: 4, core: 2. Of those that a mesh axis runs over, the one named last changes fastest.
Arguments:
- tokens: bfloat16 [512, 200, 384], P(('groups', 'lat', 'lon')), parts along dimension 0, may hold values from -130 to 130, as said below
- land_bits: int32 [512, 200], P(('groups', 'lat', 'lon')), parts along dimension 0, may hold values from 0 to 1, as said below
- ocean_list: int32 [4, 128], P(('groups', 'lat')), parts along dimension 0, may hold values from 0 to 128, as said below
- w_qkv: bfloat16 [2, 3, 384, 384], P(None, None, None, 'sub'), as said below
- w_out: bfloat16 [2, 384, 384], P(None, 'sub'), may hold values from -0.3125 to 0.3125
Outputs:
- advanced: bfloat16 [512, 200, 384], P(('groups', 'lat', 'lon')), parts along dimension 0
The draws below stay inside these ranges and needn't reach their ends.
There are 2 independent parts, one for each index of `groups`. The reference program is written for one: setup_inputs(seed, part) draws one part's arguments, and reference() takes and returns one part's arrays. A program takes and returns all parts, laid end to end along the dimension named above; an argument that names none is the same for every part. Nothing has to cross between parts.
Inputs may be any that keep to these rules, and one draw needn't show every extreme that they name: `ocean_list`: each row lists its band's ocean windows in increasing order and then holds 128. A row lists at least 72 and at most 96 windows; some row lists exactly 96. In each window row of a band the listed windows form one run along longitude, which may wrap around. `land_bits`: every token of a window that its band's row of ocean_list does not list is land; in listed windows about a quarter of the tokens are land. `tokens`: finite values. `w_qkv`: entries lie within 165 / sqrt(384) in magnitude.
All inputs are finite; a program needn't handle non-finite values.
Results may differ from the reference program's by a relative error of at most 0.013.
Values may be sent and summed in bfloat16 or wider, within the bound.
No kernel may reach another device: no remote copies, remote signals or barrier semaphores. Data moves between devices by JAX's collectives and lax.ppermute only.
A program may use at most 64 MiB of HBM per device.

```python
import jax
import jax.numpy as jnp
from jax import lax

D = 384
HEADS = 12
HD = 32
HGROUPS = 2
WH = 10
WW = 20
P_SIZE = 200
LONW = 32
WROW_DEV = 4
BANDS = 2
LATW = 8
BAND_WINDOWS = 128
WINDOWS = 256
OCEAN_MOST = 96
NLAT = 80
NLON = 640


def ocean_layout(key):
    seeds = jax.random.split(jax.random.fold_in(key, 31), 4)
    shortfall = jax.random.randint(seeds[0], (BANDS,), 0, OCEAN_MOST // 4 + 1)
    fullest = jax.random.randint(seeds[1], (), 0, BANDS)
    band_index = jnp.arange(BANDS, dtype=jnp.int32)
    ocean_count = jnp.where(band_index == fullest, OCEAN_MOST, OCEAN_MOST - shortfall)
    row_index = jnp.arange(WROW_DEV, dtype=jnp.int32)[None, :]
    row_count = ocean_count[:, None] // WROW_DEV + (row_index < ocean_count[:, None] % WROW_DEV).astype(jnp.int32)
    offset = jax.random.randint(seeds[2], (BANDS, WROW_DEV, 1), 0, LONW)
    column = jnp.arange(LONW, dtype=jnp.int32)[None, None, :]
    is_ocean = (column - offset) % LONW < row_count[:, :, None]
    local = jnp.swapaxes(is_ocean, 1, 2).reshape(BANDS, BAND_WINDOWS)
    return (local, ocean_count, seeds[3])


def draw_ocean_list(key, part):
    local, ocean_count, unused = ocean_layout(key)
    window_index = jnp.broadcast_to(jnp.arange(BAND_WINDOWS, dtype=jnp.int32)[None, :], (BANDS, BAND_WINDOWS))
    ordering = jnp.where(local, window_index, window_index + BAND_WINDOWS)
    ranked = jnp.sort(ordering, axis=1)
    position = jnp.arange(BAND_WINDOWS, dtype=jnp.int32)[None, :]
    return jnp.where(position < ocean_count[:, None], ranked, BAND_WINDOWS).astype(jnp.int32)


def draw_land_bits(key, part):
    local, ocean_count, coast_key = ocean_layout(key)
    window_ocean = local.reshape(WINDOWS)
    coastal = jax.random.randint(coast_key, (WINDOWS, P_SIZE), 0, 4) == 0
    return jnp.where(window_ocean[:, None], coastal, True).astype(jnp.int32)


def draw_tokens(key, part):
    seeds = jax.random.split(jax.random.fold_in(key, 11), 1)
    drawn = jnp.clip(jax.random.normal(seeds[0], (WINDOWS, P_SIZE, D)), -6.0, 6.0)
    return drawn.astype(jnp.bfloat16)


def draw_w_qkv(key, part):
    seeds = jax.random.split(jax.random.fold_in(key, 23), 1)
    raw = jnp.clip(jax.random.normal(seeds[0], (2, 3, D, D)), -6.0, 6.0) * D ** (-0.5)
    factor = jnp.array([1.7, 1.7, 1.0], dtype=jnp.float32)[None, :, None, None]
    weights = raw * factor
    return weights.astype(jnp.bfloat16)


def levels(key, dims, shards, least, largest):
    gain, own = 1.0, jax.random.fold_in(key, 6)
    for axis_at, blocks in shards:
        draws = jnp.exp(jax.random.uniform(jax.random.fold_in(own, axis_at), (blocks,), jnp.float32, least / len(shards), largest / len(shards)))
        gain = gain * jnp.repeat(draws, dims[axis_at] // blocks).reshape([-1 if axis == axis_at else 1 for axis in range(len(dims))])
    return gain


def gaussian(key, extent, width, bound, cuts=(), kind=jnp.bfloat16):
    values = width * jax.random.normal(key, extent, jnp.float32)
    if cuts:
        values = values * levels(key, extent, cuts, -0.22, 0.18)
    return jnp.clip(values, -bound, bound).astype(kind)


def setup_inputs(seed: int = 0, part: int = 0) -> dict:
    keys = jax.random.split(jax.random.key(seed), 6)
    part_keys = jax.random.split(jax.random.fold_in(keys[5], part), 6)
    tokens = draw_tokens(jax.random.fold_in(jax.random.fold_in(keys[5], part), 71), part)
    land_bits = draw_land_bits(jax.random.fold_in(jax.random.fold_in(keys[5], part), 71), part)
    ocean_list = draw_ocean_list(jax.random.fold_in(jax.random.fold_in(keys[5], part), 71), part)
    w_qkv = draw_w_qkv(jax.random.fold_in(keys[5], 71), part)
    w_out = gaussian(keys[4], (2, D, D), D ** -0.5, 0.3125, ((1, 2),))
    return {"tokens": tokens, "land_bits": land_bits, "ocean_list": ocean_list, "w_qkv": w_qkv, "w_out": w_out}


def layer_normal(values):
    center = lax.optimization_barrier(jnp.mean(values, axis=-1, keepdims=True))
    centred = values - center
    variance = lax.optimization_barrier(jnp.mean(centred * centred, axis=-1, keepdims=True))
    return centred * lax.rsqrt(variance + 1e-05)

def rounded(values):
    return lax.optimization_barrier(values.astype(jnp.bfloat16)).astype(jnp.float32)

def window_terms(windows, land_keys, w_qkv_block, w_out_block):
    window_count = windows.shape[0]
    normed = rounded(layer_normal(windows.astype(jnp.float32)))

    def project(which_part):
        product = jnp.einsum('wpd,de->wpe', normed, w_qkv_block[which_part].astype(jnp.float32))
        return rounded(product).reshape(window_count, P_SIZE, HEADS, HD)
    query = project(0)
    keyed = project(1)
    valued = project(2)
    scores = jnp.einsum('wphe,wkhe->whpk', query, keyed) * HD ** (-0.5)
    scores = jnp.where(land_keys[:, None, None, :] > 0, -1e+30, scores)
    highest = lax.optimization_barrier(jnp.max(scores, axis=-1, keepdims=True))
    powers = jnp.exp(scores - highest)
    probs = rounded(powers / lax.optimization_barrier(jnp.sum(powers, axis=-1, keepdims=True)))
    blended = rounded(jnp.einsum('whpk,wkhe->wphe', probs, valued).reshape(window_count, P_SIZE, D))
    group_width = D // HGROUPS
    update = jnp.zeros((window_count, P_SIZE, D), jnp.float32)
    for group in range(HGROUPS):
        lower = group * group_width
        partial_value = jnp.einsum('wpe,ed->wpd', blended[:, :, lower:lower + group_width], w_out_block[lower:lower + group_width].astype(jnp.float32))
        update = update + rounded(partial_value)
    return update

def to_grid(windows):
    tail = windows.shape[2:]
    split = windows.reshape((BANDS, LONW, WROW_DEV, WH, WW) + tail)
    moved = jnp.transpose(split, (0, 2, 3, 1, 4) + tuple(range(5, 5 + len(tail))))
    return moved.reshape((NLAT, NLON) + tail)

def from_grid(image):
    tail = image.shape[2:]
    split = image.reshape((BANDS, WROW_DEV, WH, LONW, WW) + tail)
    moved = jnp.transpose(split, (0, 3, 1, 2, 4) + tuple(range(5, 5 + len(tail))))
    return moved.reshape((WINDOWS, P_SIZE) + tail)

def to_windows(image):
    tail = image.shape[2:]
    split = image.reshape((LATW, WH, LONW, WW) + tail)
    moved = jnp.swapaxes(split, 1, 2)
    return moved.reshape((LATW * LONW, P_SIZE) + tail)

def from_windows(windows):
    tail = windows.shape[2:]
    split = windows.reshape((LATW, LONW, WH, WW) + tail)
    return jnp.swapaxes(split, 1, 2).reshape((NLAT, NLON) + tail)

def apply_block(image, land, active, w_qkv_block, w_out_block):
    windows = to_windows(image)
    land_windows = to_windows(land)
    grouped = windows.reshape(LATW, LONW, P_SIZE, D)
    grouped_land = land_windows.reshape(LATW, LONW, P_SIZE)

    def inner(packed):
        return window_terms(packed[0], packed[1], w_qkv_block, w_out_block)
    updates = lax.map(inner, (grouped, grouped_land)).reshape(LATW * LONW, P_SIZE, D)
    ocean = 1.0 - land_windows.astype(jnp.float32)
    keeping = (active.reshape(LATW * LONW, 1).astype(jnp.float32) * ocean)[:, :, None]
    result = (windows.astype(jnp.float32) + updates * keeping).astype(jnp.bfloat16)
    return from_windows(result)

def reference(tokens, land_bits, ocean_list, w_qkv, w_out):
    grid = to_grid(tokens)
    land_grid = to_grid(land_bits)
    band_index = jnp.arange(BAND_WINDOWS, dtype=jnp.int32)
    listed_local = jnp.any(ocean_list[:, :, None] == band_index[None, None, :], axis=1)
    listed = jnp.swapaxes(listed_local.reshape(BANDS, LONW, WROW_DEV), 1, 2).reshape(LATW, LONW)
    first = apply_block(grid, land_grid, listed, w_qkv[0], w_out[0])
    half_rows = WH // 2
    half_cols = WW // 2
    rolled = jnp.roll(first, (-half_rows, -half_cols), axis=(0, 1))
    rolled_land = jnp.roll(land_grid, (-half_rows, -half_cols), axis=(0, 1))
    valid = jnp.broadcast_to((jnp.arange(LATW) < LATW - 1)[:, None], (LATW, LONW))
    finished = apply_block(rolled, rolled_land, valid, w_qkv[1], w_out[1])
    return from_grid(jnp.roll(finished, (half_rows, half_cols), axis=(0, 1)))
```

```python
import functools

import jax
import jax.numpy as jnp
import numpy as np
from jax import lax
from jax.experimental import pallas as pl
from jax.experimental.pallas import tpu as pltpu
from jax.sharding import PartitionSpec as P

HD = 32
WH = 10
WW = 20
T = WH * WW
ROWS = 4
TP = 208
KP = 256
REC = 224
HALF = 112
SENT = HALF + 16
NEG = -1e30
SCALE = HD**-0.5 * 1.4426950408889634
f32 = jnp.float32
bf16 = jnp.bfloat16
ANY = pl.BlockSpec(memory_space=pl.ANY)
SMEM = pl.BlockSpec(memory_space=pltpu.SMEM)
VMEM = pl.BlockSpec(memory_space=pltpu.VMEM)


def normed(x):
    centred = x - jnp.mean(x, axis=-1, keepdims=True)
    variance = jnp.mean(centred * centred, axis=-1, keepdims=True)
    return (centred * lax.rsqrt(variance + 1e-05)).astype(bf16)


def lane_masks():
    lane = lax.broadcasted_iota(jnp.int32, (1, 128), 1)
    return [jnp.where((lane >= HD * i) & (lane < HD * i + HD), 1.0, 0.0).astype(bf16) for i in range(4)]


def attention(qkv, base, bias, mixed):
    width = mixed.shape[1]
    lane = lax.broadcasted_iota(jnp.int32, (1, 128), 1)
    masks = lane_masks()
    picks = jnp.broadcast_to(jnp.where(lane == 0, 1.0, 0.0), (TP, 128)).astype(bf16)
    added = jnp.where(lax.broadcasted_iota(jnp.int32, (KP, 128), 1) == 0, bias, 0.0).astype(bf16)
    pad = jnp.zeros((KP - TP, 128), bf16)
    for g in range(width // 128):
        q = qkv[base : base + TP, 128 * g : 128 * g + 128]
        k = qkv[base : base + TP, width + 128 * g : width + 128 * g + 128]
        v = qkv[base : base + TP, 2 * width + 128 * g : 2 * width + 128 * g + 128]
        left = jnp.concatenate([q, picks], axis=1)
        probs, values = [], []
        for mask in masks:
            right = jnp.concatenate([jnp.concatenate([k * mask, pad], axis=0), added], axis=1)
            scores = lax.dot_general(left, right, (((1,), (1,)), ((), ())), preferred_element_type=f32)
            powers = jnp.exp2(scores - jnp.max(scores, axis=1, keepdims=True))
            probs.append(powers.astype(bf16))
            ones = jnp.broadcast_to(mask, (KP, 128))
            values.append(jnp.concatenate([jnp.concatenate([v * mask, pad], axis=0), ones], axis=1))
        both = jnp.dot(
            jnp.concatenate(probs, axis=1), jnp.concatenate(values, axis=0), preferred_element_type=f32
        )
        mixed[base : base + TP, 128 * g : 128 * g + 128] = (both[:, :128] / both[:, 128:]).astype(bf16)


def windows_step(count, x_at, land_rows, keeps, put, wqkv, wout, norm, qkv, mixed):
    width = wout.shape[0]
    rows = jnp.concatenate(list(land_rows) + [land_rows[0]] * (8 - count), axis=0)
    land = jnp.transpose(rows)
    for i in range(count):
        norm[i * TP : i * TP + T, :] = normed(x_at(i).astype(f32))
    query = jnp.dot(norm[...], wqkv[:, :width], preferred_element_type=f32)
    qkv[:, :width] = (query * SCALE).astype(bf16)
    qkv[:, width:] = jnp.dot(norm[...], wqkv[:, width:], preferred_element_type=f32).astype(bf16)
    for i in range(count):
        attention(qkv, i * TP, land[:, i : i + 1] * NEG, mixed)
    update = jnp.dot(mixed[...], wout[...], preferred_element_type=f32)
    for i in range(count):
        keep = (1.0 - land[:T, i : i + 1]) * keeps[i]
        put(i, (x_at(i).astype(f32) + update[i * TP : i * TP + T] * keep).astype(bf16))


def join_weights(block, own_qkv, own_out, other_qkv, other_out, buffers, wqkv, wout, sem):
    bq0, bo0, bq1, bo1 = buffers
    copies = [
        pltpu.make_async_copy(a.at[block], b, sem.at[n])
        for n, (a, b) in enumerate([(own_qkv, bq0), (own_out, bo0), (other_qkv, bq1), (other_out, bo1)])
    ]
    for c in copies:
        c.start()
    for c in copies:
        c.wait()
    half = wout.shape[0] // 2
    full = half // 128 * 128
    for part in range(3):
        at = part * 2 * half
        a, b = bq0[part], bq1[part]
        pieces = [a, b[:, full:], b[:, :full]] if full else [a, b]
        wqkv[:, at : at + 2 * half] = jnp.concatenate(pieces, axis=1)
    wout[:half] = bo0[...]
    wout[half : 2 * half - full] = bo1[full:]
    if full:
        wout[2 * half - full :] = bo1[:full]


def quarter(top, left, a, b, c, d):
    return jnp.where(top, jnp.where(left, d, c), jnp.where(left, b, a))


def token_masks(shape, dim):
    token = lax.broadcasted_iota(jnp.int32, shape, dim)
    return token < T // 2, token % WW < WW // 2


class Plan:
    def __init__(self, columns):
        self.c = c = columns
        self.low = low = (c + 1) // 2
        self.up = c > low
        last = ROWS - 1
        sent = [(0, r) for r in range(ROWS)]
        sent += [(x, 0) for x in range(1, min(low, c - 1) + 1)]
        sent += [(x, last) for x in range(max(low, 1), c)]
        self.first_a = sent
        self.first_b = [(x, r) for x in range(c) for r in range(ROWS) if (x, r) not in sent]
        self.to_left = [(0, r) for r in range(ROWS)]
        self.to_above = [(x, 0) for x in range(min(low, c - 1) + 1)]
        self.to_below = [(x, last) for x in range(low, c)]
        self.to_diag = (0, last) if self.up else (0, 0)
        self.rim = [(c - 1, r) for r in range(last)]
        self.lower = [(x, last) for x in range(low)]
        self.upper = [(x, -1) for x in range(low, c)]
        self.inner = [(x, r) for x in range(c - 1) for r in range(last)]
        self.extra = (len(self.rim) + len(self.lower)) % 2 if self.inner else 0
        self.back_right = [(c - 1, r) for r in (range(-1, last) if self.up else range(ROWS))]

    def index(self, window):
        return window[0] * ROWS + window[1]


def first_kernel(plan, which, group, d, *refs):
    windows = plan.first_a if which == 0 else plan.first_b
    tokens, land, listed, own_qkv, own_out, other_qkv, other_out = refs[:7]
    refs = refs[7:]
    if which:
        refs = refs[1:]
    out, refs = refs[0], refs[1:]
    if which == 0:
        left, above, below, diag = refs[:4]
        refs = refs[4:]
    x_in, rec, bq0, bo0, bq1, bo1, wqkv, wout, norm, qkv, mixed, sem_in, sem_out, sem_w = refs
    count = len(windows)
    start = lax.axis_index("sub") * (plan.c * ROWS)
    for j, w in enumerate(windows):
        pltpu.make_async_copy(tokens.at[start + plan.index(w)], x_in.at[j], sem_in.at[j]).start()
    join_weights(0, own_qkv, own_out, other_qkv, other_out, (bq0, bo0, bq1, bo1), wqkv, wout, sem_w)
    for i in range(group):
        norm[i * TP + TP - 16 : i * TP + TP, :] = jnp.zeros((16, d), bf16)

    for step in range(count // group):
        for i in range(group):
            j = step * group + i
            pltpu.make_async_copy(tokens.at[0], x_in.at[j], sem_in.at[j]).wait()
        at = [plan.index(windows[step * group + i]) for i in range(group)]
        rows = [land[pl.ds(start + w, 1), :] for w in at]
        keeps = [listed[start + w] for w in at]

        def put(i, value, step=step):
            rec[step * group + i, :T, :] = value

        windows_step(
            group, lambda i: x_in[step * group + i], [r[:, :KP] for r in rows], keeps, put,
            wqkv, wout, norm, qkv, mixed,
        )
        for i in range(group):
            j = step * group + i
            rec[j, TP:, :] = jnp.broadcast_to(rows[i].astype(bf16), (REC - TP, d))
            pltpu.make_async_copy(rec.at[j], out.at[at[i]], sem_out.at[j]).start()
    waits = [pltpu.make_async_copy(rec.at[j], out.at[plan.index(w)], sem_out.at[j]) for j, w in enumerate(windows)]
    if which == 0:
        slot = {w: j for j, w in enumerate(windows)}
        n = count
        more = [(rec.at[slot[w]], left.at[k]) for k, w in enumerate(plan.to_left)]
        halves = [(above, k, w, 0) for k, w in enumerate(plan.to_above)]
        halves += [(below, k, w, T - HALF + 8) for k, w in enumerate(plan.to_below)]
        halves += [(diag, 0, plan.to_diag, T - HALF + 8 if plan.up else 0)]
        for to, k, w, row in halves:
            more.append((rec.at[slot[w], pl.ds(row, HALF)], to.at[k, pl.ds(0, HALF)]))
            more.append((rec.at[slot[w], pl.ds(TP, REC - TP)], to.at[k, pl.ds(HALF, SENT - HALF)]))
        for a, b in more:
            c = pltpu.make_async_copy(a, b, sem_out.at[n])
            c.start()
            waits.append(c)
            n += 1
    for c in waits:
        c.wait()


def second_kernel(plan, which, group, d, *refs):
    first, own_qkv, own_out, other_qkv, other_out = refs[:5]
    refs = refs[5:]
    ins = []
    if which == 0:
        right, above, below, diag = refs[:4]
        refs = refs[4:]
    out, refs = refs[0], refs[1:]
    if which == 0:
        to_right, to_below, to_above, to_diag = refs[:4]
        refs = refs[4:]
    ext, res, xs, bq0, bo0, bq1, bo1, wqkv, wout, norm, qkv, mixed, sem_in, sem_out, sem_w = refs
    c, last = plan.c, ROWS - 1
    windows = plan.rim + plan.inner[: plan.extra] if which == 0 else plan.inner[plan.extra :]
    need = set()
    shifted = windows + (plan.lower + plan.upper if which == 0 else [])
    for x, r in shifted:
        need |= {(x, r), (x + 1, r), (x, r + 1), (x + 1, r + 1)}
    copies = []
    for x, r in sorted(need):
        if 0 <= r < ROWS:
            copies.append((first.at[plan.index((x, r))] if x < c else right.at[r], ext.at[x, r + 1]))
            continue
        if r == ROWS:
            src = above.at[x] if x < len(plan.to_above) else diag.at[0]
            row = 0
        else:
            src = below.at[x - plan.low] if x < c else diag.at[0]
            row = T - HALF + 8
        copies.append((src.at[pl.ds(0, HALF)], ext.at[x, r + 1, pl.ds(row, HALF)]))
        copies.append((src.at[pl.ds(HALF, SENT - HALF)], ext.at[x, r + 1, pl.ds(TP, REC - TP)]))
    for n, (a, b) in enumerate(copies):
        pltpu.make_async_copy(a, b, sem_in.at[n]).start()
    join_weights(1, own_qkv, own_out, other_qkv, other_out, (bq0, bo0, bq1, bo1), wqkv, wout, sem_w)
    for i in range(group):
        norm[i * TP + TP - 16 : i * TP + TP, :] = jnp.zeros((16, d), bf16)
    for n, (a, b) in enumerate(copies):
        pltpu.make_async_copy(a, b, sem_in.at[n]).wait()
    top, left_half = token_masks((T, d), 0)
    top_row, left_row = token_masks((1, KP), 1)
    inside_row = lax.broadcasted_iota(jnp.int32, (1, KP), 1) < T

    def gathered(x, r):
        a, b = ext[x, r + 1, :T, :].astype(f32), ext[x + 1, r + 1, :T, :].astype(f32)
        e, f = ext[x, r + 2, :T, :].astype(f32), ext[x + 1, r + 2, :T, :].astype(f32)
        return quarter(top, left_half, a, b, e, f).astype(bf16)

    def land_of(x, r):
        quads = [ext[x + i, r + 1 + j, TP : TP + 16, :KP].astype(f32)[:1] for i, j in ((0, 0), (1, 0), (0, 1), (1, 1))]
        return jnp.where(inside_row, quarter(top_row, left_row, *quads), 1.0)

    def run(at, xs_r, slots):
        rows = []
        for i in range(group):
            xs[i] = gathered(*at[i])
            rows.append(land_of(*at[i]))

        def put(i, value):
            res[slots[i]] = value

        windows_step(group, lambda i: xs[i], rows, [1.0] * group, put, wqkv, wout, norm, qkv, mixed)

    for step in range(len(windows) // group):
        at = windows[step * group : step * group + group]
        run(at, None, [step * group + i for i in range(group)])
    base = len(windows) // group * group
    tail = windows[base:]
    assert not tail or which == 0
    if which == 0:
        band, bands = lax.axis_index("lat"), lax.axis_size("lat")
        todo = [(w, None) for w in tail]
        todo += [(w, band < bands - 1) for w in plan.lower] + [(w, band > 0) for w in plan.upper]
        table = []
        count = jnp.int32(0)
        sources = []
        order = []
        for n, (w, on) in enumerate(todo):
            order.append(jnp.int32(1) if on is None else on.astype(jnp.int32))
        active = sum(order)
        place = []
        seen, unseen = jnp.int32(0), active
        for n in range(len(todo)):
            place.append(jnp.where(order[n] > 0, seen, unseen))
            seen, unseen = seen + order[n], unseen + 1 - order[n]

        def nth(k):
            x, r, s = jnp.int32(0), jnp.int32(0), jnp.int32(0)
            for n, (w, _) in enumerate(todo):
                hit = place[n] == k
                x, r, s = jnp.where(hit, w[0], x), jnp.where(hit, w[1], r), jnp.where(hit, base + n, s)
            return x, r, s

        def body(step, _):
            at = [nth(jnp.minimum(step * group + i, len(todo) - 1)) for i in range(group)]
            run([(x, r) for x, r, _ in at], None, [s for _, _, s in at])
            return 0

        lax.fori_loop(0, (active + group - 1) // group, body, 0)
        for n, (w, on) in enumerate(todo):
            if on is not None:

                @pl.when(jnp.logical_not(on))
                def _(n=n, w=w):
                    res[base + n] = gathered(*w)

    places = windows + (plan.lower + plan.upper if which == 0 else [])
    pairs = [(res.at[j], out.at[j]) for j in range(len(places))]
    if which == 0:
        slot = {w: j for j, w in enumerate(places)}
        pairs += [(res.at[slot[w]], to_right.at[k]) for k, w in enumerate(plan.back_right)]
        pairs += [(res.at[slot[w], pl.ds(0, HALF)], to_below.at[k]) for k, w in enumerate(plan.lower)]
        low = pl.ds(T - HALF + 8, T - (T - HALF + 8))
        pairs += [(res.at[slot[w], low], to_above.at[k]) for k, w in enumerate(plan.upper)]
        corner = plan.back_right[0] if plan.up else plan.back_right[-1]
        pairs += [(res.at[slot[corner], low if plan.up else pl.ds(0, HALF)], to_diag.at[0])]
    done = []
    for n, (a, b) in enumerate(pairs):
        copy = pltpu.make_async_copy(a, b, sem_out.at[n])
        copy.start()
        done.append(copy)
    for copy in done:
        copy.wait()


def place_kernel(plan, d, *refs):
    raw_c, raw_d, lefts, aboves, belows, corner = refs[:6]
    out, sent = refs[6:8]
    grid, fin, sem_in, sem_out = refs[8:]
    c, last = plan.c, ROWS - 1
    copies = []
    rim = plan.rim + plan.inner[: plan.extra] + plan.lower + plan.upper
    for j, (x, r) in enumerate(rim):
        copies.append((raw_c.at[j], grid.at[x + 1, r + 1]))
    for j, (x, r) in enumerate(plan.inner[plan.extra :]):
        copies.append((raw_d.at[j], grid.at[x + 1, r + 1]))
    for k, (_, r) in enumerate(plan.back_right):
        copies.append((lefts.at[k], grid.at[0, r + 1]))
    low = pl.ds(T - HALF + 8, T - (T - HALF + 8))
    up = pl.ds(0, HALF)
    for k, (x, _) in enumerate(plan.lower):
        copies.append((aboves.at[k], grid.at[x + 1, 0, up]))
    for k, (x, _) in enumerate(plan.upper):
        copies.append((belows.at[k], grid.at[x + 1, ROWS, low]))
    copies.append((corner.at[0], grid.at[0, ROWS, low] if plan.up else grid.at[0, 0, up]))
    for n, (a, b) in enumerate(copies):
        pltpu.make_async_copy(a, b, sem_in.at[n]).start()
    for n, (a, b) in enumerate(copies):
        pltpu.make_async_copy(a, b, sem_in.at[n]).wait()
    top, left = token_masks((T, d), 0)
    start = lax.axis_index("sub") * (c * ROWS)

    def body(w, _):
        x, r = w // ROWS, w % ROWS
        a, b = grid[x + 1, r + 1].astype(f32), grid[x, r + 1].astype(f32)
        e, f = grid[x + 1, r].astype(f32), grid[x, r].astype(f32)
        fin[w] = quarter(top, left, a, b, e, f).astype(bf16)
        pltpu.make_async_copy(fin.at[w], out.at[start + w], sem_out.at[0, w]).start()
        pltpu.make_async_copy(fin.at[w], sent.at[w], sem_out.at[1, w]).start()
        return 0

    lax.fori_loop(0, c * ROWS, body, 0)

    def finish(w, _):
        pltpu.make_async_copy(fin.at[w], out.at[start + w], sem_out.at[0, w]).wait()
        pltpu.make_async_copy(fin.at[w], sent.at[w], sem_out.at[1, w]).wait()
        return 0

    lax.fori_loop(0, c * ROWS, finish, 0)


def store_kernel(plan, got, _, out, buf, sem_in, sem_out):
    n = plan.c * ROWS
    start = (1 - lax.axis_index("sub")) * n
    for w in range(n):
        pltpu.make_async_copy(got.at[w], buf.at[w], sem_in.at[w]).start()
    for w in range(n):
        pltpu.make_async_copy(got.at[w], buf.at[w], sem_in.at[w]).wait()
        pltpu.make_async_copy(buf.at[w], out.at[start + w], sem_out.at[w]).start()
    for w in range(n):
        pltpu.make_async_copy(buf.at[w], out.at[start + w], sem_out.at[w]).wait()


def ring(value, axes, by):
    sizes = [lax.axis_size(a) for a in axes]
    total = int(np.prod(sizes))
    grid = np.arange(total).reshape(sizes)
    moved = grid
    for dim, step in enumerate(by):
        moved = np.roll(moved, -step, axis=dim)
    pairs = list(zip(grid.ravel().tolist(), moved.ravel().tolist()))
    return lax.ppermute(value, tuple(axes), pairs)


def beside(value, lat, step):
    lon, sub, lats = lax.axis_size("lon"), lax.axis_size("sub"), lax.axis_size("lat")
    ident = np.arange(lon * lats * sub).reshape(lon, lats, sub)
    line = np.transpose(ident, (1, 0, 2)).reshape(lats, lon * sub)
    axes = ("lon", "lat", "sub")
    if not lat:
        line, axes = np.arange(lon * sub)[None], ("lon", "sub")
    moved = np.roll(line, (-lat, -step), axis=(0, 1))
    return lax.ppermute(value, axes, list(zip(line.ravel().tolist(), moved.ravel().tolist())))


def call(body, name, ins, outs, scratch, alias, flops):
    params = pltpu.CompilerParams(vmem_limit_bytes=60000 * 1024)
    total = sum(int(np.prod(o.shape)) * 2 for o in outs)
    return pl.pallas_call(
        body, in_specs=ins, out_specs=[ANY] * len(outs), out_shape=outs, scratch_shapes=scratch,
        input_output_aliases=alias, compiler_params=params, name=name,
        cost_estimate=pl.CostEstimate(flops=flops, bytes_accessed=2 * total, transcendentals=0),
    )


def shards(tokens, land_bits, ocean_list, w_qkv, w_out):
    window_count, _, d = tokens.shape
    half = w_out.shape[1]
    mine = window_count // lax.axis_size("sub")
    plan = Plan(mine // ROWS)
    other_qkv, other_out = ring((w_qkv, w_out), ("sub",), (1,))
    own_ids = lax.axis_index("lon") * window_count + jnp.arange(window_count, dtype=jnp.int32)
    listed = jnp.any(ocean_list[0][None, :] == own_ids[:, None], axis=1).astype(f32)
    land = jnp.pad(land_bits.astype(f32), ((0, 0), (0, d - T)), constant_values=1.0)
    weights = (w_qkv, w_out, other_qkv, other_out)
    buffers = [
        pltpu.VMEM((3, d, half), bf16), pltpu.VMEM((half, d), bf16),
        pltpu.VMEM((3, d, half), bf16), pltpu.VMEM((half, d), bf16),
        pltpu.VMEM((d, 6 * half), bf16), pltpu.VMEM((2 * half, d), bf16),
    ]

    def shape(*s):
        return jax.ShapeDtypeStruct(s, bf16)

    def work(group):
        return [
            pltpu.VMEM((group * TP, d), bf16), pltpu.VMEM((group * TP, 6 * half), bf16),
            pltpu.VMEM((group * TP, 2 * half), bf16),
        ]

    def sems(a, b):
        return [pltpu.SemaphoreType.DMA((a,)), pltpu.SemaphoreType.DMA((b,)), pltpu.SemaphoreType.DMA((4,))]

    per_window = 600_000_000

    def first_call(which, ins, outs, alias):
        n = len(plan.first_b if which else plan.first_a)
        group = 4 if n % 4 == 0 else 2 if n % 2 == 0 else 1
        scratch = [pltpu.VMEM((n, T, d), bf16), pltpu.VMEM((n, REC, d), bf16)] + buffers + work(group) + sems(n, n + 40)
        body = functools.partial(first_kernel, plan, which, group, d)
        specs = [ANY, VMEM, SMEM] + [ANY] * (len(ins) - 3)
        return call(body, f"first_{which}", specs, outs, scratch, alias, n * per_window)(*ins)

    halves = [shape(n, SENT, d) for n in (len(plan.to_above), max(len(plan.to_below), 1), 1)]
    first, left, above, below, diag = first_call(
        0, (tokens, land, listed) + weights, [shape(mine, REC, d), shape(ROWS, REC, d)] + halves, {}
    )
    right = beside(left, 0, -1)
    from_below = ring(above, ("lat",), (-1,))
    from_above = ring(below, ("lat",), (1,)) if plan.up else below
    from_diag = beside(diag, 1 if plan.up else -1, -1)
    if plan.first_b:
        first = first_call(1, (tokens, land, listed) + weights + (first,), [shape(mine, REC, d)], {7: 0})[0]

    def second_call(which, ins, outs):
        n = outs[0].shape[0]
        group = 2
        scratch = [pltpu.VMEM((plan.c + 1, ROWS + 2, REC, d), bf16), pltpu.VMEM((n, T, d), bf16)]
        scratch += [pltpu.VMEM((group, T, d), bf16)] + buffers + work(group) + sems(80, n + 20)
        body = functools.partial(second_kernel, plan, which, group, d)
        return call(body, f"second_{which}", [ANY] * len(ins), outs, scratch, {}, n * per_window)(*ins)

    rim = len(plan.rim) + plan.extra + len(plan.lower) + len(plan.upper)
    low = T - (T - HALF + 8)
    raw_c, to_right, to_below, to_above, to_diag = second_call(
        0,
        (first,) + weights + (right, from_below, from_above, from_diag),
        [
            shape(rim, T, d), shape(ROWS, T, d), shape(len(plan.lower), HALF, d),
            shape(max(len(plan.upper), 1), low, d), shape(1, low if plan.up else HALF, d),
        ],
    )
    lefts = beside(to_right, 0, 1)
    aboves = ring(to_below, ("lat",), (1,))
    belows = ring(to_above, ("lat",), (-1,)) if plan.up else to_above
    corner = beside(to_diag, -1 if plan.up else 1, 1)
    inner = len(plan.inner) - plan.extra
    raw_d = second_call(1, (first,) + weights, [shape(inner, T, d)])[0] if inner else raw_c
    out, sent = call(
        functools.partial(place_kernel, plan, d), "place", [ANY] * 6,
        [shape(window_count, T, d), shape(mine, T, d)],
        [
            pltpu.VMEM((plan.c + 1, ROWS + 1, T, d), bf16), pltpu.VMEM((mine, T, d), bf16),
            pltpu.SemaphoreType.DMA((60,)), pltpu.SemaphoreType.DMA((2, mine)),
        ],
        {}, 1000,
    )(raw_c, raw_d, lefts, aboves, belows, corner)
    got = ring(sent, ("sub",), (1,))
    return call(
        functools.partial(store_kernel, plan), "store", [ANY, ANY], [shape(window_count, T, d)],
        [pltpu.VMEM((mine, T, d), bf16), pltpu.SemaphoreType.DMA((mine,)), pltpu.SemaphoreType.DMA((mine,))],
        {1: 0}, 1000,
    )(got, out)[0]


def solution(mesh):
    placed = (
        P(("groups", "lat", "lon"), None, None),
        P(("groups", "lat", "lon"), None),
        P(("groups", "lat"), None),
        P(None, None, None, "sub"),
        P(None, "sub", None),
    )
    return jax.shard_map(
        shards,
        mesh=mesh,
        in_specs=placed,
        out_specs=P(("groups", "lat", "lon"), None, None),
        check_vma=False,
    )
```

```python
import functools

import jax
import jax.numpy as jnp
import numpy as np
from jax import lax
from jax.experimental import pallas as pl
from jax.experimental.pallas import tpu as pltpu
from jax.sharding import PartitionSpec as P

HD = 32
WH = 10
WW = 20
T = WH * WW
ROWS = 4
TP = 208
KP = 256
LIMIT = 32
REC = 224
HALF = 112
SENT = HALF + 16
NEG = -1e30
SCALE = HD**-0.5 * 1.4426950408889634
f32 = jnp.float32
bf16 = jnp.bfloat16
NT = (((1,), (1,)), ((), ()))
HBM = pl.BlockSpec(memory_space=pltpu.HBM)
ANY = pl.BlockSpec(memory_space=pl.ANY)
VMEM = pl.BlockSpec(memory_space=pltpu.VMEM)


def normed(x):
    centred = x - jnp.mean(x, axis=-1, keepdims=True)
    variance = jnp.mean(centred * centred, axis=-1, keepdims=True)
    return (centred * lax.rsqrt(variance + 1e-05)).astype(bf16)


def blocks(pairs, load, again, land_rows, keeps, put, ready, weights, slots, heads=4, ahead=1):
    wqk, wv, wout = weights
    d = wv.shape[0]
    lane = lax.broadcasted_iota(jnp.int32, (1, 128), 1)
    masks = [jnp.where((lane >= HD * j) & (lane < HD * j + HD), 1.0, 0.0).astype(bf16) for j in range(4)]
    unit = jnp.broadcast_to(jnp.where(lane == 0, 1.0, 0.0), (TP, 128)).astype(bf16)
    ones = jnp.ones((16, TP), bf16)
    total = len(pairs)

    def before(t):
        norm, qk, values, mixed, joined, bias, land = slots[t % 2]

        def normal(i):
            norm[i * TP : i * TP + T, :] = normed(load(t, i))

        def mask():
            rows = land_rows(t)
            land[...] = jnp.transpose(jnp.concatenate(rows + [rows[0]] * 6, axis=0))
            for i in range(2):
                bias[i] = jnp.where(lane == 0, land[:TP, i : i + 1] * NEG, 0.0).astype(bf16)

        def project(at):
            wide = lax.broadcasted_iota(jnp.int32, (1, 256), 1) + at
            got = lax.dot_general(norm[...], wqk[at : at + 256], NT, preferred_element_type=f32)
            qk[:, at : at + 256] = (got * jnp.where(wide < d, SCALE, 1.0)).astype(bf16)

        def value(i):
            got = lax.dot_general(wv[...], norm[i * TP : i * TP + TP], NT, preferred_element_type=f32)
            values[i] = got.astype(bf16)

        return (
            [functools.partial(normal, i) for i in range(2)] + [mask]
            + [functools.partial(project, at) for at in range(0, 2 * d, 256)]
            + [functools.partial(value, i) for i in range(2)]
        )

    def after(t):
        norm, qk, values, mixed, joined, bias, land = slots[t % 2]
        held = {}

        def turn(i):
            joined[i * TP : i * TP + TP] = jnp.transpose(mixed[i])

        def out():
            held["update"] = jnp.dot(joined[...], wout[...], preferred_element_type=f32)

        def add(i):
            keep = (1.0 - land[:T, i : i + 1]) * keeps(t, i)
            put(t, i, (again(t, i) + held["update"][i * TP : i * TP + T] * keep).astype(bf16))

        return [functools.partial(turn, i) for i in range(2)] + [out] + [functools.partial(add, i) for i in range(2)]

    units = [
        (t, i, g, tuple(range(a, a + heads)))
        for t in range(total) for i in range(2) for g in range(d // 128) for a in range(0, 4, heads)
    ]
    per = len(units) // total
    scores, probs = {}, {}

    def score(u):
        t, i, g, hs = units[u]
        qk, bias = slots[t % 2][1], slots[t % 2][5]
        k = qk[i * TP : i * TP + TP, d + 128 * g : d + 128 * g + 128]
        q = jnp.concatenate([qk[i * TP : i * TP + TP, 128 * g : 128 * g + 128], unit], axis=1)
        b = bias[i]
        keyed = jnp.concatenate([jnp.concatenate([k * masks[j], b], axis=1) for j in hs], axis=0)
        got = lax.dot_general(keyed, q, NT, preferred_element_type=f32)
        scores[u] = [got[n * TP : n * TP + TP] for n in range(len(hs))]

    def soften(u):
        probs[u] = [
            jnp.exp2((s - jnp.max(s, axis=0, keepdims=True)).astype(bf16)) for s in scores.pop(u)
        ]

    def mix(u):
        t, i, g, hs = units[u]
        values, mixed = slots[t % 2][2], slots[t % 2][3]
        for j, p in zip(hs, probs.pop(u)):
            at = 128 * g + HD * j
            both = jnp.dot(
                jnp.concatenate([values[i, at : at + HD], ones], axis=0), p, preferred_element_type=f32
            )
            mixed[i, at : at + HD] = (both[:HD] * (1.0 / both[HD : HD + 1])).astype(bf16)

    for piece in before(0):
        piece()
    ready()
    pieces, step, place = [], 1.0, 1
    for k in range(len(units) + 2 * ahead):
        t, at = k // per, k % per
        if at == 2 * ahead:
            pieces = (after(t - 1) if t else []) + (before(t + 1) if t + 1 < total else [])
            step, place = (per - 2 * ahead) / (len(pieces) + 1), 1
        if k < len(units):
            score(k)
        if 0 <= k - ahead < len(units):
            soften(k - ahead)
        if 0 <= k - 2 * ahead:
            mix(k - 2 * ahead)
        while pieces and (at == per - 1 or at - 2 * ahead + 1 >= place * step):
            pieces.pop(0)()
            place += 1
    for piece in pieces + after(total - 1):
        piece()


def paired(windows):
    padded = list(windows) + [windows[-1]] * (len(windows) % 2)
    return [padded[n : n + 2] for n in range(0, len(padded), 2)]


def weight_copies(block, own_qkv, own_out, other_qkv, other_out, weights, sem):
    wqk, wv, wout = weights
    half = own_out.shape[1]
    pairs = []
    for n, (qkv, out) in enumerate(((own_qkv, own_out), (other_qkv, other_out))):
        for part in range(2):
            pairs.append((qkv.at[block, part], wqk.at[pl.ds((2 * part + n) * half, half)]))
        pairs.append((qkv.at[block, 2], wv.at[pl.ds(n * half, half)]))
        pairs.append((out.at[block], wout.at[pl.ds(n * half, half)]))
    return [pltpu.make_async_copy(a, b, sem.at[n]) for n, (a, b) in enumerate(pairs)]


def clear_pads(slots):
    for slot in slots:
        for i in range(2):
            slot[0][i * TP + TP - 16 : i * TP + TP, :] = jnp.zeros((16, slot[0].shape[1]), bf16)


LOW = T - HALF + 8
MID = T // 2 // 16 * 16


def merged(at, d):
    token = lax.broadcasted_iota(jnp.int32, (T, d), 0)
    left = token % WW < WW // 2
    top = token < T // 2

    def pick(below, lo, hi):
        return jnp.where(left[lo:hi], at(1, below, slice(lo, hi)), at(0, below, slice(lo, hi)))

    middle = jnp.where(top[MID:HALF], pick(1, MID, HALF), pick(0, MID, HALF))
    return jnp.concatenate([pick(1, 0, MID), middle, pick(0, HALF, T)], axis=0)


class Plan:
    def __init__(self, columns):
        self.c = c = columns
        self.low = low = (c + 1) // 2
        self.up = c > low
        last = ROWS - 1
        sent = [(0, r) for r in range(ROWS)]
        sent += [(x, 0) for x in range(1, min(low, c - 1) + 1)]
        sent += [(x, last) for x in range(max(low, 1), c)]
        self.first_a = sent
        self.first_b = [(x, r) for x in range(c) for r in range(ROWS) if (x, r) not in sent]
        self.to_left = [(0, r) for r in range(ROWS)]
        self.to_above = [(x, 0) for x in range(min(low, c - 1) + 1)]
        self.to_below = [(x, last) for x in range(low, c)]
        self.to_diag = (0, last) if self.up else (0, 0)
        self.rim = [(c - 1, r) for r in range(last)]
        self.lower = [(x, last) for x in range(low)]
        self.upper = [(x, -1) for x in range(low, c)]
        self.inner = [(x, r) for x in range(c - 1) for r in range(last)]
        self.extra = len(self.rim) % 2 if self.inner else 0
        self.some = self.rim + self.inner[: self.extra]
        self.rest = self.inner[self.extra :]
        self.back_right = [(c - 1, r) for r in (range(-1, last) if self.up else range(ROWS))]

    def index(self, window):
        return window[0] * ROWS + window[1]


def first_kernel(plan, which, d, *refs):
    windows = plan.first_b if which else plan.first_a
    tokens, land, ocean = refs[:3]
    sources, refs = refs[3:7], refs[7:]
    if which:
        refs = refs[1:]
    out, refs = refs[0], refs[1:]
    if which == 0:
        left, above, below, diag = refs[:4]
        refs = refs[4:]
    x_in, rec, bits, sem_in, sem_out, sem_w = refs[:6]
    weights, slots = refs[6:9], (refs[9:16], refs[16:23])
    pairs = paired(list(range(len(windows))))
    start = lax.axis_index("sub") * (plan.c * ROWS)
    copies = weight_copies(0, *sources, weights, sem_w)
    reads = [
        pltpu.make_async_copy(tokens.at[start + plan.index(w)], x_in.at[j], sem_in.at[j])
        for j, w in enumerate(windows)
    ]
    for copy in reads[:2] + copies + reads[2:]:
        copy.start()
    clear_pads(slots)
    bits[...] = jnp.ones(bits.shape, f32)
    bits[:, :T] = land[...].astype(f32)
    for copy in reads[:2] + copies:
        copy.wait()

    def ready():
        for copy in reads[2:]:
            copy.wait()

    def row(j):
        return bits[pl.ds(start + plan.index(windows[j]), 1), :]

    def listed(j):
        ident = lax.axis_index("lon") * (plan.c * ROWS * lax.axis_size("sub")) + start + plan.index(windows[j])
        return jnp.max(jnp.where(ocean[...] == ident, 1.0, 0.0), axis=1, keepdims=True)

    def put(t, i, value):
        rec[pairs[t][i], :T, :] = value

    def load(t, i):
        return x_in[pairs[t][i]].astype(f32)

    blocks(
        pairs, load, load, lambda t: [row(j) for j in pairs[t]], lambda t, i: listed(pairs[t][i]), put, ready,
        weights, slots,
    )
    for j in range(len(windows)):
        rec[j, TP:, : KP] = jnp.broadcast_to(row(j).astype(bf16), (REC - TP, KP))
    ends = [(rec.at[j], out.at[plan.index(w)]) for j, w in enumerate(windows)]
    if which == 0:
        slot = {w: j for j, w in enumerate(windows)}
        ends += [(rec.at[slot[w]], left.at[k]) for k, w in enumerate(plan.to_left)]
        halves = [(above, k, w, 0) for k, w in enumerate(plan.to_above)]
        halves += [(below, k, w, LOW) for k, w in enumerate(plan.to_below)]
        halves += [(diag, 0, plan.to_diag, LOW if plan.up else 0)]
        for to, k, w, at in halves:
            ends.append((rec.at[slot[w], pl.ds(at, HALF)], to.at[k, pl.ds(0, HALF)]))
            ends.append((rec.at[slot[w], pl.ds(TP, REC - TP)], to.at[k, pl.ds(HALF, SENT - HALF)]))
    ends = [pltpu.make_async_copy(a, b, sem_out.at[n]) for n, (a, b) in enumerate(ends)]
    for copy in ends:
        copy.start()
    for copy in ends:
        copy.wait()


def second_kernel(plan, which, d, *refs):
    first, sources, refs = refs[0], refs[1:5], refs[5 + which :]
    if which == 0:
        right, above, below, diag = refs[:4]
        refs = refs[4:]
    out, refs = refs[0], refs[1:]
    if which == 0:
        to_right, to_below, to_above, to_diag = refs[:4]
        refs = refs[4:]
    ext, res, kept, sem_in, sem_out, sem_w = refs[:6]
    weights, slots = refs[6:9], (refs[9:16], refs[16:23])
    c = plan.c
    windows = plan.rest if which else plan.some
    all_windows = list(windows) if which else windows + plan.lower + plan.upper
    copies, asked = [], set()
    for x, r in all_windows:
        for place in ((x, r), (x + 1, r), (x, r + 1), (x + 1, r + 1)):
            if place in asked:
                continue
            asked.add(place)
            u, v = place
            if 0 <= v < ROWS:
                copies.append((first.at[plan.index(place)] if u < c else right.at[v], ext.at[u, v + 1]))
                continue
            if v == ROWS:
                source, at = above.at[u] if u < len(plan.to_above) else diag.at[0], 0
            else:
                source, at = below.at[u - plan.low] if u < c else diag.at[0], LOW
            copies.append((source.at[pl.ds(0, HALF)], ext.at[u, v + 1, pl.ds(at, HALF)]))
            copies.append((source.at[pl.ds(HALF, SENT - HALF)], ext.at[u, v + 1, pl.ds(TP, REC - TP)]))
    reads = [pltpu.make_async_copy(a, b, sem_in.at[n]) for n, (a, b) in enumerate(copies)]
    loads = weight_copies(1, *sources, weights, sem_w)
    early = 6 if len(reads) > 6 else len(reads)
    for copy in reads[:early] + loads + reads[early:]:
        copy.start()
    clear_pads(slots)
    token = lax.broadcasted_iota(jnp.int32, (1, KP), 1)
    left_row, top_row = token % WW < WW // 2, token < T // 2
    for copy in reads[:early] + loads:
        copy.wait()

    def ready():
        for copy in reads[early:]:
            copy.wait()

    def gathered(x, r):
        return merged(lambda i, j, rows: ext[x + i, r + 1 + j, rows, :].astype(f32), d)

    def land_of(x, r):
        a, b, e, f = [
            ext[x + i, r + 1 + j, TP : TP + 16, :KP].astype(f32)[:1] for j in (0, 1) for i in (0, 1)
        ]
        return jnp.where(
            token < T, jnp.where(top_row, jnp.where(left_row, f, e), jnp.where(left_row, b, a)), 1.0
        )

    places = [(w[0], w[1], n, 1.0) for n, w in enumerate(windows)]
    base = len(windows)

    def moving(lower_set, on):
        found = []
        for j in range(len(plan.lower)):
            other = min(j, max(len(plan.upper) - 1, 0))
            x = jnp.where(lower_set, j, plan.low + other)
            r = jnp.where(lower_set, ROWS - 1, -1)
            found.append((x, r, base + jnp.where(lower_set, j, len(plan.lower) + other), on))
        return found

    band, bands = lax.axis_index("lat"), lax.axis_size("lat")
    listing = [paired(places)] if places else [[]]
    if which == 0:
        lower_set = band < bands - 1 if plan.up else band >= 0
        on = jnp.where(lower_set, band < bands - 1, band > 0).astype(f32)
        listing[0] = listing[0] + paired(moving(lower_set, on))

    def run(pairs, ready):
        def load(t, i):
            x, r, _, _ = pairs[t][i]
            value = gathered(x, r)
            kept[2 * (t % 3) + i] = value.astype(bf16)
            return value

        def again(t, i):
            return kept[2 * (t % 3) + i].astype(f32)

        def put(t, i, value):
            res[pairs[t][i][2]] = value

        blocks(
            pairs, load, again, lambda t: [land_of(x, r) for x, r, _, _ in pairs[t]], lambda t, i: pairs[t][i][3],
            put, ready, weights, slots,
        )

    run(listing[0], ready)
    if which == 0 and plan.up:
        both = (band > 0) & (band < bands - 1)
        if bands > 2:

            @pl.when(both)
            def _():
                run(paired(moving(band < 0, jnp.float32(1))), lambda: None)

        for n, (w, idle) in enumerate(
            [(w, band == bands - 1) for w in plan.lower] + [(w, band == 0) for w in plan.upper]
        ):

            @pl.when(idle)
            def _(n=n, w=w):
                res[base + n] = gathered(*w).astype(bf16)

    ends = [(res.at[j], out.at[j]) for j in range(len(all_windows))]
    if which == 0:
        slot = {w: j for j, w in enumerate(all_windows)}
        ends += [(res.at[slot[w]], to_right.at[k]) for k, w in enumerate(plan.back_right)]
        ends += [(res.at[slot[w], pl.ds(0, HALF)], to_below.at[k]) for k, w in enumerate(plan.lower)]
        tail = pl.ds(LOW, T - LOW)
        ends += [(res.at[slot[w], tail], to_above.at[k]) for k, w in enumerate(plan.upper)]
        corner = plan.back_right[0] if plan.up else plan.back_right[-1]
        ends += [(res.at[slot[corner], tail if plan.up else pl.ds(0, HALF)], to_diag.at[0])]
    ends = [pltpu.make_async_copy(a, b, sem_out.at[n]) for n, (a, b) in enumerate(ends)]
    for copy in ends:
        copy.start()
    for copy in ends:
        copy.wait()


def place_kernel(plan, which, d, *refs):
    raw_c, raw_d, lefts, aboves, belows, corner = refs[:6]
    out, grid, fin, sem_in, sem_out = refs[6 + which :]
    c = plan.c
    tail, head = pl.ds(LOW, T - LOW), pl.ds(0, HALF)
    moves = {}
    for j, (x, r) in enumerate(plan.some + plan.lower + plan.upper):
        moves[x, r] = (raw_c.at[j], grid.at[x + 1, r + 1])
    for j, (x, r) in enumerate(plan.rest):
        moves[x, r] = (raw_d.at[j], grid.at[x + 1, r + 1])
    for k, (_, r) in enumerate(plan.back_right):
        moves[-1, r] = (lefts.at[k], grid.at[0, r + 1])
    for k, (x, _) in enumerate(plan.lower):
        moves[x, -1] = (aboves.at[k], grid.at[x + 1, 0, head])
    for k, (x, _) in enumerate(plan.upper):
        moves[x, ROWS - 1] = (belows.at[k], grid.at[x + 1, ROWS, tail])
    if plan.up:
        moves[-1, ROWS - 1] = (corner.at[0], grid.at[0, ROWS, tail])
    else:
        moves[-1, -1] = (corner.at[0], grid.at[0, 0, head])
    copies = {k: pltpu.make_async_copy(*moves[k], sem_in.at[n]) for n, k in enumerate(sorted(moves))}
    for k in sorted(moves):
        copies[k].start()
    me = lax.axis_index("sub")
    start = (1 - me if which else me) * (c * ROWS)
    for x in range(-1, c):
        for r in range(-1, ROWS):
            copies[x, r].wait()
        if x < 0:
            continue

        def body(r, _, x=x):
            w = x * ROWS + r
            fin[w] = merged(
                lambda i, j, rows: grid[x + 1 - i, r + 1 - j, rows, :].astype(f32), d
            ).astype(bf16)
            pltpu.make_async_copy(fin.at[w], out.at[start + w], sem_out.at[w]).start()
            return 0

        lax.fori_loop(0, ROWS, body, 0)
    for w in range(c * ROWS):
        pltpu.make_async_copy(fin.at[w], out.at[start + w], sem_out.at[w]).wait()


def ring(value, axes, by):
    sizes = [lax.axis_size(a) for a in axes]
    total = int(np.prod(sizes))
    grid = np.arange(total).reshape(sizes)
    moved = grid
    for dim, step in enumerate(by):
        moved = np.roll(moved, -step, axis=dim)
    pairs = list(zip(grid.ravel().tolist(), moved.ravel().tolist()))
    return lax.ppermute(value, tuple(axes), pairs)


def beside(value, lat, step):
    lon, sub, lats = lax.axis_size("lon"), lax.axis_size("sub"), lax.axis_size("lat")
    ident = np.arange(lon * lats * sub).reshape(lon, lats, sub)
    line = np.transpose(ident, (1, 0, 2)).reshape(lats, lon * sub)
    axes = ("lon", "lat", "sub")
    if not lat:
        line, axes = np.arange(lon * sub)[None], ("lon", "sub")
    moved = np.roll(line, (-lat, -step), axis=(0, 1))
    return lax.ppermute(value, axes, list(zip(line.ravel().tolist(), moved.ravel().tolist())))


def call(body, name, ins, outs, scratch, alias, flops, limit):
    total = sum(int(np.prod(o.shape)) * 2 for o in outs)
    return pl.pallas_call(
        body, in_specs=ins, out_specs=[ANY] * len(outs), out_shape=outs, scratch_shapes=scratch,
        input_output_aliases=alias, name=name,
        compiler_params=pltpu.CompilerParams(vmem_limit_bytes=limit * 2**20),
        cost_estimate=pl.CostEstimate(flops=flops, bytes_accessed=2 * total, transcendentals=0),
    )


def shards(tokens, land_bits, ocean_list, w_qkv, w_out):
    window_count, _, d = tokens.shape
    mine = window_count // lax.axis_size("sub")
    plan = Plan(mine // ROWS)
    turned = jnp.swapaxes(w_qkv, 2, 3)
    other_qkv, other_out = ring((turned, w_out), ("sub",), (1,))
    weights = (turned, w_out, other_qkv, other_out)
    per_window = 600_000_000

    def shape(*s):
        return jax.ShapeDtypeStruct(s, bf16)

    def sems(*counts):
        return [pltpu.SemaphoreType.DMA((n,)) for n in counts]

    slot = [
        pltpu.VMEM((2 * TP, d), bf16), pltpu.VMEM((2 * TP, 2 * d), bf16), pltpu.VMEM((2, d, TP), bf16),
        pltpu.VMEM((2, d, TP), bf16), pltpu.VMEM((2 * TP, d), bf16), pltpu.VMEM((2, TP, 128), bf16),
        pltpu.VMEM((KP, 8), f32),
    ]
    work = [pltpu.VMEM((2 * d, d), bf16), pltpu.VMEM((d, d), bf16), pltpu.VMEM((d, d), bf16)] + slot + slot

    def first_call(which, outs, extra, alias):
        n = len(plan.first_b if which else plan.first_a)
        scratch = [pltpu.VMEM((n, T, d), bf16), pltpu.VMEM((n, REC, d), bf16), pltpu.VMEM((window_count, KP), f32)]
        scratch += sems(n, n + 40, 8) + work
        specs = [HBM, VMEM, VMEM] + [ANY] * (4 + len(extra))
        return call(
            functools.partial(first_kernel, plan, which, d), f"first_{which}", specs, outs, scratch, alias,
            n * per_window, 60,
        )(tokens, land_bits, ocean_list, *weights, *extra)

    halves = [shape(n, SENT, d) for n in (len(plan.to_above), max(len(plan.to_below), 1), 1)]
    first, left, above, below, diag = first_call(0, [shape(mine, REC, d), shape(ROWS, REC, d)] + halves, (), {})
    right = beside(left, 0, -1)
    from_below = ring(above, ("lat",), (-1,))
    from_above = ring(below, ("lat",), (1,)) if plan.up else below
    from_diag = beside(diag, 1 if plan.up else -1, -1)
    if plan.first_b:
        first = first_call(1, [shape(mine, REC, d)], (first,), {7: 0})[0]

    def second_call(which, ins, outs):
        n = outs[0].shape[0]
        scratch = [pltpu.VMEM((plan.c + 1, ROWS + 2, REC, d), bf16), pltpu.VMEM((n, T, d), bf16)]
        scratch += [pltpu.VMEM((6, T, d), bf16)] + sems(80, n + 20, 8) + work
        return call(
            functools.partial(second_kernel, plan, which, d), f"second_{which}", [ANY] * len(ins), outs, scratch,
            {}, n * per_window, LIMIT,
        )(*ins)

    rim = len(plan.some) + len(plan.lower) + len(plan.upper)
    raw_c, to_right, to_below, to_above, to_diag = second_call(
        0,
        (first,) + weights + (right, from_below, from_above, from_diag),
        [
            shape(rim, T, d), shape(ROWS, T, d), shape(len(plan.lower), HALF, d),
            shape(max(len(plan.upper), 1), T - LOW, d), shape(1, T - LOW if plan.up else HALF, d),
        ],
    )
    lefts = beside(to_right, 0, 1)
    aboves = ring(to_below, ("lat",), (1,))
    belows = ring(to_above, ("lat",), (-1,)) if plan.up else to_above
    corner = beside(to_diag, -1 if plan.up else 1, 1)
    other_c = ring(raw_c, ("sub",), (1,))
    raw_d = second_call(1, (first,) + weights + (to_diag,), [shape(len(plan.rest), T, d)])[0] if plan.rest else raw_c
    other_d = ring(raw_d, ("sub",), (1,)) if plan.rest else other_c
    here = (lefts, aboves, belows, corner)
    there = ring(here, ("sub",), (1,))

    def place_call(which, *ins):
        return call(
            functools.partial(place_kernel, plan, which, d), f"place_{which}", [ANY] * 6 + [HBM] * which,
            [shape(window_count, T, d)],
            [pltpu.VMEM((plan.c + 1, ROWS + 1, T, d), bf16), pltpu.VMEM((mine, T, d), bf16)] + sems(60, mine),
            {6: 0} if which else {}, 100_000_000, 24,
        )(*ins)[0]

    out = place_call(0, raw_c, raw_d, *here)
    return place_call(1, other_c, other_d, *there, out)


def solution(mesh):
    placed = (
        P(("groups", "lat", "lon"), None, None),
        P(("groups", "lat", "lon"), None),
        P(("groups", "lat"), None),
        P(None, None, None, "sub"),
        P(None, "sub", None),
    )
    return jax.shard_map(
        shards,
        mesh=mesh,
        in_specs=placed,
        out_specs=P(("groups", "lat", "lon"), None, None),
        check_vma=False,
    )
```

```python
import functools

import jax
import jax.numpy as jnp
import numpy as np
from jax import lax
from jax.experimental import pallas as pl
from jax.experimental.pallas import tpu as pltpu
from jax.sharding import PartitionSpec as P


HD = 32
WH = 10
WW = 20
T = WH * WW
ROWS = 4
TP = 208
KP = 256
LIMIT = 60
REC = 224
HALF = 112
SENT = HALF + 16
NEG = -1e30
SCALE = HD**-0.5 * 1.4426950408889634
f32 = jnp.float32
bf16 = jnp.bfloat16
NT = (((1,), (1,)), ((), ()))
HBM = pl.BlockSpec(memory_space=pltpu.HBM)
ANY = pl.BlockSpec(memory_space=pl.ANY)
VMEM = pl.BlockSpec(memory_space=pltpu.VMEM)


def normed(x):
    centred = x - jnp.mean(x, axis=-1, keepdims=True)
    variance = jnp.mean(centred * centred, axis=-1, keepdims=True)
    return (centred * lax.rsqrt(variance + 1e-05)).astype(bf16)


def blocks(pairs, load, again, land_rows, keeps, put, ready, weights, slots, nearly=None, heads=4, ahead=1):
    wqk, wv, wout = weights
    d = wv.shape[0]
    lane = lax.broadcasted_iota(jnp.int32, (1, 128), 1)
    masks = [jnp.where((lane >= HD * j) & (lane < HD * j + HD), 1.0, 0.0).astype(bf16) for j in range(4)]
    unit = jnp.broadcast_to(jnp.where(lane == 0, 1.0, 0.0), (TP, 128)).astype(bf16)
    ones = jnp.ones((16, TP), bf16)
    total = len(pairs)

    def before(t):
        norm, qk, values, _, _, bias, land = slots[t % 2]

        def normal(i):
            norm[i * TP : i * TP + T, :] = normed(load(t, i))

        def mask():
            rows = land_rows(t)
            land[...] = jnp.transpose(jnp.concatenate(rows + [rows[0]] * 6, axis=0))
            for i in range(2):
                bias[i] = jnp.where(lane == 0, land[:TP, i : i + 1] * NEG, 0.0).astype(bf16)

        def project(at):
            wide = lax.broadcasted_iota(jnp.int32, (1, 256), 1) + at
            got = lax.dot_general(norm[...], wqk[at : at + 256], NT, preferred_element_type=f32)
            qk[:, at : at + 256] = (got * jnp.where(wide < d, SCALE, 1.0)).astype(bf16)

        def value(i):
            got = lax.dot_general(wv[...], norm[i * TP : i * TP + TP], NT, preferred_element_type=f32)
            values[i] = got.astype(bf16)

        return (
            [functools.partial(normal, i) for i in range(2)] + [mask]
            + [functools.partial(project, at) for at in range(0, 2 * d, 256)]
            + [functools.partial(value, i) for i in range(2)]
        )

    def after(t):
        _, _, _, mixed, joined, _, land = slots[t % 2]
        held = {}

        def turn(i):
            joined[i * TP : i * TP + TP] = jnp.transpose(mixed[i])

        def out():
            held["update"] = jnp.dot(joined[...], wout[...], preferred_element_type=f32)

        def add(i):
            keep = (1.0 - land[:T, i : i + 1]) * keeps(t, i)
            put(t, i, (again(t, i) + held["update"][i * TP : i * TP + T] * keep).astype(bf16))

        return [functools.partial(turn, i) for i in range(2)] + [out] + [functools.partial(add, i) for i in range(2)]

    units = [
        (t, i, g, tuple(range(a, a + heads)))
        for t in range(total) for i in range(2) for g in range(d // 128) for a in range(0, 4, heads)
    ]
    per = len(units) // total
    scores, probs = {}, {}

    def score(u):
        t, i, g, hs = units[u]
        qk, bias = slots[t % 2][1], slots[t % 2][5]
        k = qk[i * TP : i * TP + TP, d + 128 * g : d + 128 * g + 128]
        q = jnp.concatenate([qk[i * TP : i * TP + TP, 128 * g : 128 * g + 128], unit], axis=1)
        b = bias[i]
        keyed = jnp.concatenate([jnp.concatenate([k * masks[j], b], axis=1) for j in hs], axis=0)
        got = lax.dot_general(keyed, q, NT, preferred_element_type=f32)
        scores[u] = [got[n * TP : n * TP + TP] for n in range(len(hs))]

    def soften(u):
        probs[u] = [
            jnp.exp2((s - jnp.max(s, axis=0, keepdims=True)).astype(bf16)) for s in scores.pop(u)
        ]

    def mix(u):
        t, i, g, hs = units[u]
        values, mixed = slots[t % 2][2], slots[t % 2][3]
        for j, p in zip(hs, probs.pop(u)):
            at = 128 * g + HD * j
            both = jnp.dot(
                jnp.concatenate([values[i, at : at + HD], ones], axis=0), p, preferred_element_type=f32
            )
            mixed[i, at : at + HD] = (both[:HD] * (1.0 / both[HD : HD + 1])).astype(bf16)

    for piece in before(0):
        piece()
    ready()
    pieces, step, place = [], 1.0, 1
    for k in range(len(units) + 2 * ahead):
        t, at = k // per, k % per
        if at == 2 * ahead:
            pieces = (after(t - 1) if t else []) + (before(t + 1) if t + 1 < total else [])
            step, place = (per - 2 * ahead) / (len(pieces) + 1), 1
        if k < len(units):
            score(k)
        if 0 <= k - ahead < len(units):
            soften(k - ahead)
        if 0 <= k - 2 * ahead:
            mix(k - 2 * ahead)
        while pieces and (at == per - 1 or at - 2 * ahead + 1 >= place * step):
            pieces.pop(0)()
            place += 1
    if nearly is not None:
        nearly(total - 1)
    for piece in pieces + after(total - 1):
        piece()


def paired(windows):
    padded = list(windows) + [windows[-1]] * (len(windows) % 2)
    return [padded[n : n + 2] for n in range(0, len(padded), 2)]


def weight_copies(block, own_qkv, own_out, other_qkv, other_out, weights, sem):
    wqk, wv, wout = weights
    half = own_out.shape[1]
    pairs = []
    for n, (qkv, out) in enumerate(((own_qkv, own_out), (other_qkv, other_out))):
        for part in range(2):
            pairs.append((qkv.at[block, part], wqk.at[pl.ds((2 * part + n) * half, half)]))
        pairs.append((qkv.at[block, 2], wv.at[pl.ds(n * half, half)]))
        pairs.append((out.at[block], wout.at[pl.ds(n * half, half)]))
    return [pltpu.make_async_copy(a, b, sem.at[n]) for n, (a, b) in enumerate(pairs)]


def clear_pads(slots):
    for slot in slots:
        for i in range(2):
            slot[0][i * TP + TP - 16 : i * TP + TP, :] = jnp.zeros((16, slot[0].shape[1]), bf16)


LOW = T - HALF + 8
MID = T // 2 // 16 * 16


def side_masks(left):
    token = lax.broadcasted_iota(jnp.int32, left.shape, 0)
    left[...] = jnp.where(token % WW < WW // 2, 1.0, 0.0).astype(bf16)


def merged(at, left, d):
    def pick(below, lo, hi):
        side = jnp.concatenate([left[lo:hi]] * (d // 128), axis=1) > 0.5
        return jnp.where(side, at(1, below, slice(lo, hi)), at(0, below, slice(lo, hi)))

    row = lax.broadcasted_iota(jnp.int32, (HALF - MID, d), 0) + MID
    middle = jnp.where(row < T // 2, pick(1, MID, HALF).astype(f32), pick(0, MID, HALF).astype(f32)).astype(bf16)
    return jnp.concatenate([pick(1, 0, MID), middle, pick(0, HALF, T)], axis=0)


class Plan:
    def __init__(self, columns):
        self.c = c = columns
        self.low = low = (c + 1) // 2
        self.up = c > low
        last = ROWS - 1
        sent = [(0, r) for r in range(ROWS)]
        sent += [(x, 0) for x in range(1, min(low, c - 1) + 1)]
        sent += [(x, last) for x in range(max(low, 1), c)]
        self.first_a = sent
        self.first_b = [(x, r) for x in range(c) for r in range(ROWS) if (x, r) not in sent]
        self.to_left = [(0, r) for r in range(ROWS)]
        self.to_above = [(x, 0) for x in range(min(low, c - 1) + 1)]
        self.to_below = [(x, last) for x in range(low, c)]
        self.to_diag = (0, last) if self.up else (0, 0)
        self.rim = [(c - 1, r) for r in range(last)]
        self.lower = [(x, last) for x in range(low)]
        self.upper = [(x, -1) for x in range(low, c)]
        self.inner = [(x, r) for x in range(c - 1) for r in range(last)]
        self.extra = len(self.rim) % 2 if self.inner else 0
        self.some = self.rim + self.inner[: self.extra]
        self.rest = self.inner[self.extra :]
        self.back_right = [(c - 1, r) for r in (range(-1, last) if self.up else range(ROWS))]

    def index(self, window):
        return window[0] * ROWS + window[1]


def first_kernel(plan, which, *refs):
    windows = plan.first_b if which else plan.first_a
    tokens, land, ocean = refs[:3]
    sources, refs = refs[3:7], refs[7:]
    if which:
        refs = refs[1:]
    out, refs = refs[0], refs[1:]
    if which == 0:
        left, above, below, diag = refs[:4]
        refs = refs[4:]
    x_in, rec, bits, sem_in, sem_out, sem_w = refs[:6]
    weights, slots = refs[6:9], (refs[9:16], refs[16:23])
    pairs = paired(list(range(len(windows))))
    start = lax.axis_index("sub") * (plan.c * ROWS)
    copies = weight_copies(0, *sources, weights, sem_w)
    reads = [
        pltpu.make_async_copy(tokens.at[start + plan.index(w)], x_in.at[j], sem_in.at[j])
        for j, w in enumerate(windows)
    ]
    for copy in reads[:2] + copies + reads[2:]:
        copy.start()
    clear_pads(slots)
    bits[...] = jnp.ones(bits.shape, f32)
    bits[:, :T] = land[...].astype(f32)
    for copy in reads[:2] + copies:
        copy.wait()

    def ready():
        for copy in reads[2:]:
            copy.wait()

    def row(j):
        return bits[pl.ds(start + plan.index(windows[j]), 1), :]

    def listed(j):
        ident = lax.axis_index("lon") * (plan.c * ROWS * lax.axis_size("sub")) + start + plan.index(windows[j])
        return jnp.max(jnp.where(ocean[...] == ident, 1.0, 0.0), axis=1, keepdims=True)

    def put(t, i, value):
        rec[pairs[t][i], :T, :] = value

    def load(t, i):
        return x_in[pairs[t][i]].astype(f32)

    ends = [[(rec.at[j], out.at[plan.index(w)])] for j, w in enumerate(windows)]
    if which == 0:
        slot = {w: j for j, w in enumerate(windows)}
        for k, w in enumerate(plan.to_left):
            ends[slot[w]].append((rec.at[slot[w]], left.at[k]))
        halves = [(above, k, w, 0) for k, w in enumerate(plan.to_above)]
        halves += [(below, k, w, LOW) for k, w in enumerate(plan.to_below)]
        halves += [(diag, 0, plan.to_diag, LOW if plan.up else 0)]
        for to, k, w, at in halves:
            j = slot[w]
            ends[j].append((rec.at[j, pl.ds(at, HALF)], to.at[k, pl.ds(0, HALF)]))
            ends[j].append((rec.at[j, pl.ds(TP, REC - TP)], to.at[k, pl.ds(HALF, SENT - HALF)]))
    numbers = iter(range(len(windows) + 40))
    ends = [[pltpu.make_async_copy(a, b, sem_out.at[next(numbers)]) for a, b in group] for group in ends]

    def send(lo, hi):
        for j in range(lo, hi):
            for copy in ends[j]:
                copy.start()

    for j in range(len(windows)):
        rec[j, TP:, :KP] = jnp.broadcast_to(row(j).astype(bf16), (REC - TP, KP))
    blocks(
        pairs, load, load, lambda t: [row(j) for j in pairs[t]], lambda t, i: listed(pairs[t][i]), put, ready,
        weights, slots, lambda t: send(0, 2 * t),
    )
    send(2 * (len(pairs) - 1), len(windows))
    for copy in (c for group in ends for c in group):
        copy.wait()


def second_kernel(plan, which, d, *refs):
    first, sources, refs = refs[0], refs[1:5], refs[5 + which :]
    if which == 0:
        right, above, below, diag = refs[:4]
        refs = refs[4:]
    out, refs = refs[0], refs[1:]
    if which == 0:
        to_right, to_below, to_above, to_diag = refs[:4]
        refs = refs[4:]
    ext, res, kept, left, sem_in, sem_out, sem_w = refs[:7]
    weights, slots = refs[7:10], (refs[10:17], refs[17:24])
    side_masks(left)
    c = plan.c
    windows = plan.rest if which else plan.some
    all_windows = list(windows) if which else windows + plan.lower + plan.upper
    copies, asked = [], set()
    for x, r in all_windows:
        for place in ((x, r), (x + 1, r), (x, r + 1), (x + 1, r + 1)):
            if place in asked:
                continue
            asked.add(place)
            u, v = place
            if 0 <= v < ROWS:
                copies.append((first.at[plan.index(place)] if u < c else right.at[v], ext.at[u, v + 1]))
                continue
            if v == ROWS:
                source, at = above.at[u] if u < len(plan.to_above) else diag.at[0], 0
            else:
                source, at = below.at[u - plan.low] if u < c else diag.at[0], LOW
            copies.append((source.at[pl.ds(0, HALF)], ext.at[u, v + 1, pl.ds(at, HALF)]))
            copies.append((source.at[pl.ds(HALF, SENT - HALF)], ext.at[u, v + 1, pl.ds(TP, REC - TP)]))
    reads = [pltpu.make_async_copy(a, b, sem_in.at[n]) for n, (a, b) in enumerate(copies)]
    loads = weight_copies(1, *sources, weights, sem_w)
    early = 6 if len(reads) > 6 else len(reads)
    for copy in reads[:early] + loads + reads[early:]:
        copy.start()
    clear_pads(slots)
    token = lax.broadcasted_iota(jnp.int32, (1, KP), 1)
    left_row, top_row = token % WW < WW // 2, token < T // 2
    for copy in reads[:early] + loads:
        copy.wait()

    def ready():
        for copy in reads[early:]:
            copy.wait()

    def gathered(x, r):
        return merged(lambda i, j, rows: ext[x + i, r + 1 + j, rows, :], left, d)

    def land_of(x, r):
        a, b, e, f = [
            ext[x + i, r + 1 + j, TP : TP + 16, :KP].astype(f32)[:1] for j in (0, 1) for i in (0, 1)
        ]
        return jnp.where(
            token < T, jnp.where(top_row, jnp.where(left_row, f, e), jnp.where(left_row, b, a)), 1.0
        )

    places = [(w[0], w[1], n, 1.0) for n, w in enumerate(windows)]
    base = len(windows)

    def moving(lower_set, on):
        found = []
        for j in range(len(plan.lower)):
            other = min(j, max(len(plan.upper) - 1, 0))
            x = jnp.where(lower_set, j, plan.low + other)
            r = jnp.where(lower_set, ROWS - 1, -1)
            found.append((x, r, base + jnp.where(lower_set, j, len(plan.lower) + other), on))
        return found

    ends = [(res.at[j], out.at[j]) for j in range(len(all_windows))]
    if which == 0:
        slot = {w: j for j, w in enumerate(all_windows)}
        ends += [(res.at[slot[w]], to_right.at[k]) for k, w in enumerate(plan.back_right)]
        ends += [(res.at[slot[w], pl.ds(0, HALF)], to_below.at[k]) for k, w in enumerate(plan.lower)]
        tail = pl.ds(LOW, T - LOW)
        ends += [(res.at[slot[w], tail], to_above.at[k]) for k, w in enumerate(plan.upper)]
        corner = plan.back_right[0] if plan.up else plan.back_right[-1]
        ends += [(res.at[slot[corner], tail if plan.up else pl.ds(0, HALF)], to_diag.at[0])]
    ends = [pltpu.make_async_copy(a, b, sem_out.at[n]) for n, (a, b) in enumerate(ends)]
    band, bands = lax.axis_index("lat"), lax.axis_size("lat")
    listing = [paired(places)] if places else [[]]
    if which == 0:
        lower_set = band < bands - 1 if plan.up else band >= 0
        on = jnp.where(lower_set, band < bands - 1, band > 0).astype(f32)
        listing[0] = listing[0] + paired(moving(lower_set, on))

    def nearly(t):
        for copy in ends[: 2 * t]:
            copy.start()

    def run(pairs, ready, nearly=None):
        def load(t, i):
            x, r, _, _ = pairs[t][i]
            value = gathered(x, r)
            kept[2 * (t % 3) + i] = value
            return value.astype(f32)

        def again(t, i):
            return kept[2 * (t % 3) + i].astype(f32)

        def put(t, i, value):
            res[pairs[t][i][2]] = value

        blocks(
            pairs, load, again, lambda t: [land_of(x, r) for x, r, _, _ in pairs[t]], lambda t, i: pairs[t][i][3],
            put, ready, weights, slots, nearly,
        )

    run(listing[0], ready, nearly if which else None)
    if which == 0 and plan.up:
        both = (band > 0) & (band < bands - 1)
        if bands > 2:

            @pl.when(both)
            def _():
                run(paired(moving(band < 0, jnp.float32(1))), lambda: None)

        for n, (w, idle) in enumerate(
            [(w, band == bands - 1) for w in plan.lower] + [(w, band == 0) for w in plan.upper]
        ):

            @pl.when(idle)
            def _(n=n, w=w):
                res[base + n] = gathered(*w)

    for copy in ends[2 * (len(listing[0]) - 1) if which else 0 :]:
        copy.start()
    for copy in ends:
        copy.wait()


def place_kernel(plan, which, d, *refs):
    raw_c, raw_d, lefts, aboves, belows, corner = refs[:6]
    out, grid, fin, left, sem_in, sem_out = refs[6 + which :]
    c = plan.c
    tail, head = pl.ds(LOW, T - LOW), pl.ds(0, HALF)
    moves = {}
    for j, (x, r) in enumerate(plan.some + plan.lower + plan.upper):
        moves[x, r] = (raw_c.at[j], grid.at[x + 1, r + 1])
    for j, (x, r) in enumerate(plan.rest):
        moves[x, r] = (raw_d.at[j], grid.at[x + 1, r + 1])
    for k, (_, r) in enumerate(plan.back_right):
        moves[-1, r] = (lefts.at[k], grid.at[0, r + 1])
    for k, (x, _) in enumerate(plan.lower):
        moves[x, -1] = (aboves.at[k], grid.at[x + 1, 0, head])
    for k, (x, _) in enumerate(plan.upper):
        moves[x, ROWS - 1] = (belows.at[k], grid.at[x + 1, ROWS, tail])
    if plan.up:
        moves[-1, ROWS - 1] = (corner.at[0], grid.at[0, ROWS, tail])
    else:
        moves[-1, -1] = (corner.at[0], grid.at[0, 0, head])
    copies = {k: pltpu.make_async_copy(*moves[k], sem_in.at[n]) for n, k in enumerate(sorted(moves))}
    for k in sorted(moves):
        copies[k].start()
    side_masks(left)
    me = lax.axis_index("sub")
    start = (1 - me if which else me) * (c * ROWS)
    for x in range(-1, c):
        for r in range(-1, ROWS):
            copies[x, r].wait()
        if x < 0:
            continue

        def body(r, _, x=x):
            w = x * ROWS + r
            fin[w] = merged(
                lambda i, j, rows: grid[x + 1 - i, r + 1 - j, rows, :], left, d
            )
            pltpu.make_async_copy(fin.at[w], out.at[start + w], sem_out.at[w]).start()
            return 0

        lax.fori_loop(0, ROWS, body, 0)
    for w in range(c * ROWS):
        pltpu.make_async_copy(fin.at[w], out.at[start + w], sem_out.at[w]).wait()


def ring(value, axes, by):
    sizes = [lax.axis_size(a) for a in axes]
    total = int(np.prod(sizes))
    grid = np.arange(total).reshape(sizes)
    moved = grid
    for dim, step in enumerate(by):
        moved = np.roll(moved, -step, axis=dim)
    pairs = list(zip(grid.ravel().tolist(), moved.ravel().tolist()))
    return lax.ppermute(value, tuple(axes), pairs)


def beside(value, lat, step):
    lon, sub, lats = lax.axis_size("lon"), lax.axis_size("sub"), lax.axis_size("lat")
    ident = np.arange(lon * lats * sub).reshape(lon, lats, sub)
    line = np.transpose(ident, (1, 0, 2)).reshape(lats, lon * sub)
    axes = ("lon", "lat", "sub")
    if not lat:
        line, axes = np.arange(lon * sub)[None], ("lon", "sub")
    moved = np.roll(line, (-lat, -step), axis=(0, 1))
    return lax.ppermute(value, axes, list(zip(line.ravel().tolist(), moved.ravel().tolist())))


def call(body, ins, outs, scratch, alias, flops, limit):
    total = sum(int(np.prod(o.shape)) * 2 for o in outs)
    return pl.pallas_call(
        body, in_specs=ins, out_specs=[ANY] * len(outs), out_shape=outs, scratch_shapes=scratch,
        input_output_aliases=alias,
        compiler_params=pltpu.CompilerParams(vmem_limit_bytes=limit * 2**20),
        cost_estimate=pl.CostEstimate(flops=flops, bytes_accessed=2 * total, transcendentals=0),
    )


def shards(tokens, land_bits, ocean_list, w_qkv, w_out):
    window_count, _, d = tokens.shape
    mine = window_count // lax.axis_size("sub")
    plan = Plan(mine // ROWS)
    turned = jnp.swapaxes(w_qkv, 2, 3)
    other_qkv, other_out = ring((turned, w_out), ("sub",), (1,))
    weights = (turned, w_out, other_qkv, other_out)
    per_window = 12_000_000_000

    def shape(*s):
        return jax.ShapeDtypeStruct(s, bf16)

    def sems(*counts):
        return [pltpu.SemaphoreType.DMA((n,)) for n in counts]

    slot = [
        pltpu.VMEM((2 * TP, d), bf16), pltpu.VMEM((2 * TP, 2 * d), bf16), pltpu.VMEM((2, d, TP), bf16),
        pltpu.VMEM((2, d, TP), bf16), pltpu.VMEM((2 * TP, d), bf16), pltpu.VMEM((2, TP, 128), bf16),
        pltpu.VMEM((KP, 8), f32),
    ]
    work = [pltpu.VMEM((2 * d, d), bf16), pltpu.VMEM((d, d), bf16), pltpu.VMEM((d, d), bf16)] + slot + slot

    def first_call(which, outs, extra, alias):
        n = len(plan.first_b if which else plan.first_a)
        scratch = [pltpu.VMEM((n, T, d), bf16), pltpu.VMEM((n, REC, d), bf16), pltpu.VMEM((window_count, KP), f32)]
        scratch += sems(n, n + 40, 8) + work
        specs = [HBM, VMEM, VMEM] + [ANY] * (4 + len(extra))
        return call(
            functools.partial(first_kernel, plan, which), specs, outs, scratch, alias,
            n * per_window, LIMIT,
        )(tokens, land_bits, ocean_list, *weights, *extra)

    halves = [shape(n, SENT, d) for n in (len(plan.to_above), max(len(plan.to_below), 1), 1)]
    first, left, above, below, diag = first_call(0, [shape(mine, REC, d), shape(ROWS, REC, d)] + halves, (), {})
    right = beside(left, 0, -1)
    from_below = ring(above, ("lat",), (-1,))
    from_above = ring(below, ("lat",), (1,)) if plan.up else below
    from_diag = beside(diag, 1 if plan.up else -1, -1)
    if plan.first_b:
        first = first_call(1, [shape(mine, REC, d)], (first,), {7: 0})[0]

    def second_call(which, ins, outs):
        n = outs[0].shape[0]
        scratch = [pltpu.VMEM((plan.c + 1, ROWS + 2, REC, d), bf16), pltpu.VMEM((n, T, d), bf16)]
        scratch += [pltpu.VMEM((6, T, d), bf16), pltpu.VMEM((T, 128), bf16)] + sems(80, n + 20, 8) + work
        return call(
            functools.partial(second_kernel, plan, which, d), [ANY] * len(ins), outs, scratch,
            {}, n * per_window, LIMIT,
        )(*ins)

    rim = len(plan.some) + len(plan.lower) + len(plan.upper)
    raw_c, to_right, to_below, to_above, to_diag = second_call(
        0,
        (first,) + weights + (right, from_below, from_above, from_diag),
        [
            shape(rim, T, d), shape(ROWS, T, d), shape(len(plan.lower), HALF, d),
            shape(max(len(plan.upper), 1), T - LOW, d), shape(1, T - LOW if plan.up else HALF, d),
        ],
    )
    lefts = beside(to_right, 0, 1)
    aboves = ring(to_below, ("lat",), (1,))
    belows = ring(to_above, ("lat",), (-1,)) if plan.up else to_above
    corner = beside(to_diag, -1 if plan.up else 1, 1)
    other_c = ring(raw_c, ("sub",), (1,))
    raw_d = second_call(1, (first,) + weights + (to_diag,), [shape(len(plan.rest), T, d)])[0] if plan.rest else raw_c
    other_d = ring(raw_d, ("sub",), (1,)) if plan.rest else other_c
    here = (lefts, aboves, belows, corner)
    there = ring(here, ("sub",), (1,))

    def place_call(which, *ins):
        return call(
            functools.partial(place_kernel, plan, which, d), [ANY] * 6 + [HBM] * which,
            [shape(window_count, T, d)],
            [pltpu.VMEM((plan.c + 1, ROWS + 1, T, d), bf16), pltpu.VMEM((mine, T, d), bf16), pltpu.VMEM((T, 128), bf16)] + sems(60, mine),
            {6: 0} if which else {}, 100_000_000, LIMIT,
        )(*ins)[0]

    out = place_call(0, raw_c, raw_d, *here)
    return place_call(1, other_c, other_d, *there, out)


def solution(mesh):
    placed = (
        P(("groups", "lat", "lon"), None, None),
        P(("groups", "lat", "lon"), None),
        P(("groups", "lat"), None),
        P(None, None, None, "sub"),
        P(None, "sub", None),
    )
    return jax.shard_map(
        shards,
        mesh=mesh,
        in_specs=placed,
        out_specs=P(("groups", "lat", "lon"), None, None),
        check_vma=False,
    )
```

```python
import functools

import jax
import jax.numpy as jnp
import numpy as np
from jax import lax
from jax.experimental import pallas as pl
from jax.experimental.pallas import tpu as pltpu
from jax.sharding import PartitionSpec as P


HD = 32
WH = 10
WW = 20
T = WH * WW
ROWS = 4
TP = 208
KP = 256
LIMIT = 20
BRING = 56
REC = 224
HALF = 112
SENT = HALF + 16
NEG = -1e30
SCALE = HD**-0.5 * 1.4426950408889634
f32 = jnp.float32
bf16 = jnp.bfloat16
NT = (((1,), (1,)), ((), ()))
HBM = pl.BlockSpec(memory_space=pltpu.HBM)
ANY = pl.BlockSpec(memory_space=pl.ANY)
VMEM = pl.BlockSpec(memory_space=pltpu.VMEM)


def normed(x):
    centred = x - jnp.mean(x, axis=-1, keepdims=True)
    variance = jnp.mean(centred * centred, axis=-1, keepdims=True)
    return (centred * lax.rsqrt(variance + 1e-05)).astype(bf16)


def blocks(pairs, load, again, land_rows, keeps, put, weights, slots, heads=4, ahead=1):
    wqk, wv, wout = weights
    d = wv.shape[0]
    lane = lax.broadcasted_iota(jnp.int32, (1, 128), 1)
    masks = [jnp.where((lane >= HD * j) & (lane < HD * j + HD), 1.0, 0.0).astype(bf16) for j in range(4)]
    unit = jnp.broadcast_to(jnp.where(lane == 0, 1.0, 0.0), (TP, 128)).astype(bf16)
    ones = jnp.ones((16, TP), bf16)
    total = len(pairs)

    def before(t):
        norm, qk, values, _, _, bias, land = slots[t % 2]

        def normal(i):
            norm[i * TP : i * TP + T, :] = normed(load(t, i))

        def mask():
            rows = land_rows(t)
            land[...] = jnp.transpose(jnp.concatenate(rows + [rows[0]] * 6, axis=0))
            for i in range(2):
                bias[i] = jnp.where(lane == 0, land[:TP, i : i + 1] * NEG, 0.0).astype(bf16)

        def project(at):
            wide = lax.broadcasted_iota(jnp.int32, (1, 256), 1) + at
            got = lax.dot_general(norm[...], wqk[at : at + 256], NT, preferred_element_type=f32)
            qk[:, at : at + 256] = (got * jnp.where(wide < d, SCALE, 1.0)).astype(bf16)

        def value(i):
            got = lax.dot_general(wv[...], norm[i * TP : i * TP + TP], NT, preferred_element_type=f32)
            values[i] = got.astype(bf16)

        return (
            [functools.partial(normal, i) for i in range(2)] + [mask]
            + [functools.partial(project, at) for at in range(0, 2 * d, 256)]
            + [functools.partial(value, i) for i in range(2)]
        )

    def after(t):
        _, _, _, mixed, joined, _, land = slots[t % 2]
        held = {}

        def turn(i):
            joined[i * TP : i * TP + TP] = jnp.transpose(mixed[i])

        def out():
            held["update"] = jnp.dot(joined[...], wout[...], preferred_element_type=f32)

        def add(i):
            keep = (1.0 - land[:T, i : i + 1]) * keeps(t, i)
            put(t, i, (again(t, i) + held["update"][i * TP : i * TP + T] * keep).astype(bf16))

        return [functools.partial(turn, i) for i in range(2)] + [out] + [functools.partial(add, i) for i in range(2)]

    units = [
        (t, i, g, tuple(range(a, a + heads)))
        for t in range(total) for i in range(2) for g in range(d // 128) for a in range(0, 4, heads)
    ]
    per = len(units) // total
    scores, probs = {}, {}

    def score(u):
        t, i, g, hs = units[u]
        qk, bias = slots[t % 2][1], slots[t % 2][5]
        k = qk[i * TP : i * TP + TP, d + 128 * g : d + 128 * g + 128]
        q = jnp.concatenate([qk[i * TP : i * TP + TP, 128 * g : 128 * g + 128], unit], axis=1)
        b = bias[i]
        keyed = jnp.concatenate([jnp.concatenate([k * masks[j], b], axis=1) for j in hs], axis=0)
        got = lax.dot_general(keyed, q, NT, preferred_element_type=f32)
        scores[u] = [got[n * TP : n * TP + TP] for n in range(len(hs))]

    def soften(u):
        probs[u] = [
            jnp.exp2((s - jnp.max(s, axis=0, keepdims=True)).astype(bf16)) for s in scores.pop(u)
        ]

    def mix(u):
        t, i, g, hs = units[u]
        values, mixed = slots[t % 2][2], slots[t % 2][3]
        for j, p in zip(hs, probs.pop(u)):
            at = 128 * g + HD * j
            both = jnp.dot(
                jnp.concatenate([values[i, at : at + HD], ones], axis=0), p, preferred_element_type=f32
            )
            mixed[i, at : at + HD] = (both[:HD] * (1.0 / both[HD : HD + 1])).astype(bf16)

    for piece in before(0):
        piece()
    pieces, step, place = [], 1.0, 1
    for k in range(len(units) + 2 * ahead):
        t, at = k // per, k % per
        if at == 2 * ahead:
            pieces = (after(t - 1) if t else []) + (before(t + 1) if t + 1 < total else [])
            step, place = (per - 2 * ahead) / (len(pieces) + 1), 1
        if k < len(units):
            score(k)
        if 0 <= k - ahead < len(units):
            soften(k - ahead)
        if 0 <= k - 2 * ahead:
            mix(k - 2 * ahead)
        while pieces and (at == per - 1 or at - 2 * ahead + 1 >= place * step):
            pieces.pop(0)()
            place += 1
    for piece in pieces + after(total - 1):
        piece()


def paired(windows):
    padded = list(windows) + [windows[-1]] * (len(windows) % 2)
    return [padded[n : n + 2] for n in range(0, len(padded), 2)]


def join_weights(block, sources, weights):
    wqk, wv, wout = weights
    for n in range(2):
        qkv, out = sources[2 * n : 2 * n + 2]
        half = out.shape[1]
        rows = slice(n * half, n * half + half)
        for part in range(2):
            wqk[part * 2 * half + n * half : part * 2 * half + n * half + half] = qkv[block, part]
        wv[rows] = qkv[block, 2]
        wout[rows] = out[block]


def clear_pads(slots):
    for slot in slots:
        for i in range(2):
            slot[0][i * TP + TP - 16 : i * TP + TP, :] = jnp.zeros((16, slot[0].shape[1]), bf16)


LOW = T - HALF + 8
MID = T // 2 // 16 * 16


def side_masks(left):
    token = lax.broadcasted_iota(jnp.int32, left.shape, 0)
    left[...] = jnp.where(token % WW < WW // 2, 1.0, 0.0).astype(bf16)


def merged(at, left, d):
    def pick(below, lo, hi):
        side = jnp.concatenate([left[lo:hi]] * (d // 128), axis=1) > 0.5
        return jnp.where(side, at(1, below, slice(lo, hi)), at(0, below, slice(lo, hi)))

    row = lax.broadcasted_iota(jnp.int32, (HALF - MID, d), 0) + MID
    middle = jnp.where(row < T // 2, pick(1, MID, HALF).astype(f32), pick(0, MID, HALF).astype(f32)).astype(bf16)
    return jnp.concatenate([pick(1, 0, MID), middle, pick(0, HALF, T)], axis=0)


class Plan:
    def __init__(self, columns):
        self.c = c = columns
        self.low = low = (c + 1) // 2
        self.up = c > low
        last = ROWS - 1
        sent = [(0, r) for r in range(ROWS)]
        sent += [(x, 0) for x in range(1, min(low, c - 1) + 1)]
        sent += [(x, last) for x in range(max(low, 1), c)]
        self.first_a = sent
        self.first_b = [(x, r) for x in range(c) for r in range(ROWS) if (x, r) not in sent]
        self.to_left = [(0, r) for r in range(ROWS)]
        self.to_above = [(x, 0) for x in range(min(low, c - 1) + 1)]
        self.to_below = [(x, last) for x in range(low, c)]
        self.to_diag = (0, last) if self.up else (0, 0)
        self.rim = [(c - 1, r) for r in range(last)]
        self.lower = [(x, last) for x in range(low)]
        self.upper = [(x, -1) for x in range(low, c)]
        self.inner = [(x, r) for x in range(c - 1) for r in range(last)]
        self.extra = len(self.rim) % 2 if self.inner else 0
        self.some = self.rim + self.inner[: self.extra]
        self.rest = self.inner[self.extra :]
        self.back_right = [(c - 1, r) for r in (range(-1, last) if self.up else range(ROWS))]

    def index(self, window):
        return window[0] * ROWS + window[1]


def bring_kernel(plan, *refs):
    sources, ends, sem = refs[:5], refs[5:10], refs[10]
    start = lax.axis_index("sub") * (plan.c * ROWS)
    pairs = [(sources[0].at[pl.ds(start, plan.c * ROWS)], ends[0])] + list(zip(sources[1:], ends[1:]))
    copies = [pltpu.make_async_copy(a, b, sem.at[n]) for n, (a, b) in enumerate(pairs)]
    for copy in copies:
        copy.start()
    for copy in copies:
        copy.wait()


def first_kernel(plan, which, *refs):
    windows = plan.first_b if which else plan.first_a
    tokens, land, ocean = refs[:3]
    sources, refs = refs[3:7], refs[7:]
    out, refs = refs[0], refs[1:]
    if which == 0:
        left, above, below, diag = refs[:4]
        refs = refs[4:]
    bits, weights, slots = refs[0], refs[1:4], (refs[4:11], refs[11:18])
    pairs = paired(list(range(len(windows))))
    start = lax.axis_index("sub") * (plan.c * ROWS)
    clear_pads(slots)
    bits[...] = jnp.ones(bits.shape, f32)
    bits[:, :T] = land[...].astype(f32)
    join_weights(0, sources, weights)

    def row(j):
        return bits[pl.ds(start + plan.index(windows[j]), 1), :]

    def listed(j):
        ident = lax.axis_index("lon") * (plan.c * ROWS * lax.axis_size("sub")) + start + plan.index(windows[j])
        return jnp.max(jnp.where(ocean[...] == ident, 1.0, 0.0), axis=1, keepdims=True)

    def put(t, i, value):
        j = pairs[t][i]
        w = windows[j]
        bottom = jnp.broadcast_to(row(j).astype(bf16), (REC - TP, KP))
        ends = [(out, j, 0)]
        if which == 0:
            ends += [(left, k, 0) for k, v in enumerate(plan.to_left) if v == w]
        for to, k, _ in ends:
            to[k, :T, :] = value
            to[k, TP:, :KP] = bottom
        if which == 0:
            halves = [(above, k, 0) for k, v in enumerate(plan.to_above) if v == w]
            halves += [(below, k, LOW) for k, v in enumerate(plan.to_below) if v == w]
            if w == plan.to_diag:
                halves.append((diag, 0, LOW if plan.up else 0))
            for to, k, at in halves:
                end = min(at + HALF, T)
                to[k, : end - at, :] = value[at:end]
                to[k, HALF:, :KP] = bottom[: SENT - HALF]

    def load(t, i):
        return tokens[plan.index(windows[pairs[t][i]])].astype(f32)

    blocks(
        pairs, load, load, lambda t: [row(j) for j in pairs[t]], lambda t, i: listed(pairs[t][i]), put, weights, slots
    )


def second_kernel(plan, which, d, *refs):
    firsts = refs[: 2 if plan.first_b else 1]
    refs = refs[len(firsts) :]
    sources, refs = refs[:4], refs[4 + which :]
    if which == 0:
        right, above, below, diag = refs[:4]
        refs = refs[4:]
    out, refs = refs[0], refs[1:]
    if which == 0:
        to_right, to_below, to_above, to_diag = refs[:4]
        refs = refs[4:]
    kept, left = refs[:2]
    weights, slots = refs[2:5], (refs[5:12], refs[12:19])
    side_masks(left)
    clear_pads(slots)
    join_weights(1, sources, weights)
    c = plan.c
    windows = plan.rest if which else plan.some
    all_windows = list(windows) if which else windows + plan.lower + plan.upper

    def record(x, r):
        if r == ROWS:
            return (above, x, 0, HALF) if x < len(plan.to_above) else (diag, 0, 0, HALF)
        if r < 0:
            return (below, x - plan.low, LOW, HALF) if x < c else (diag, 0, LOW, HALF)
        if x == c:
            return right, r, 0, TP
        if (x, r) in plan.first_a:
            return firsts[0], plan.first_a.index((x, r)), 0, TP
        return firsts[1], plan.first_b.index((x, r)), 0, TP

    token = lax.broadcasted_iota(jnp.int32, (1, KP), 1)
    left_row, top_row = token % WW < WW // 2, token < T // 2

    def gathered(x, r):
        def at(i, j, rows):
            ref, k, base, _ = record(x + i, r + j)
            return ref[k, rows.start - base : rows.stop - base, :]

        return merged(at, left, d)

    def land_of(x, r):
        a, b, e, f = [
            ref[k, at : at + 16, :KP].astype(f32)[:1]
            for ref, k, _, at in (record(x + i, r + j) for j in (0, 1) for i in (0, 1))
        ]
        return jnp.where(
            token < T, jnp.where(top_row, jnp.where(left_row, f, e), jnp.where(left_row, b, a)), 1.0
        )

    def store(n, value):
        out[n] = value
        if which:
            return
        w = all_windows[n]
        if w in plan.back_right:
            to_right[plan.back_right.index(w)] = value
        if w in plan.lower:
            to_below[plan.lower.index(w)] = value[:HALF]
        if w in plan.upper:
            to_above[plan.upper.index(w)] = value[LOW:]
        if w == (plan.back_right[0] if plan.up else plan.back_right[-1]):
            to_diag[0] = value[LOW:] if plan.up else value[:HALF]

    band, bands = lax.axis_index("lat"), lax.axis_size("lat")
    base = len(windows)
    lower_set = band < bands - 1 if plan.up else band >= 0
    on = jnp.where(lower_set, band < bands - 1, band > 0).astype(f32)

    def either(a, b):
        return jnp.where(lower_set, a.astype(f32), b.astype(f32)).astype(a.dtype)

    def window(place):
        if place[0] != "set":
            return gathered(*place)
        j = place[1]
        low = gathered(*plan.lower[j])
        return either(low, gathered(*plan.upper[min(j, len(plan.upper) - 1)])) if plan.up else low

    def land(place):
        if place[0] != "set":
            return land_of(*place)
        j = place[1]
        low = land_of(*plan.lower[j])
        return either(low, land_of(*plan.upper[min(j, len(plan.upper) - 1)])) if plan.up else low

    def finish(place, value):
        if place[0] != "set":
            return store(all_windows.index(place), value)
        j = place[1]
        if not plan.up:
            return store(base + j, value)
        store(base + j, either(value, gathered(*plan.lower[j])))
        if j < len(plan.upper):
            store(base + len(plan.lower) + j, either(gathered(*plan.upper[j]), value))

    def run(places, keep):
        pairs = paired(places)

        def load(t, i):
            value = window(pairs[t][i])
            kept[2 * (t % 3) + i] = value
            return value.astype(f32)

        def again(t, i):
            return kept[2 * (t % 3) + i].astype(f32)

        blocks(
            pairs, load, again, lambda t: [land(p) for p in pairs[t]], lambda t, i: keep(pairs[t][i]),
            lambda t, i, value: finish(pairs[t][i], value), weights, slots,
        )

    moving = [] if which else [("set", j) for j in range(len(plan.lower))]
    run(list(windows) + moving, lambda place: on if place[0] == "set" else 1.0)
    if which == 0 and plan.up and bands > 2:

        @pl.when((band > 0) & (band < bands - 1))
        def _():
            run(plan.upper, lambda place: 1.0)


def place_kernel(plan, which, d, *refs):
    raw_c, raw_d, lefts, aboves, belows, corner = refs[:6]
    out, fin, left, sem_out = refs[6 + which :]
    c = plan.c
    side_masks(left)
    where = {}
    for j, w in enumerate(plan.some + plan.lower + plan.upper):
        where[w] = (raw_c, j, 0)
    for j, w in enumerate(plan.rest):
        where[w] = (raw_d, j, 0)
    for k, (_, r) in enumerate(plan.back_right):
        where[-1, r] = (lefts, k, 0)
    for k, (x, _) in enumerate(plan.lower):
        where[x, -1] = (aboves, k, 0)
    for k, (x, _) in enumerate(plan.upper):
        where[x, ROWS - 1] = (belows, k, LOW)
    where[(-1, ROWS - 1) if plan.up else (-1, -1)] = (corner, 0, LOW if plan.up else 0)
    me = lax.axis_index("sub")
    start = (1 - me if which else me) * (c * ROWS)
    copies = []
    for x in range(c):
        for r in range(ROWS):
            w = x * ROWS + r

            def at(i, j, rows, x=x, r=r):
                ref, k, base = where[x - i, r - j]
                return ref[k, rows.start - base : rows.stop - base, :]

            fin[w] = merged(at, left, d)
            copies.append(pltpu.make_async_copy(fin.at[w], out.at[start + w], sem_out.at[w]))
            copies[-1].start()
    for copy in copies:
        copy.wait()


def ring(value, axes, by):
    sizes = [lax.axis_size(a) for a in axes]
    total = int(np.prod(sizes))
    grid = np.arange(total).reshape(sizes)
    moved = grid
    for dim, step in enumerate(by):
        moved = np.roll(moved, -step, axis=dim)
    pairs = list(zip(grid.ravel().tolist(), moved.ravel().tolist()))
    return lax.ppermute(value, tuple(axes), pairs)


def beside(value, lat, step):
    lon, sub, lats = lax.axis_size("lon"), lax.axis_size("sub"), lax.axis_size("lat")
    ident = np.arange(lon * lats * sub).reshape(lon, lats, sub)
    line = np.transpose(ident, (1, 0, 2)).reshape(lats, lon * sub)
    axes = ("lon", "lat", "sub")
    if not lat:
        line, axes = np.arange(lon * sub)[None], ("lon", "sub")
    moved = np.roll(line, (-lat, -step), axis=(0, 1))
    return lax.ppermute(value, axes, list(zip(line.ravel().tolist(), moved.ravel().tolist())))


def call(body, ins, outs, scratch, alias, flops, limit, where):
    total = sum(int(np.prod(o.shape)) * 2 for o in outs)
    return pl.pallas_call(
        body, in_specs=ins, out_specs=[where] * len(outs), out_shape=outs, scratch_shapes=scratch,
        input_output_aliases=alias,
        compiler_params=pltpu.CompilerParams(vmem_limit_bytes=limit * 2**20),
        cost_estimate=pl.CostEstimate(flops=flops, bytes_accessed=2 * total, transcendentals=0),
    )


def shards(tokens, land_bits, ocean_list, w_qkv, w_out):
    window_count, _, d = tokens.shape
    mine = window_count // lax.axis_size("sub")
    plan = Plan(mine // ROWS)
    turned = jnp.swapaxes(w_qkv, 2, 3)
    other_qkv, other_out = ring((turned, w_out), ("sub",), (1,))
    per_window = 12_000_000_000

    def shape(*s):
        return jax.ShapeDtypeStruct(s, bf16)

    def like(a):
        return jax.ShapeDtypeStruct(a.shape, a.dtype)

    own = call(
        functools.partial(bring_kernel, plan), [ANY] * 5,
        [shape(mine, T, d), like(land_bits), like(ocean_list), like(turned), like(w_out)],
        [pltpu.SemaphoreType.DMA((5,))], {}, 1_000_000, BRING, VMEM,
    )(tokens, land_bits, ocean_list, turned, w_out)
    weights = (own[3], own[4], other_qkv, other_out)
    slot = [
        pltpu.VMEM((2 * TP, d), bf16), pltpu.VMEM((2 * TP, 2 * d), bf16), pltpu.VMEM((2, d, TP), bf16),
        pltpu.VMEM((2, d, TP), bf16), pltpu.VMEM((2 * TP, d), bf16), pltpu.VMEM((2, TP, 128), bf16),
        pltpu.VMEM((KP, 8), f32),
    ]
    work = [pltpu.VMEM((2 * d, d), bf16), pltpu.VMEM((d, d), bf16), pltpu.VMEM((d, d), bf16)] + slot + slot

    def first_call(which, outs):
        n = len(plan.first_b if which else plan.first_a)
        return call(
            functools.partial(first_kernel, plan, which), [VMEM] * 7, outs,
            [pltpu.VMEM((window_count, KP), f32)] + work, {}, n * per_window, LIMIT, VMEM,
        )(*own[:3], *weights)

    halves = [shape(n, SENT, d) for n in (len(plan.to_above), max(len(plan.to_below), 1), 1)]
    first_a, left, above, below, diag = first_call(
        0, [shape(len(plan.first_a), REC, d), shape(ROWS, REC, d)] + halves
    )
    right = beside(left, 0, -1)
    from_below = ring(above, ("lat",), (-1,))
    from_above = ring(below, ("lat",), (1,)) if plan.up else below
    from_diag = beside(diag, 1 if plan.up else -1, -1)
    firsts = (first_a,)
    if plan.first_b:
        firsts += tuple(first_call(1, [shape(len(plan.first_b), REC, d)]))

    def second_call(which, ins, outs):
        scratch = [pltpu.VMEM((6, T, d), bf16), pltpu.VMEM((T, 128), bf16)] + work
        return call(
            functools.partial(second_kernel, plan, which, d), [VMEM] * len(ins), outs, scratch,
            {}, outs[0].shape[0] * per_window, LIMIT, VMEM,
        )(*ins)

    rim = len(plan.some) + len(plan.lower) + len(plan.upper)
    raw_c, to_right, to_below, to_above, to_diag = second_call(
        0,
        firsts + weights + (right, from_below, from_above, from_diag),
        [
            shape(rim, T, d), shape(ROWS, T, d), shape(len(plan.lower), HALF, d),
            shape(max(len(plan.upper), 1), T - LOW, d), shape(1, T - LOW if plan.up else HALF, d),
        ],
    )
    lefts = beside(to_right, 0, 1)
    aboves = ring(to_below, ("lat",), (1,))
    belows = ring(to_above, ("lat",), (-1,)) if plan.up else to_above
    corner = beside(to_diag, -1 if plan.up else 1, 1)
    other_c = ring(raw_c, ("sub",), (1,))
    raw_d = raw_c
    if plan.rest:
        raw_d = second_call(1, firsts + weights + (to_diag,), [shape(len(plan.rest), T, d)])[0]
    other_d = ring(raw_d, ("sub",), (1,)) if plan.rest else other_c
    here = (lefts, aboves, belows, corner)
    there = ring(here, ("sub",), (1,))

    def place_call(which, *ins):
        return call(
            functools.partial(place_kernel, plan, which, d), [VMEM] * 6 + [HBM] * which,
            [shape(window_count, T, d)],
            [pltpu.VMEM((mine, T, d), bf16), pltpu.VMEM((T, 128), bf16), pltpu.SemaphoreType.DMA((mine,))],
            {6: 0} if which else {}, 100_000_000, LIMIT, HBM,
        )(*ins)[0]

    out = place_call(0, raw_c, raw_d, *here)
    return place_call(1, other_c, other_d, *there, out)


def solution(mesh):
    placed = (
        P(("groups", "lat", "lon"), None, None),
        P(("groups", "lat", "lon"), None),
        P(("groups", "lat"), None),
        P(None, None, None, "sub"),
        P(None, "sub", None),
    )
    return jax.shard_map(
        shards,
        mesh=mesh,
        in_specs=placed,
        out_specs=P(("groups", "lat", "lon"), None, None),
        check_vma=False,
    )
```

```python
import functools

import jax
import jax.numpy as jnp
import numpy as np
from jax import lax
from jax.experimental import pallas as pl
from jax.experimental.pallas import tpu as pltpu
from jax.sharding import PartitionSpec as P


HD = 32
WH = 10
WW = 20
T = WH * WW
ROWS = 4
TP = 208
KP = 256
LIMIT = 20
BRING = 48
REC = 224
HALF = 112
SENT = HALF + 16
NEG = -1e30
SCALE = HD**-0.5 * 1.4426950408889634
f32 = jnp.float32
bf16 = jnp.bfloat16
NT = (((1,), (1,)), ((), ()))
HBM = pl.BlockSpec(memory_space=pltpu.HBM)
ANY = pl.BlockSpec(memory_space=pl.ANY)
VMEM = pl.BlockSpec(memory_space=pltpu.VMEM)


def normed(x):
    centred = x - jnp.mean(x, axis=-1, keepdims=True)
    variance = jnp.mean(centred * centred, axis=-1, keepdims=True)
    return (centred * lax.rsqrt(variance + 1e-05)).astype(bf16)


def blocks(pairs, load, again, land_rows, keeps, put, weights, slots, heads=4, ahead=1):
    wqk, wv, wout = weights
    d = wv.shape[0]
    lane = lax.broadcasted_iota(jnp.int32, (1, 128), 1)
    masks = [jnp.where((lane >= HD * j) & (lane < HD * j + HD), 1.0, 0.0).astype(bf16) for j in range(4)]
    unit = jnp.broadcast_to(jnp.where(lane == 0, 1.0, 0.0), (TP, 128)).astype(bf16)
    ones = jnp.ones((16, TP), bf16)
    total = len(pairs)

    def before(t):
        norm, qk, values, _, _, bias, land = slots[t % 2]

        def normal(i):
            norm[i * TP : i * TP + T, :] = normed(load(t, i))

        def mask():
            rows = land_rows(t)
            land[...] = jnp.transpose(jnp.concatenate(rows + [rows[0]] * 6, axis=0))
            for i in range(2):
                bias[i] = jnp.where(lane == 0, land[:TP, i : i + 1] * NEG, 0.0).astype(bf16)

        def project(at):
            wide = lax.broadcasted_iota(jnp.int32, (1, 256), 1) + at
            got = lax.dot_general(norm[...], wqk[at : at + 256], NT, preferred_element_type=f32)
            qk[:, at : at + 256] = (got * jnp.where(wide < d, SCALE, 1.0)).astype(bf16)

        def value(i):
            got = lax.dot_general(wv[...], norm[i * TP : i * TP + TP], NT, preferred_element_type=f32)
            values[i] = got.astype(bf16)

        return (
            [functools.partial(normal, i) for i in range(2)] + [mask]
            + [functools.partial(project, at) for at in range(0, 2 * d, 256)]
            + [functools.partial(value, i) for i in range(2)]
        )

    def after(t):
        _, _, _, mixed, joined, _, land = slots[t % 2]
        held = {}

        def turn(i):
            joined[i * TP : i * TP + TP] = jnp.transpose(mixed[i])

        def out():
            held["update"] = jnp.dot(joined[...], wout[...], preferred_element_type=f32)

        def add(i):
            keep = (1.0 - land[:T, i : i + 1]) * keeps(t, i)
            put(t, i, (again(t, i) + held["update"][i * TP : i * TP + T] * keep).astype(bf16))

        return [functools.partial(turn, i) for i in range(2)] + [out] + [functools.partial(add, i) for i in range(2)]

    units = [
        (t, i, g, tuple(range(a, a + heads)))
        for t in range(total) for i in range(2) for g in range(d // 128) for a in range(0, 4, heads)
    ]
    per = len(units) // total
    scores, probs = {}, {}

    def score(u):
        t, i, g, hs = units[u]
        qk, bias = slots[t % 2][1], slots[t % 2][5]
        k = qk[i * TP : i * TP + TP, d + 128 * g : d + 128 * g + 128]
        q = jnp.concatenate([qk[i * TP : i * TP + TP, 128 * g : 128 * g + 128], unit], axis=1)
        b = bias[i]
        keyed = jnp.concatenate([jnp.concatenate([k * masks[j], b], axis=1) for j in hs], axis=0)
        got = lax.dot_general(keyed, q, NT, preferred_element_type=f32)
        scores[u] = [got[n * TP : n * TP + TP] for n in range(len(hs))]

    def soften(u):
        probs[u] = [
            jnp.exp2((s - jnp.max(s, axis=0, keepdims=True)).astype(bf16)) for s in scores.pop(u)
        ]

    def mix(u):
        t, i, g, hs = units[u]
        values, mixed = slots[t % 2][2], slots[t % 2][3]
        for j, p in zip(hs, probs.pop(u)):
            at = 128 * g + HD * j
            both = jnp.dot(
                jnp.concatenate([values[i, at : at + HD], ones], axis=0), p, preferred_element_type=f32
            )
            mixed[i, at : at + HD] = (both[:HD] * (1.0 / both[HD : HD + 1])).astype(bf16)

    for piece in before(0):
        piece()
    pieces, step, place = [], 1.0, 1
    for k in range(len(units) + 2 * ahead):
        t, at = k // per, k % per
        if at == 2 * ahead:
            pieces = (after(t - 1) if t else []) + (before(t + 1) if t + 1 < total else [])
            step, place = (per - 2 * ahead) / (len(pieces) + 1), 1
        if k < len(units):
            score(k)
        if 0 <= k - ahead < len(units):
            soften(k - ahead)
        if 0 <= k - 2 * ahead:
            mix(k - 2 * ahead)
        while pieces and (at == per - 1 or at - 2 * ahead + 1 >= place * step):
            pieces.pop(0)()
            place += 1
    for piece in pieces + after(total - 1):
        piece()


def paired(windows):
    padded = list(windows) + [windows[-1]] * (len(windows) % 2)
    return [padded[n : n + 2] for n in range(0, len(padded), 2)]


def join_weights(block, sources, weights):
    wqk, wv, wout = weights
    for n in range(2):
        qkv, out = sources[2 * n : 2 * n + 2]
        half = out.shape[1]
        rows = slice(n * half, n * half + half)
        for part in range(2):
            wqk[part * 2 * half + n * half : part * 2 * half + n * half + half] = qkv[block, part]
        wv[rows] = qkv[block, 2]
        wout[rows] = out[block]


def clear_pads(slots):
    for slot in slots:
        for i in range(2):
            slot[0][i * TP + TP - 16 : i * TP + TP, :] = jnp.zeros((16, slot[0].shape[1]), bf16)


LOW = T - HALF + 8
MID = T // 2 // 16 * 16


def side_masks(left):
    token = lax.broadcasted_iota(jnp.int32, left.shape, 0)
    left[...] = jnp.where(token % WW < WW // 2, 1.0, 0.0).astype(bf16)


def merged(at, left, d):
    def pick(below, lo, hi):
        side = jnp.concatenate([left[lo:hi]] * (d // 128), axis=1) > 0.5
        return jnp.where(side, at(1, below, slice(lo, hi)), at(0, below, slice(lo, hi)))

    row = lax.broadcasted_iota(jnp.int32, (HALF - MID, d), 0) + MID
    middle = jnp.where(row < T // 2, pick(1, MID, HALF).astype(f32), pick(0, MID, HALF).astype(f32)).astype(bf16)
    return jnp.concatenate([pick(1, 0, MID), middle, pick(0, HALF, T)], axis=0)


class Plan:
    def __init__(self, columns, bands):
        self.c = c = columns
        self.low = low = (c + 1) // 2
        self.up = c > low
        last = ROWS - 1
        sent = [(0, r) for r in range(ROWS)]
        sent += [(x, 0) for x in range(1, min(low, c - 1) + 1)]
        sent += [(x, last) for x in range(max(low, 1), c)]
        self.first_a = sent
        self.first_b = [(x, r) for x in range(c) for r in range(ROWS) if (x, r) not in sent]
        self.to_left = [(0, r) for r in range(ROWS)]
        self.to_above = [(x, 0) for x in range(min(low, c - 1) + 1)]
        self.to_below = [(x, last) for x in range(low, c)]
        self.to_diag = (0, last) if self.up else (0, 0)
        self.rim = [(c - 1, r) for r in range(last)]
        self.lower = [(x, last) for x in range(low)]
        self.upper = [(x, -1) for x in range(low, c)]
        self.inner = [(x, r) for x in range(c - 1) for r in range(last)]
        self.extra = len(self.rim) % 2 if self.inner else 0
        self.some = self.rim + self.inner[: self.extra]
        self.rest = self.inner[self.extra :]
        self.joined = self.up and bands == 2
        self.back_right = [(c - 1, r) for r in (range(-1, last) if self.up else range(ROWS))]

    def index(self, window):
        return window[0] * ROWS + window[1]


def bring_kernel(plan, tokens, land, ocean, qkv, out, mine, sem):
    start = lax.axis_index("sub") * (plan.c * ROWS)
    copy = pltpu.make_async_copy(tokens.at[pl.ds(start, plan.c * ROWS)], mine, sem)
    copy.start()
    copy.wait()


def first_kernel(plan, which, *refs):
    windows = plan.first_b if which else plan.first_a
    tokens, land, ocean = refs[:3]
    sources, refs = refs[3:7], refs[7:]
    out, refs = refs[0], refs[1:]
    if which == 0 and plan.joined:
        (left, above, diag), refs = refs[:3], refs[3:]
        below = above
    elif which == 0:
        (left, above, below, diag), refs = refs[:4], refs[4:]
    bits, weights, slots = refs[0], refs[1:4], (refs[4:11], refs[11:18])
    pairs = paired(list(range(len(windows))))
    start = lax.axis_index("sub") * (plan.c * ROWS)
    clear_pads(slots)
    bits[...] = jnp.ones(bits.shape, f32)
    bits[:, :T] = land[...].astype(f32)
    join_weights(0, sources, weights)

    def row(j):
        return bits[pl.ds(start + plan.index(windows[j]), 1), :]

    def listed(j):
        ident = lax.axis_index("lon") * (plan.c * ROWS * lax.axis_size("sub")) + start + plan.index(windows[j])
        return jnp.max(jnp.where(ocean[...] == ident, 1.0, 0.0), axis=1, keepdims=True)

    def put(t, i, value):
        j = pairs[t][i]
        w = windows[j]
        bottom = jnp.broadcast_to(row(j).astype(bf16), (REC - TP, KP))
        ends = [(out, j, 0)]
        if which == 0:
            ends += [(left, k, 0) for k, v in enumerate(plan.to_left) if v == w]
        for to, k, _ in ends:
            to[k, :T, :] = value
            to[k, TP:, :KP] = bottom
        if which == 0:
            halves = [(above, k, 0) for k, v in enumerate(plan.to_above) if v == w]
            skip = len(plan.to_above) if plan.joined else 0
            halves += [(below, skip + k, LOW) for k, v in enumerate(plan.to_below) if v == w]
            if w == plan.to_diag:
                halves.append((diag, 0, LOW if plan.up else 0))
            for to, k, at in halves:
                end = min(at + HALF, T)
                to[k, : end - at, :] = value[at:end]
                to[k, HALF:, :KP] = bottom[: SENT - HALF]

    def load(t, i):
        return tokens[plan.index(windows[pairs[t][i]])].astype(f32)

    blocks(
        pairs, load, load, lambda t: [row(j) for j in pairs[t]], lambda t, i: listed(pairs[t][i]), put, weights, slots
    )


def second_kernel(plan, which, d, *refs):
    firsts = refs[: 2 if plan.first_b else 1]
    refs = refs[len(firsts) :]
    sources, refs = refs[:4], refs[4 + which :]
    if which == 0 and plan.joined:
        (right, above, diag), refs = refs[:3], refs[3:]
        below = above
    elif which == 0:
        (right, above, below, diag), refs = refs[:4], refs[4:]
    out, refs = refs[0], refs[1:]
    if which == 0 and plan.joined:
        (to_right, to_below, to_diag), refs = refs[:3], refs[3:]
        to_above = to_below
    elif which == 0:
        (to_right, to_below, to_above, to_diag), refs = refs[:4], refs[4:]
    skip = len(plan.lower) if plan.joined else 0
    kept, left = refs[:2]
    weights, slots = refs[2:5], (refs[5:12], refs[12:19])
    side_masks(left)
    clear_pads(slots)
    join_weights(1, sources, weights)
    c = plan.c
    windows = plan.rest if which else plan.some
    all_windows = list(windows) if which else windows + plan.lower + plan.upper

    def record(x, r):
        if r == ROWS:
            return (above, x, 0, HALF) if x < len(plan.to_above) else (diag, 0, 0, HALF)
        if r < 0:
            before = len(plan.to_above) if plan.joined else 0
            return (below, before + x - plan.low, LOW, HALF) if x < c else (diag, 0, LOW, HALF)
        if x == c:
            return right, r, 0, TP
        if (x, r) in plan.first_a:
            return firsts[0], plan.first_a.index((x, r)), 0, TP
        return firsts[1], plan.first_b.index((x, r)), 0, TP

    token = lax.broadcasted_iota(jnp.int32, (1, KP), 1)
    left_row, top_row = token % WW < WW // 2, token < T // 2

    def gathered(x, r):
        def at(i, j, rows):
            ref, k, base, _ = record(x + i, r + j)
            return ref[k, rows.start - base : rows.stop - base, :]

        return merged(at, left, d)

    def land_of(x, r):
        a, b, e, f = [
            ref[k, at : at + 16, :KP].astype(f32)[:1]
            for ref, k, _, at in (record(x + i, r + j) for j in (0, 1) for i in (0, 1))
        ]
        return jnp.where(
            token < T, jnp.where(top_row, jnp.where(left_row, f, e), jnp.where(left_row, b, a)), 1.0
        )

    def store(n, value):
        out[n] = value
        if which:
            return
        w = all_windows[n]
        if w in plan.back_right:
            to_right[plan.back_right.index(w)] = value
        if w in plan.lower:
            to_below[plan.lower.index(w)] = value[:HALF]
        if w in plan.upper:
            to_above[skip + plan.upper.index(w), : T - LOW] = value[LOW:]
        if w == (plan.back_right[0] if plan.up else plan.back_right[-1]):
            to_diag[0] = value[LOW:] if plan.up else value[:HALF]

    band, bands = lax.axis_index("lat"), lax.axis_size("lat")
    base = len(windows)
    lower_set = band < bands - 1 if plan.up else band >= 0
    on = jnp.where(lower_set, band < bands - 1, band > 0).astype(f32)

    def either(a, b):
        return jnp.where(lower_set, a.astype(f32), b.astype(f32)).astype(a.dtype)

    def window(place):
        if place[0] != "set":
            return gathered(*place)
        j = place[1]
        low = gathered(*plan.lower[j])
        return either(low, gathered(*plan.upper[min(j, len(plan.upper) - 1)])) if plan.up else low

    def land(place):
        if place[0] != "set":
            return land_of(*place)
        j = place[1]
        low = land_of(*plan.lower[j])
        return either(low, land_of(*plan.upper[min(j, len(plan.upper) - 1)])) if plan.up else low

    def finish(place, value):
        if place[0] != "set":
            return store(all_windows.index(place), value)
        j = place[1]
        if not plan.up:
            return store(base + j, value)
        store(base + j, either(value, gathered(*plan.lower[j])))
        if j < len(plan.upper):
            store(base + len(plan.lower) + j, either(gathered(*plan.upper[j]), value))

    def run(places, keep):
        pairs = paired(places)

        def load(t, i):
            value = window(pairs[t][i])
            kept[2 * (t % 3) + i] = value
            return value.astype(f32)

        def again(t, i):
            return kept[2 * (t % 3) + i].astype(f32)

        blocks(
            pairs, load, again, lambda t: [land(p) for p in pairs[t]], lambda t, i: keep(pairs[t][i]),
            lambda t, i, value: finish(pairs[t][i], value), weights, slots,
        )

    moving = [] if which else [("set", j) for j in range(len(plan.lower))]
    run(list(windows) + moving, lambda place: on if place[0] == "set" else 1.0)
    if which == 0 and plan.up and bands > 2:

        @pl.when((band > 0) & (band < bands - 1))
        def _():
            run(plan.upper, lambda place: 1.0)


def place_kernel(plan, which, d, *refs):
    (raw_c, raw_d, lefts, aboves), refs = refs[:4], refs[4:]
    (belows, refs) = (aboves, refs) if plan.joined else (refs[0], refs[1:])
    corner, refs = refs[0], refs[1 + which :]
    out, fin, left, sem_out = refs
    skip = len(plan.lower) if plan.joined else 0
    c = plan.c
    side_masks(left)
    where = {}
    for j, w in enumerate(plan.some + plan.lower + plan.upper):
        where[w] = (raw_c, j, 0)
    for j, w in enumerate(plan.rest):
        where[w] = (raw_d, j, 0)
    for k, (_, r) in enumerate(plan.back_right):
        where[-1, r] = (lefts, k, 0)
    for k, (x, _) in enumerate(plan.lower):
        where[x, -1] = (aboves, k, 0)
    for k, (x, _) in enumerate(plan.upper):
        where[x, ROWS - 1] = (belows, skip + k, LOW)
    where[(-1, ROWS - 1) if plan.up else (-1, -1)] = (corner, 0, LOW if plan.up else 0)
    me = lax.axis_index("sub")
    start = (1 - me if which else me) * (c * ROWS)
    copies = []
    for x in range(c):
        for r in range(ROWS):
            w = x * ROWS + r

            def at(i, j, rows, x=x, r=r):
                ref, k, base = where[x - i, r - j]
                return ref[k, rows.start - base : rows.stop - base, :]

            fin[w] = merged(at, left, d)
            copies.append(pltpu.make_async_copy(fin.at[w], out.at[start + w], sem_out.at[w]))
            copies[-1].start()
    for copy in copies:
        copy.wait()


def ring(value, axes, by):
    sizes = [lax.axis_size(a) for a in axes]
    total = int(np.prod(sizes))
    grid = np.arange(total).reshape(sizes)
    moved = grid
    for dim, step in enumerate(by):
        moved = np.roll(moved, -step, axis=dim)
    pairs = list(zip(grid.ravel().tolist(), moved.ravel().tolist()))
    return lax.ppermute(value, tuple(axes), pairs)


def beside(value, lat, step):
    lon, sub, lats = lax.axis_size("lon"), lax.axis_size("sub"), lax.axis_size("lat")
    ident = np.arange(lon * lats * sub).reshape(lon, lats, sub)
    line = np.transpose(ident, (1, 0, 2)).reshape(lats, lon * sub)
    axes = ("lon", "lat", "sub")
    if not lat:
        line, axes = np.arange(lon * sub)[None], ("lon", "sub")
    moved = np.roll(line, (-lat, -step), axis=(0, 1))
    return lax.ppermute(value, axes, list(zip(line.ravel().tolist(), moved.ravel().tolist())))


def call(body, ins, outs, scratch, alias, flops, limit, where):
    total = sum(int(np.prod(o.shape)) * 2 for o in outs)
    return pl.pallas_call(
        body, in_specs=ins, out_specs=[where] * len(outs), out_shape=outs, scratch_shapes=scratch,
        input_output_aliases=alias,
        compiler_params=pltpu.CompilerParams(vmem_limit_bytes=limit * 2**20),
        cost_estimate=pl.CostEstimate(flops=flops, bytes_accessed=2 * total, transcendentals=0),
    )


def shards(tokens, land_bits, ocean_list, w_qkv, w_out):
    window_count, _, d = tokens.shape
    mine = window_count // lax.axis_size("sub")
    plan = Plan(mine // ROWS, lax.axis_size("lat"))
    turned = jnp.swapaxes(w_qkv, 2, 3)
    other_qkv, other_out = ring((turned, w_out), ("sub",), (1,))
    per_window = 12_000_000_000

    def shape(*s):
        return jax.ShapeDtypeStruct(s, bf16)

    brought = call(
        functools.partial(bring_kernel, plan), [HBM] + [VMEM] * 4, [shape(mine, T, d)],
        [pltpu.SemaphoreType.DMA], {}, 1_000_000, BRING, VMEM,
    )(tokens, land_bits, ocean_list, turned, w_out)[0]
    weights = (turned, w_out, other_qkv, other_out)
    slot = [
        pltpu.VMEM((2 * TP, d), bf16), pltpu.VMEM((2 * TP, 2 * d), bf16), pltpu.VMEM((2, d, TP), bf16),
        pltpu.VMEM((2, d, TP), bf16), pltpu.VMEM((2 * TP, d), bf16), pltpu.VMEM((2, TP, 128), bf16),
        pltpu.VMEM((KP, 8), f32),
    ]
    work = [pltpu.VMEM((2 * d, d), bf16), pltpu.VMEM((d, d), bf16), pltpu.VMEM((d, d), bf16)] + slot + slot

    def first_call(which, outs):
        n = len(plan.first_b if which else plan.first_a)
        return call(
            functools.partial(first_kernel, plan, which), [VMEM] * 7, outs,
            [pltpu.VMEM((window_count, KP), f32)] + work, {}, n * per_window, LIMIT, VMEM,
        )(brought, land_bits, ocean_list, *weights)

    counts = (len(plan.to_above), max(len(plan.to_below), 1))
    halves = [shape(n, SENT, d) for n in ((sum(counts),) if plan.joined else counts) + (1,)]
    first_a, left, *bands, diag = first_call(0, [shape(len(plan.first_a), REC, d), shape(ROWS, REC, d)] + halves)
    right = beside(left, 0, -1)
    bands[0] = ring(bands[0], ("lat",), (-1,))
    if plan.up and not plan.joined:
        bands[1] = ring(bands[1], ("lat",), (1,))
    from_diag = beside(diag, 1 if plan.up else -1, -1)
    firsts = (first_a,)
    if plan.first_b:
        firsts += tuple(first_call(1, [shape(len(plan.first_b), REC, d)]))

    def second_call(which, ins, outs):
        scratch = [pltpu.VMEM((6, T, d), bf16), pltpu.VMEM((T, 128), bf16)] + work
        return call(
            functools.partial(second_kernel, plan, which, d), [VMEM] * len(ins), outs, scratch,
            {}, outs[0].shape[0] * per_window, LIMIT, VMEM,
        )(*ins)

    rim = len(plan.some) + len(plan.lower) + len(plan.upper)
    counts = (len(plan.lower), max(len(plan.upper), 1))
    backs = [shape(sum(counts), HALF, d)] if plan.joined else [shape(counts[0], HALF, d), shape(counts[1], T - LOW, d)]
    raw_c, to_right, *backs, to_diag = second_call(
        0,
        firsts + weights + (right, *bands, from_diag),
        [
            shape(rim, T, d), shape(ROWS, T, d), *backs, shape(1, T - LOW if plan.up else HALF, d),
        ],
    )
    lefts = beside(to_right, 0, 1)
    backs[0] = ring(backs[0], ("lat",), (1,))
    if plan.up and not plan.joined:
        backs[1] = ring(backs[1], ("lat",), (-1,))
    corner = beside(to_diag, -1 if plan.up else 1, 1)
    other_c = ring(raw_c, ("sub",), (1,))
    raw_d = raw_c
    if plan.rest:
        raw_d = second_call(1, firsts + weights + (to_diag,), [shape(len(plan.rest), T, d)])[0]
    other_d = ring(raw_d, ("sub",), (1,)) if plan.rest else other_c
    here = (lefts, *backs, corner)
    there = ring(here, ("sub",), (1,))

    def place_call(which, *ins):
        return call(
            functools.partial(place_kernel, plan, which, d), [VMEM] * (len(ins) - which) + [HBM] * which,
            [shape(window_count, T, d)],
            [pltpu.VMEM((mine, T, d), bf16), pltpu.VMEM((T, 128), bf16), pltpu.SemaphoreType.DMA((mine,))],
            {len(ins) - 1: 0} if which else {}, 100_000_000, LIMIT, HBM,
        )(*ins)[0]

    out = place_call(0, raw_c, raw_d, *here)
    return place_call(1, other_c, other_d, *there, out)


def solution(mesh):
    placed = (
        P(("groups", "lat", "lon"), None, None),
        P(("groups", "lat", "lon"), None),
        P(("groups", "lat"), None),
        P(None, None, None, "sub"),
        P(None, "sub", None),
    )
    return jax.shard_map(
        shards,
        mesh=mesh,
        in_specs=placed,
        out_specs=P(("groups", "lat", "lon"), None, None),
        check_vma=False,
    )
```

```python
import functools

import jax
import jax.numpy as jnp
import numpy as np
from jax import lax
from jax.experimental import pallas as pl
from jax.experimental.pallas import tpu as pltpu
from jax.sharding import PartitionSpec as P


HD = 32
WH = 10
WW = 20
T = WH * WW
ROWS = 4
TP = 208
KP = 256
LIMIT = 20
BRING = 48
REC = 224
HALF = 112
SENT = HALF + 16
NEG = -1e30
SCALE = HD**-0.5 * 1.4426950408889634
f32 = jnp.float32
bf16 = jnp.bfloat16
NT = (((1,), (1,)), ((), ()))
HBM = pl.BlockSpec(memory_space=pltpu.HBM)
ANY = pl.BlockSpec(memory_space=pl.ANY)
VMEM = pl.BlockSpec(memory_space=pltpu.VMEM)


def normed(x):
    centred = x - jnp.mean(x, axis=-1, keepdims=True)
    variance = jnp.mean(centred * centred, axis=-1, keepdims=True)
    return (centred * lax.rsqrt(variance + 1e-05)).astype(bf16)


def blocks(pairs, load, again, land_rows, keeps, put, weights, slots, heads=4, ahead=1):
    wqk, wv, wout = weights
    d = wv.shape[0]
    lane = lax.broadcasted_iota(jnp.int32, (1, 128), 1)
    masks = [jnp.where((lane >= HD * j) & (lane < HD * j + HD), 1.0, 0.0).astype(bf16) for j in range(4)]
    unit = jnp.broadcast_to(jnp.where(lane == 0, 1.0, 0.0), (TP, 128)).astype(bf16)
    ones = jnp.ones((16, TP), bf16)
    total = len(pairs)

    def before(t):
        norm, qk, values, _, _, bias, land = slots[t % 2]

        def normal(i):
            norm[i * TP : i * TP + T, :] = normed(load(t, i))

        def mask():
            rows = land_rows(t)
            land[...] = jnp.transpose(jnp.concatenate(rows + [rows[0]] * 6, axis=0))
            for i in range(2):
                bias[i] = jnp.where(lane == 0, land[:TP, i : i + 1] * NEG, 0.0).astype(bf16)

        def project(at):
            wide = lax.broadcasted_iota(jnp.int32, (1, 256), 1) + at
            got = lax.dot_general(norm[...], wqk[at : at + 256], NT, preferred_element_type=f32)
            qk[:, at : at + 256] = (got * jnp.where(wide < d, SCALE, 1.0)).astype(bf16)

        def value(i):
            got = lax.dot_general(wv[...], norm[i * TP : i * TP + TP], NT, preferred_element_type=f32)
            values[i] = got.astype(bf16)

        return (
            [functools.partial(normal, i) for i in range(2)] + [mask]
            + [functools.partial(project, at) for at in range(0, 2 * d, 256)]
            + [functools.partial(value, i) for i in range(2)]
        )

    def after(t):
        _, _, _, mixed, joined, _, land = slots[t % 2]
        held = {}

        def turn(i):
            joined[i * TP : i * TP + TP] = jnp.transpose(mixed[i])

        def out():
            held["update"] = jnp.dot(joined[...], wout[...], preferred_element_type=f32)

        def add(i):
            keep = (1.0 - land[:T, i : i + 1]) * keeps(t, i)
            put(t, i, (again(t, i) + held["update"][i * TP : i * TP + T] * keep).astype(bf16))

        return [functools.partial(turn, i) for i in range(2)] + [out] + [functools.partial(add, i) for i in range(2)]

    units = [
        (t, i, g, tuple(range(a, a + heads)))
        for t in range(total) for i in range(2) for g in range(d // 128) for a in range(0, 4, heads)
    ]
    per = len(units) // total
    scores, probs = {}, {}

    def score(u):
        t, i, g, hs = units[u]
        qk, bias = slots[t % 2][1], slots[t % 2][5]
        k = qk[i * TP : i * TP + TP, d + 128 * g : d + 128 * g + 128]
        q = jnp.concatenate([qk[i * TP : i * TP + TP, 128 * g : 128 * g + 128], unit], axis=1)
        b = bias[i]
        keyed = jnp.concatenate([jnp.concatenate([k * masks[j], b], axis=1) for j in hs], axis=0)
        got = lax.dot_general(keyed, q, NT, preferred_element_type=f32)
        scores[u] = [got[n * TP : n * TP + TP] for n in range(len(hs))]

    def soften(u):
        probs[u] = [
            jnp.exp2((s - jnp.max(s, axis=0, keepdims=True)).astype(bf16)) for s in scores.pop(u)
        ]

    def mix(u):
        t, i, g, hs = units[u]
        values, mixed = slots[t % 2][2], slots[t % 2][3]
        for j, p in zip(hs, probs.pop(u)):
            at = 128 * g + HD * j
            both = jnp.dot(
                jnp.concatenate([values[i, at : at + HD], ones], axis=0), p, preferred_element_type=f32
            )
            mixed[i, at : at + HD] = (both[:HD] * (1.0 / both[HD : HD + 1])).astype(bf16)

    for piece in before(0):
        piece()
    pieces, step, place = [], 1.0, 1
    for k in range(len(units) + 2 * ahead):
        t, at = k // per, k % per
        if at == 2 * ahead:
            pieces = (after(t - 1) if t else []) + (before(t + 1) if t + 1 < total else [])
            step, place = (per - 2 * ahead) / (len(pieces) + 1), 1
        if k < len(units):
            score(k)
        if 0 <= k - ahead < len(units):
            soften(k - ahead)
        if 0 <= k - 2 * ahead:
            mix(k - 2 * ahead)
        while pieces and (at == per - 1 or at - 2 * ahead + 1 >= place * step):
            pieces.pop(0)()
            place += 1
    for piece in pieces + after(total - 1):
        piece()


def paired(windows):
    padded = list(windows) + [windows[-1]] * (len(windows) % 2)
    return [padded[n : n + 2] for n in range(0, len(padded), 2)]


def join_weights(block, sources, weights):
    wqk, wv, wout = weights
    for n in range(2):
        qkv, out = sources[2 * n : 2 * n + 2]
        half = out.shape[1]
        rows = slice(n * half, n * half + half)
        for part in range(2):
            wqk[part * 2 * half + n * half : part * 2 * half + n * half + half] = qkv[block, part]
        wv[rows] = qkv[block, 2]
        wout[rows] = out[block]


def clear_pads(slots):
    for slot in slots:
        for i in range(2):
            slot[0][i * TP + TP - 16 : i * TP + TP, :] = jnp.zeros((16, slot[0].shape[1]), bf16)


LOW = T - HALF + 8
MID = T // 2 // 16 * 16


def side_masks(left):
    token = lax.broadcasted_iota(jnp.int32, left.shape, 0)
    left[...] = jnp.where(token % WW < WW // 2, 1.0, 0.0).astype(bf16)


def merged(at, left, d):
    def pick(below, lo, hi):
        side = jnp.concatenate([left[lo:hi]] * (d // 128), axis=1) > 0.5
        return jnp.where(side, at(1, below, slice(lo, hi)), at(0, below, slice(lo, hi)))

    row = lax.broadcasted_iota(jnp.int32, (HALF - MID, d), 0) + MID
    middle = jnp.where(row < T // 2, pick(1, MID, HALF).astype(f32), pick(0, MID, HALF).astype(f32)).astype(bf16)
    return jnp.concatenate([pick(1, 0, MID), middle, pick(0, HALF, T)], axis=0)


class Plan:
    def __init__(self, columns, bands):
        self.c = c = columns
        self.low = low = (c + 1) // 2
        self.up = c > low
        last = ROWS - 1
        sent = [(0, r) for r in range(ROWS)]
        sent += [(x, 0) for x in range(1, min(low, c - 1) + 1)]
        sent += [(x, last) for x in range(max(low, 1), c)]
        self.first_a = sent
        self.first_b = [(x, r) for x in range(c) for r in range(ROWS) if (x, r) not in sent]
        self.to_left = [(0, r) for r in range(ROWS)]
        self.to_above = [(x, 0) for x in range(min(low, c - 1) + 1)]
        self.to_below = [(x, last) for x in range(low, c)]
        self.to_diag = (0, last) if self.up else (0, 0)
        self.rim = [(c - 1, r) for r in range(last)]
        self.lower = [(x, last) for x in range(low)]
        self.upper = [(x, -1) for x in range(low, c)]
        self.inner = [(x, r) for x in range(c - 1) for r in range(last)]
        self.extra = len(self.rim) % 2 if self.inner else 0
        self.some = self.rim + self.inner[: self.extra]
        self.rest = self.inner[self.extra :]
        self.joined = self.up and bands == 2
        self.back_right = [(c - 1, r) for r in (range(-1, last) if self.up else range(ROWS))]

    def index(self, window):
        return window[0] * ROWS + window[1]


def bring_kernel(plan, tokens, land, ocean, qkv, out, mine, sem):
    start = lax.axis_index("sub") * (plan.c * ROWS)
    copy = pltpu.make_async_copy(tokens.at[pl.ds(start, plan.c * ROWS)], mine, sem)
    copy.start()
    copy.wait()


def first_kernel(plan, which, *refs):
    windows = plan.first_b if which else plan.first_a
    tokens, land, ocean = refs[:3]
    sources, refs = refs[3:7], refs[7:]
    out, refs = refs[0], refs[1:]
    if which == 0 and plan.joined:
        (left, across, diag), refs = refs[:3], refs[3:]
        above = below = refs[18]
    elif which == 0:
        (left, above, below, diag), refs = refs[:4], refs[4:]
    bits, weights, slots = refs[0], refs[1:4], (refs[4:11], refs[11:18])
    pairs = paired(list(range(len(windows))))
    start = lax.axis_index("sub") * (plan.c * ROWS)
    clear_pads(slots)
    bits[...] = jnp.ones(bits.shape, f32)
    bits[:, :T] = land[...].astype(f32)
    join_weights(0, sources, weights)

    def row(j):
        return bits[pl.ds(start + plan.index(windows[j]), 1), :]

    def listed(j):
        ident = lax.axis_index("lon") * (plan.c * ROWS * lax.axis_size("sub")) + start + plan.index(windows[j])
        return jnp.max(jnp.where(ocean[...] == ident, 1.0, 0.0), axis=1, keepdims=True)

    def put(t, i, value):
        j = pairs[t][i]
        w = windows[j]
        bottom = jnp.broadcast_to(row(j).astype(bf16), (REC - TP, KP))
        ends = [(out, j, 0)]
        if which == 0:
            ends += [(left, k, 0) for k, v in enumerate(plan.to_left) if v == w]
        for to, k, _ in ends:
            to[k, :T, :] = value
            to[k, TP:, :KP] = bottom
        if which == 0:
            halves = [(above, k, 0) for k, v in enumerate(plan.to_above) if v == w]
            skip = len(plan.to_above) if plan.joined else 0
            halves += [(below, skip + k, LOW) for k, v in enumerate(plan.to_below) if v == w]
            if w == plan.to_diag:
                halves.append((diag, 0, LOW if plan.up else 0))
            for to, k, at in halves:
                end = min(at + HALF, T)
                to[k, : end - at, :] = value[at:end]
                to[k, HALF:, :KP] = bottom[: SENT - HALF]

    def load(t, i):
        return tokens[plan.index(windows[pairs[t][i]])].astype(f32)

    blocks(
        pairs, load, load, lambda t: [row(j) for j in pairs[t]], lambda t, i: listed(pairs[t][i]), put, weights, slots
    )
    if which == 0 and plan.joined:
        for k in range(len(plan.to_above)):
            down = above[len(plan.to_above) + min(k, len(plan.to_below) - 1)].astype(f32)
            across[k] = jnp.where(lax.axis_index("lat") == 0, down, above[k].astype(f32)).astype(bf16)


def second_kernel(plan, which, d, *refs):
    firsts = refs[: 2 if plan.first_b else 1]
    refs = refs[len(firsts) :]
    sources, refs = refs[:4], refs[4 + which :]
    if which == 0 and plan.joined:
        (right, above, diag), refs = refs[:3], refs[3:]
        below = above
    elif which == 0:
        (right, above, below, diag), refs = refs[:4], refs[4:]
    out, refs = refs[0], refs[1:]
    if which == 0 and plan.joined:
        (to_right, across, to_diag, edge), refs = refs[:4], refs[4:]
    elif which == 0:
        (to_right, to_below, to_above, to_diag), refs = refs[:4], refs[4:]
    kept, left = refs[:2]
    weights, slots = refs[2:5], (refs[5:12], refs[12:19])
    side_masks(left)
    clear_pads(slots)
    join_weights(1, sources, weights)
    c = plan.c
    windows = plan.rest if which else plan.some
    all_windows = list(windows) if which else windows + plan.lower + plan.upper

    def record(x, r):
        if r == ROWS:
            return (above, x, 0, HALF) if x < len(plan.to_above) else (diag, 0, 0, HALF)
        if r < 0:
            return (below, x - plan.low, LOW, HALF) if x < c else (diag, 0, LOW, HALF)
        if x == c:
            return right, r, 0, TP
        if (x, r) in plan.first_a:
            return firsts[0], plan.first_a.index((x, r)), 0, TP
        return firsts[1], plan.first_b.index((x, r)), 0, TP

    token = lax.broadcasted_iota(jnp.int32, (1, KP), 1)
    left_row, top_row = token % WW < WW // 2, token < T // 2

    def gathered(x, r):
        def at(i, j, rows):
            ref, k, base, _ = record(x + i, r + j)
            return ref[k, rows.start - base : rows.stop - base, :]

        return merged(at, left, d)

    def land_of(x, r):
        a, b, e, f = [
            ref[k, at : at + 16, :KP].astype(f32)[:1]
            for ref, k, _, at in (record(x + i, r + j) for j in (0, 1) for i in (0, 1))
        ]
        return jnp.where(
            token < T, jnp.where(top_row, jnp.where(left_row, f, e), jnp.where(left_row, b, a)), 1.0
        )

    def store(n, value):
        out[n] = value
        if which:
            return
        w = all_windows[n]
        if w in plan.back_right:
            to_right[plan.back_right.index(w)] = value
        if w in plan.lower and not plan.joined:
            to_below[plan.lower.index(w)] = value[:HALF]
        if w in plan.upper and not plan.joined:
            to_above[plan.upper.index(w)] = value[LOW:]
        if w == (plan.back_right[0] if plan.up else plan.back_right[-1]):
            to_diag[0] = value[LOW:] if plan.up else value[:HALF]

    band, bands = lax.axis_index("lat"), lax.axis_size("lat")
    base = len(windows)
    lower_set = band < bands - 1 if plan.up else band >= 0
    on = jnp.where(lower_set, band < bands - 1, band > 0).astype(f32)

    def either(a, b):
        return jnp.where(lower_set, a.astype(f32), b.astype(f32)).astype(a.dtype)

    def window(place):
        if place[0] != "set":
            return gathered(*place)
        j = place[1]
        low = gathered(*plan.lower[j])
        return either(low, gathered(*plan.upper[min(j, len(plan.upper) - 1)])) if plan.up else low

    def land(place):
        if place[0] != "set":
            return land_of(*place)
        j = place[1]
        low = land_of(*plan.lower[j])
        return either(low, land_of(*plan.upper[min(j, len(plan.upper) - 1)])) if plan.up else low

    def finish(place, value):
        if place[0] != "set":
            return store(all_windows.index(place), value)
        j = place[1]
        if not plan.up:
            return store(base + j, value)
        if plan.joined:
            across[j, : T - LOW] = either(value[: T - LOW], value[LOW:])
            across[j, T - LOW :] = value[T - LOW : HALF]
        store(base + j, either(value, gathered(*plan.lower[j])))
        if j < len(plan.upper):
            store(base + len(plan.lower) + j, either(gathered(*plan.upper[j]), value))

    def run(places, keep):
        pairs = paired(places)

        def load(t, i):
            value = window(pairs[t][i])
            kept[2 * (t % 3) + i] = value
            return value.astype(f32)

        def again(t, i):
            return kept[2 * (t % 3) + i].astype(f32)

        blocks(
            pairs, load, again, lambda t: [land(p) for p in pairs[t]], lambda t, i: keep(pairs[t][i]),
            lambda t, i, value: finish(pairs[t][i], value), weights, slots,
        )

    if which == 0 and plan.joined:
        for x in range(c):
            (a, i, _, _), (b, j, _, _) = record(x, 0), record(x, ROWS - 1)
            edge[x] = either(a[i, :HALF, :], b[j, LOW : LOW + HALF, :])

    moving = [] if which else [("set", j) for j in range(len(plan.lower))]
    run(list(windows) + moving, lambda place: on if place[0] == "set" else 1.0)
    if which == 0 and plan.up and bands > 2:

        @pl.when((band > 0) & (band < bands - 1))
        def _():
            run(plan.upper, lambda place: 1.0)


def place_kernel(plan, which, d, *refs):
    (raw_c, raw_d, lefts, aboves), refs = refs[:4], refs[4:]
    (belows, refs) = (aboves, refs) if plan.joined else (refs[0], refs[1:])
    corner, refs = refs[0], refs[1:]
    if plan.joined:
        edge, refs = refs[0], refs[1:]
    out, fin, left, sem_out = refs[which:]
    c = plan.c
    side_masks(left)
    where = {}
    for j, w in enumerate(plan.some + plan.lower + plan.upper):
        where[w] = (raw_c, j, 0)
    for j, w in enumerate(plan.rest):
        where[w] = (raw_d, j, 0)
    for k, (_, r) in enumerate(plan.back_right):
        where[-1, r] = (lefts, k, 0)
    for k, (x, _) in enumerate(plan.lower):
        where[x, -1] = (aboves, k, 0)
    for k, (x, _) in enumerate(plan.upper):
        where[x, ROWS - 1] = (belows, k, LOW)
    where[(-1, ROWS - 1) if plan.up else (-1, -1)] = (corner, 0, LOW if plan.up else 0)
    me = lax.axis_index("sub")
    start = (1 - me if which else me) * (c * ROWS)
    copies = []

    def keep_edge(w, x, first, band):
        low = LOW if first else 0
        rows = slice(low, min(low + HALF, T))
        token = lax.broadcasted_iota(jnp.int32, (rows.stop - low, d), 0) + low
        own = (lax.axis_index("lat") == band) & (token >= first) & (token < first + T // 2)
        value = jnp.where(own, edge[x, : rows.stop - low].astype(f32), fin[w, rows].astype(f32))
        fin[w, rows] = value.astype(bf16)

    for x in range(c):
        for r in range(ROWS):
            w = x * ROWS + r

            def at(i, j, rows, x=x, r=r):
                ref, k, base = where[x - i, r - j]
                return ref[k, rows.start - base : rows.stop - base, :]

            fin[w] = merged(at, left, d)
            if plan.joined and r == 0:
                keep_edge(w, x, 0, 0)
            if plan.joined and r == ROWS - 1:
                keep_edge(w, x, T // 2, 1)
            copies.append(pltpu.make_async_copy(fin.at[w], out.at[start + w], sem_out.at[w]))
            copies[-1].start()
    for copy in copies:
        copy.wait()


def ring(value, axes, by):
    sizes = [lax.axis_size(a) for a in axes]
    total = int(np.prod(sizes))
    grid = np.arange(total).reshape(sizes)
    moved = grid
    for dim, step in enumerate(by):
        moved = np.roll(moved, -step, axis=dim)
    pairs = list(zip(grid.ravel().tolist(), moved.ravel().tolist()))
    return lax.ppermute(value, tuple(axes), pairs)


def beside(value, lat, step):
    lon, sub, lats = lax.axis_size("lon"), lax.axis_size("sub"), lax.axis_size("lat")
    ident = np.arange(lon * lats * sub).reshape(lon, lats, sub)
    line = np.transpose(ident, (1, 0, 2)).reshape(lats, lon * sub)
    axes = ("lon", "lat", "sub")
    if not lat:
        line, axes = np.arange(lon * sub)[None], ("lon", "sub")
    moved = np.roll(line, (-lat, -step), axis=(0, 1))
    return lax.ppermute(value, axes, list(zip(line.ravel().tolist(), moved.ravel().tolist())))


def call(body, ins, outs, scratch, alias, flops, limit, where):
    total = sum(int(np.prod(o.shape)) * 2 for o in outs)
    return pl.pallas_call(
        body, in_specs=ins, out_specs=[where] * len(outs), out_shape=outs, scratch_shapes=scratch,
        input_output_aliases=alias,
        compiler_params=pltpu.CompilerParams(vmem_limit_bytes=limit * 2**20),
        cost_estimate=pl.CostEstimate(flops=flops, bytes_accessed=2 * total, transcendentals=0),
    )


def shards(tokens, land_bits, ocean_list, w_qkv, w_out):
    window_count, _, d = tokens.shape
    mine = window_count // lax.axis_size("sub")
    plan = Plan(mine // ROWS, lax.axis_size("lat"))
    turned = jnp.swapaxes(w_qkv, 2, 3)
    other_qkv, other_out = ring((turned, w_out), ("sub",), (1,))
    per_window = 12_000_000_000

    def shape(*s):
        return jax.ShapeDtypeStruct(s, bf16)

    brought = call(
        functools.partial(bring_kernel, plan), [HBM] + [VMEM] * 4, [shape(mine, T, d)],
        [pltpu.SemaphoreType.DMA], {}, 1_000_000, BRING, VMEM,
    )(tokens, land_bits, ocean_list, turned, w_out)[0]
    weights = (turned, w_out, other_qkv, other_out)
    slot = [
        pltpu.VMEM((2 * TP, d), bf16), pltpu.VMEM((2 * TP, 2 * d), bf16), pltpu.VMEM((2, d, TP), bf16),
        pltpu.VMEM((2, d, TP), bf16), pltpu.VMEM((2 * TP, d), bf16), pltpu.VMEM((2, TP, 128), bf16),
        pltpu.VMEM((KP, 8), f32),
    ]
    work = [pltpu.VMEM((2 * d, d), bf16), pltpu.VMEM((d, d), bf16), pltpu.VMEM((d, d), bf16)] + slot + slot

    def first_call(which, outs):
        n = len(plan.first_b if which else plan.first_a)
        return call(
            functools.partial(first_kernel, plan, which), [VMEM] * 7, outs,
            [pltpu.VMEM((window_count, KP), f32)] + work + [pltpu.VMEM((plan.c + 1, SENT, d), bf16)], {},
            n * per_window, LIMIT, VMEM,
        )(brought, land_bits, ocean_list, *weights)

    counts = (len(plan.to_above), max(len(plan.to_below), 1))
    halves = [shape(n, SENT, d) for n in (counts[:1] if plan.joined else counts) + (1,)]
    first_a, left, *bands, diag = first_call(0, [shape(len(plan.first_a), REC, d), shape(ROWS, REC, d)] + halves)
    right = beside(left, 0, -1)
    bands[0] = ring(bands[0], ("lat",), (-1,))
    if plan.up and not plan.joined:
        bands[1] = ring(bands[1], ("lat",), (1,))
    from_diag = beside(diag, 1 if plan.up else -1, -1)
    firsts = (first_a,)
    if plan.first_b:
        firsts += tuple(first_call(1, [shape(len(plan.first_b), REC, d)]))

    def second_call(which, ins, outs):
        scratch = [pltpu.VMEM((6, T, d), bf16), pltpu.VMEM((T, 128), bf16)] + work
        return call(
            functools.partial(second_kernel, plan, which, d), [VMEM] * len(ins), outs, scratch,
            {}, outs[0].shape[0] * per_window, LIMIT, VMEM,
        )(*ins)

    rim = len(plan.some) + len(plan.lower) + len(plan.upper)
    counts = (len(plan.lower), max(len(plan.upper), 1))
    backs = [shape(counts[0], HALF, d)] if plan.joined else [shape(counts[0], HALF, d), shape(counts[1], T - LOW, d)]
    raw_c, to_right, *backs = second_call(
        0,
        firsts + weights + (right, *bands, from_diag),
        [
            shape(rim, T, d), shape(ROWS, T, d), *backs, shape(1, T - LOW if plan.up else HALF, d),
        ] + ([shape(plan.c, HALF, d)] if plan.joined else []),
    )
    edge = (backs.pop(),) if plan.joined else ()
    to_diag = backs.pop()
    lefts = beside(to_right, 0, 1)
    backs[0] = ring(backs[0], ("lat",), (1,))
    if plan.up and not plan.joined:
        backs[1] = ring(backs[1], ("lat",), (-1,))
    corner = beside(to_diag, -1 if plan.up else 1, 1)
    other_c = ring(raw_c, ("sub",), (1,))
    other_edge = (ring(edge[0], ("sub",), (1,)),) if plan.joined else ()
    raw_d = raw_c
    if plan.rest:
        raw_d = second_call(1, firsts + weights + (to_diag,), [shape(len(plan.rest), T, d)])[0]
    other_d = ring(raw_d, ("sub",), (1,)) if plan.rest else other_c
    here = (lefts, *backs, corner)
    there = ring(here, ("sub",), (1,))

    def place_call(which, *ins):
        return call(
            functools.partial(place_kernel, plan, which, d), [VMEM] * (len(ins) - which) + [HBM] * which,
            [shape(window_count, T, d)],
            [pltpu.VMEM((mine, T, d), bf16), pltpu.VMEM((T, 128), bf16), pltpu.SemaphoreType.DMA((mine,))],
            {len(ins) - 1: 0} if which else {}, 100_000_000, LIMIT, HBM,
        )(*ins)[0]

    out = place_call(0, raw_c, raw_d, *here, *edge)
    return place_call(1, other_c, other_d, *there, *other_edge, out)


def solution(mesh):
    placed = (
        P(("groups", "lat", "lon"), None, None),
        P(("groups", "lat", "lon"), None),
        P(("groups", "lat"), None),
        P(None, None, None, "sub"),
        P(None, "sub", None),
    )
    return jax.shard_map(
        shards,
        mesh=mesh,
        in_specs=placed,
        out_specs=P(("groups", "lat", "lon"), None, None),
        check_vma=False,
    )
```

```python
import functools

import jax
import jax.numpy as jnp
import numpy as np
from jax import lax
from jax.experimental import pallas as pl
from jax.experimental.pallas import tpu as pltpu
from jax.sharding import PartitionSpec as P


HD = 32
WH = 10
WW = 20
T = WH * WW
ROWS = 4
TP = 208
KP = 256
LIMIT = 20
BRING = 48
REC = 224
HALF = 112
SENT = HALF + 16
NEG = -1e30
SCALE = HD**-0.5 * 1.4426950408889634
f32 = jnp.float32
bf16 = jnp.bfloat16
NT = (((1,), (1,)), ((), ()))
HBM = pl.BlockSpec(memory_space=pltpu.HBM)
ANY = pl.BlockSpec(memory_space=pl.ANY)
VMEM = pl.BlockSpec(memory_space=pltpu.VMEM)


def normed(x):
    centred = x - jnp.mean(x, axis=-1, keepdims=True)
    variance = jnp.mean(centred * centred, axis=-1, keepdims=True)
    return (centred * lax.rsqrt(variance + 1e-05)).astype(bf16)


def blocks(pairs, load, again, land_rows, keeps, put, weights, slots, heads=4, ahead=1):
    wqk, wv, wout = weights
    d = wv.shape[0]
    lane = lax.broadcasted_iota(jnp.int32, (1, 128), 1)
    masks = [jnp.where((lane >= HD * j) & (lane < HD * j + HD), 1.0, 0.0).astype(bf16) for j in range(4)]
    unit = jnp.broadcast_to(jnp.where(lane == 0, 1.0, 0.0), (TP, 128)).astype(bf16)
    ones = jnp.ones((16, TP), bf16)
    total = len(pairs)

    def before(t):
        norm, qk, values, _, _, bias, land = slots[t % 2]

        def normal(i):
            norm[i * TP : i * TP + T, :] = normed(load(t, i))

        def mask():
            rows = land_rows(t)
            land[...] = jnp.transpose(jnp.concatenate(rows + [rows[0]] * 6, axis=0))
            for i in range(2):
                bias[i] = jnp.where(lane == 0, land[:TP, i : i + 1] * NEG, 0.0).astype(bf16)

        def project(at):
            wide = lax.broadcasted_iota(jnp.int32, (1, 256), 1) + at
            got = lax.dot_general(norm[...], wqk[at : at + 256], NT, preferred_element_type=f32)
            qk[:, at : at + 256] = (got * jnp.where(wide < d, SCALE, 1.0)).astype(bf16)

        def value(i):
            got = lax.dot_general(wv[...], norm[i * TP : i * TP + TP], NT, preferred_element_type=f32)
            values[i] = got.astype(bf16)

        return (
            [functools.partial(normal, i) for i in range(2)] + [mask]
            + [functools.partial(project, at) for at in range(0, 2 * d, 256)]
            + [functools.partial(value, i) for i in range(2)]
        )

    def after(t):
        _, _, _, mixed, joined, _, land = slots[t % 2]
        held = {}

        def turn(i):
            joined[i * TP : i * TP + TP] = jnp.transpose(mixed[i])

        def out():
            held["update"] = jnp.dot(joined[...], wout[...], preferred_element_type=f32)

        def add(i):
            keep = (1.0 - land[:T, i : i + 1]) * keeps(t, i)
            put(t, i, (again(t, i) + held["update"][i * TP : i * TP + T] * keep).astype(bf16))

        return [functools.partial(turn, i) for i in range(2)] + [out] + [functools.partial(add, i) for i in range(2)]

    units = [
        (t, i, g, tuple(range(a, a + heads)))
        for t in range(total) for i in range(2) for g in range(d // 128) for a in range(0, 4, heads)
    ]
    per = len(units) // total
    scores, probs = {}, {}

    def score(u):
        t, i, g, hs = units[u]
        qk, bias = slots[t % 2][1], slots[t % 2][5]
        k = qk[i * TP : i * TP + TP, d + 128 * g : d + 128 * g + 128]
        q = jnp.concatenate([qk[i * TP : i * TP + TP, 128 * g : 128 * g + 128], unit], axis=1)
        b = bias[i]
        keyed = jnp.concatenate([jnp.concatenate([k * masks[j], b], axis=1) for j in hs], axis=0)
        got = lax.dot_general(keyed, q, NT, preferred_element_type=f32)
        scores[u] = [got[n * TP : n * TP + TP] for n in range(len(hs))]

    def soften(u):
        probs[u] = [
            jnp.exp2((s - jnp.max(s, axis=0, keepdims=True)).astype(bf16)) for s in scores.pop(u)
        ]

    def mix(u):
        t, i, g, hs = units[u]
        values, mixed = slots[t % 2][2], slots[t % 2][3]
        for j, p in zip(hs, probs.pop(u)):
            at = 128 * g + HD * j
            both = jnp.dot(
                jnp.concatenate([values[i, at : at + HD], ones], axis=0), p, preferred_element_type=f32
            )
            mixed[i, at : at + HD] = (both[:HD] * (1.0 / both[HD : HD + 1])).astype(bf16)

    for piece in before(0):
        piece()
    pieces, step, place = [], 1.0, 1
    for k in range(len(units) + 2 * ahead):
        t, at = k // per, k % per
        if at == 2 * ahead:
            pieces = (after(t - 1) if t else []) + (before(t + 1) if t + 1 < total else [])
            step, place = (per - 2 * ahead) / (len(pieces) + 1), 1
        if k < len(units):
            score(k)
        if 0 <= k - ahead < len(units):
            soften(k - ahead)
        if 0 <= k - 2 * ahead:
            mix(k - 2 * ahead)
        while pieces and (at == per - 1 or at - 2 * ahead + 1 >= place * step):
            pieces.pop(0)()
            place += 1
    for piece in pieces + after(total - 1):
        piece()


def paired(windows):
    padded = list(windows) + [windows[-1]] * (len(windows) % 2)
    return [padded[n : n + 2] for n in range(0, len(padded), 2)]


def join_weights(block, sources, weights):
    wqk, wv, wout = weights
    for n in range(2):
        qkv, out = sources[2 * n : 2 * n + 2]
        half = out.shape[1]
        rows = slice(n * half, n * half + half)
        for part in range(2):
            wqk[part * 2 * half + n * half : part * 2 * half + n * half + half] = qkv[block, part]
        wv[rows] = qkv[block, 2]
        wout[rows] = out[block]


def clear_pads(slots):
    for slot in slots:
        for i in range(2):
            slot[0][i * TP + TP - 16 : i * TP + TP, :] = jnp.zeros((16, slot[0].shape[1]), bf16)


LOW = T - HALF + 8
MID = T // 2 // 16 * 16


def side_masks(left):
    token = lax.broadcasted_iota(jnp.int32, left.shape, 0)
    left[...] = jnp.where(token % WW < WW // 2, 1.0, 0.0).astype(bf16)


def merged(at, left, d):
    def pick(below, lo, hi):
        side = jnp.concatenate([left[lo:hi]] * (d // 128), axis=1) > 0.5
        return jnp.where(side, at(1, below, slice(lo, hi)), at(0, below, slice(lo, hi)))

    row = lax.broadcasted_iota(jnp.int32, (HALF - MID, d), 0) + MID
    middle = jnp.where(row < T // 2, pick(1, MID, HALF).astype(f32), pick(0, MID, HALF).astype(f32)).astype(bf16)
    return jnp.concatenate([pick(1, 0, MID), middle, pick(0, HALF, T)], axis=0)


class Plan:
    def __init__(self, columns, bands):
        self.c = c = columns
        self.low = low = (c + 1) // 2
        self.up = c > low
        last = ROWS - 1
        sent = [(0, r) for r in range(ROWS)]
        sent += [(x, 0) for x in range(1, min(low, c - 1) + 1)]
        sent += [(x, last) for x in range(max(low, 1), c)]
        self.first_a = sent
        self.first_b = [(x, r) for x in range(c) for r in range(ROWS) if (x, r) not in sent]
        self.to_left = [(0, r) for r in range(ROWS)]
        self.to_above = [(x, 0) for x in range(min(low, c - 1) + 1)]
        self.to_below = [(x, last) for x in range(low, c)]
        self.to_diag = (0, last) if self.up else (0, 0)
        self.rim = [(c - 1, r) for r in range(last)]
        self.lower = [(x, last) for x in range(low)]
        self.upper = [(x, -1) for x in range(low, c)]
        self.inner = [(x, r) for x in range(c - 1) for r in range(last)]
        self.extra = len(self.rim) % 2 if self.inner else 0
        self.some = self.rim + self.inner[: self.extra]
        self.rest = self.inner[self.extra :]
        self.joined = self.up and bands == 2
        self.back_right = [(c - 1, r) for r in (range(-1, last) if self.up else range(ROWS))]

    def index(self, window):
        return window[0] * ROWS + window[1]


def bring_kernel(plan, tokens, qkv, mine, sem):
    start = lax.axis_index("sub") * (plan.c * ROWS)
    copy = pltpu.make_async_copy(tokens.at[pl.ds(start, plan.c * ROWS)], mine, sem)
    copy.start()
    copy.wait()


def first_kernel(plan, which, *refs):
    windows = plan.first_b if which else plan.first_a
    tokens, land, ocean = refs[:3]
    sources, refs = refs[3:7], refs[7:]
    out, refs = refs[0], refs[1:]
    if which == 0 and plan.joined:
        (left, across, diag), refs = refs[:3], refs[3:]
        above = below = refs[18]
    elif which == 0:
        (left, above, below, diag), refs = refs[:4], refs[4:]
    bits, weights, slots = refs[0], refs[1:4], (refs[4:11], refs[11:18])
    pairs = paired(list(range(len(windows))))
    start = lax.axis_index("sub") * (plan.c * ROWS)
    clear_pads(slots)
    bits[...] = jnp.ones(bits.shape, f32)
    bits[:, :T] = land[...].astype(f32)
    join_weights(0, sources, weights)

    def row(j):
        return bits[pl.ds(start + plan.index(windows[j]), 1), :]

    def listed(j):
        ident = lax.axis_index("lon") * (plan.c * ROWS * lax.axis_size("sub")) + start + plan.index(windows[j])
        return jnp.max(jnp.where(ocean[...] == ident, 1.0, 0.0), axis=1, keepdims=True)

    def put(t, i, value):
        j = pairs[t][i]
        w = windows[j]
        bottom = jnp.broadcast_to(row(j).astype(bf16), (REC - TP, KP))
        ends = [(out, j, 0)]
        if which == 0:
            ends += [(left, k, 0) for k, v in enumerate(plan.to_left) if v == w]
        for to, k, _ in ends:
            to[k, :T, :] = value
            to[k, TP:, :KP] = bottom
        if which == 0:
            halves = [(above, k, 0) for k, v in enumerate(plan.to_above) if v == w]
            skip = len(plan.to_above) if plan.joined else 0
            halves += [(below, skip + k, LOW) for k, v in enumerate(plan.to_below) if v == w]
            if w == plan.to_diag:
                halves.append((diag, 0, LOW if plan.up else 0))
            for to, k, at in halves:
                end = min(at + HALF, T)
                to[k, : end - at, :] = value[at:end]
                to[k, HALF:, :KP] = bottom[: SENT - HALF]

    def load(t, i):
        return tokens[plan.index(windows[pairs[t][i]])].astype(f32)

    blocks(
        pairs, load, load, lambda t: [row(j) for j in pairs[t]], lambda t, i: listed(pairs[t][i]), put, weights, slots
    )
    if which == 0 and plan.joined:
        for k in range(len(plan.to_above)):
            down = above[len(plan.to_above) + min(k, len(plan.to_below) - 1)].astype(f32)
            across[k] = jnp.where(lax.axis_index("lat") == 0, down, above[k].astype(f32)).astype(bf16)


def second_kernel(plan, which, d, *refs):
    firsts = refs[: 2 if plan.first_b else 1]
    refs = refs[len(firsts) :]
    sources, refs = refs[:4], refs[4 + which :]
    if which == 0 and plan.joined:
        (right, above, diag), refs = refs[:3], refs[3:]
        below = above
    elif which == 0:
        (right, above, below, diag), refs = refs[:4], refs[4:]
    out, refs = refs[0], refs[1:]
    if which == 0 and plan.joined:
        (to_right, across, to_diag, edge), refs = refs[:4], refs[4:]
    elif which == 0:
        (to_right, to_below, to_above, to_diag), refs = refs[:4], refs[4:]
    kept, left = refs[:2]
    weights, slots = refs[2:5], (refs[5:12], refs[12:19])
    side_masks(left)
    clear_pads(slots)
    join_weights(1, sources, weights)
    c = plan.c
    windows = plan.rest if which else plan.some
    all_windows = list(windows) if which else windows + plan.lower + plan.upper

    def record(x, r):
        if r == ROWS:
            return (above, x, 0, HALF) if x < len(plan.to_above) else (diag, 0, 0, HALF)
        if r < 0:
            return (below, x - plan.low, LOW, HALF) if x < c else (diag, 0, LOW, HALF)
        if x == c:
            return right, r, 0, TP
        if (x, r) in plan.first_a:
            return firsts[0], plan.first_a.index((x, r)), 0, TP
        return firsts[1], plan.first_b.index((x, r)), 0, TP

    token = lax.broadcasted_iota(jnp.int32, (1, KP), 1)
    left_row, top_row = token % WW < WW // 2, token < T // 2

    def gathered(x, r):
        def at(i, j, rows):
            ref, k, base, _ = record(x + i, r + j)
            return ref[k, rows.start - base : rows.stop - base, :]

        return merged(at, left, d)

    def land_of(x, r):
        a, b, e, f = [
            ref[k, at : at + 16, :KP].astype(f32)[:1]
            for ref, k, _, at in (record(x + i, r + j) for j in (0, 1) for i in (0, 1))
        ]
        return jnp.where(
            token < T, jnp.where(top_row, jnp.where(left_row, f, e), jnp.where(left_row, b, a)), 1.0
        )

    def store(n, value):
        out[n] = value
        if which:
            return
        w = all_windows[n]
        if w in plan.back_right:
            to_right[plan.back_right.index(w)] = value
        if w in plan.lower and not plan.joined:
            to_below[plan.lower.index(w)] = value[:HALF]
        if w in plan.upper and not plan.joined:
            to_above[plan.upper.index(w)] = value[LOW:]
        if w == (plan.back_right[0] if plan.up else plan.back_right[-1]):
            to_diag[0] = value[LOW:] if plan.up else value[:HALF]

    band, bands = lax.axis_index("lat"), lax.axis_size("lat")
    base = len(windows)
    lower_set = band < bands - 1 if plan.up else band >= 0
    on = jnp.where(lower_set, band < bands - 1, band > 0).astype(f32)

    def either(a, b):
        return jnp.where(lower_set, a.astype(f32), b.astype(f32)).astype(a.dtype)

    def window(place):
        if place[0] != "set":
            return gathered(*place)
        j = place[1]
        low = gathered(*plan.lower[j])
        return either(low, gathered(*plan.upper[min(j, len(plan.upper) - 1)])) if plan.up else low

    def land(place):
        if place[0] != "set":
            return land_of(*place)
        j = place[1]
        low = land_of(*plan.lower[j])
        return either(low, land_of(*plan.upper[min(j, len(plan.upper) - 1)])) if plan.up else low

    def finish(place, value):
        if place[0] != "set":
            return store(all_windows.index(place), value)
        j = place[1]
        if not plan.up:
            return store(base + j, value)
        if plan.joined:
            across[j, : T - LOW] = either(value[: T - LOW], value[LOW:])
            across[j, T - LOW :] = value[T - LOW : HALF]
        store(base + j, either(value, gathered(*plan.lower[j])))
        if j < len(plan.upper):
            store(base + len(plan.lower) + j, either(gathered(*plan.upper[j]), value))

    def run(places, keep):
        pairs = paired(places)

        def load(t, i):
            value = window(pairs[t][i])
            kept[2 * (t % 3) + i] = value
            return value.astype(f32)

        def again(t, i):
            return kept[2 * (t % 3) + i].astype(f32)

        blocks(
            pairs, load, again, lambda t: [land(p) for p in pairs[t]], lambda t, i: keep(pairs[t][i]),
            lambda t, i, value: finish(pairs[t][i], value), weights, slots,
        )

    if which == 0 and plan.joined:
        for x in range(c):
            (a, i, _, _), (b, j, _, _) = record(x, 0), record(x, ROWS - 1)
            edge[x] = either(a[i, :HALF, :], b[j, LOW : LOW + HALF, :])

    moving = [] if which else [("set", j) for j in range(len(plan.lower))]
    run(list(windows) + moving, lambda place: on if place[0] == "set" else 1.0)
    if which == 0 and plan.up and bands > 2:

        @pl.when((band > 0) & (band < bands - 1))
        def _():
            run(plan.upper, lambda place: 1.0)


def place_kernel(plan, which, d, *refs):
    (raw_c, raw_d, lefts, aboves), refs = refs[:4], refs[4:]
    (belows, refs) = (aboves, refs) if plan.joined else (refs[0], refs[1:])
    corner, refs = refs[0], refs[1:]
    if plan.joined:
        edge, refs = refs[0], refs[1:]
    out, fin, left, sem_out = refs[which:]
    c = plan.c
    side_masks(left)
    where = {}
    for j, w in enumerate(plan.some + plan.lower + plan.upper):
        where[w] = (raw_c, j, 0)
    for j, w in enumerate(plan.rest):
        where[w] = (raw_d, j, 0)
    for k, (_, r) in enumerate(plan.back_right):
        where[-1, r] = (lefts, k, 0)
    for k, (x, _) in enumerate(plan.lower):
        where[x, -1] = (aboves, k, 0)
    for k, (x, _) in enumerate(plan.upper):
        where[x, ROWS - 1] = (belows, k, LOW)
    where[(-1, ROWS - 1) if plan.up else (-1, -1)] = (corner, 0, LOW if plan.up else 0)
    me = lax.axis_index("sub")
    start = (1 - me if which else me) * (c * ROWS)
    copies = []

    def keep_edge(w, x, first, band):
        low = LOW if first else 0
        rows = slice(low, min(low + HALF, T))
        token = lax.broadcasted_iota(jnp.int32, (rows.stop - low, d), 0) + low
        own = (lax.axis_index("lat") == band) & (token >= first) & (token < first + T // 2)
        value = jnp.where(own, edge[x, : rows.stop - low].astype(f32), fin[w, rows].astype(f32))
        fin[w, rows] = value.astype(bf16)

    for x in range(c):
        for r in range(ROWS):
            w = x * ROWS + r

            def at(i, j, rows, x=x, r=r):
                ref, k, base = where[x - i, r - j]
                return ref[k, rows.start - base : rows.stop - base, :]

            fin[w] = merged(at, left, d)
            if plan.joined and r == 0:
                keep_edge(w, x, 0, 0)
            if plan.joined and r == ROWS - 1:
                keep_edge(w, x, T // 2, 1)
            copies.append(pltpu.make_async_copy(fin.at[w], out.at[start + w], sem_out.at[w]))
            copies[-1].start()
    for copy in copies:
        copy.wait()


def ring(value, axes, by):
    sizes = [lax.axis_size(a) for a in axes]
    total = int(np.prod(sizes))
    grid = np.arange(total).reshape(sizes)
    moved = grid
    for dim, step in enumerate(by):
        moved = np.roll(moved, -step, axis=dim)
    pairs = list(zip(grid.ravel().tolist(), moved.ravel().tolist()))
    return lax.ppermute(value, tuple(axes), pairs)


def beside(value, lat, step):
    lon, sub, lats = lax.axis_size("lon"), lax.axis_size("sub"), lax.axis_size("lat")
    ident = np.arange(lon * lats * sub).reshape(lon, lats, sub)
    line = np.transpose(ident, (1, 0, 2)).reshape(lats, lon * sub)
    axes = ("lon", "lat", "sub")
    if not lat:
        line, axes = np.arange(lon * sub)[None], ("lon", "sub")
    moved = np.roll(line, (-lat, -step), axis=(0, 1))
    return lax.ppermute(value, axes, list(zip(line.ravel().tolist(), moved.ravel().tolist())))


def call(body, ins, outs, scratch, alias, flops, limit, where):
    total = sum(int(np.prod(o.shape)) * 2 for o in outs)
    return pl.pallas_call(
        body, in_specs=ins, out_specs=[where] * len(outs), out_shape=outs, scratch_shapes=scratch,
        input_output_aliases=alias,
        compiler_params=pltpu.CompilerParams(vmem_limit_bytes=limit * 2**20),
        cost_estimate=pl.CostEstimate(flops=flops, bytes_accessed=2 * total, transcendentals=0),
    )


def shards(tokens, land_bits, ocean_list, w_qkv, w_out):
    window_count, _, d = tokens.shape
    mine = window_count // lax.axis_size("sub")
    plan = Plan(mine // ROWS, lax.axis_size("lat"))
    turned = jnp.swapaxes(w_qkv, 2, 3)
    other_qkv, other_out = ring((turned, w_out), ("sub",), (1,))
    per_window = 12_000_000_000

    def shape(*s):
        return jax.ShapeDtypeStruct(s, bf16)

    brought = call(
        functools.partial(bring_kernel, plan), [HBM, VMEM], [shape(mine, T, d)],
        [pltpu.SemaphoreType.DMA], {}, 1_000_000, BRING, VMEM,
    )(tokens, turned)[0]
    weights = (turned, w_out, other_qkv, other_out)
    slot = [
        pltpu.VMEM((2 * TP, d), bf16), pltpu.VMEM((2 * TP, 2 * d), bf16), pltpu.VMEM((2, d, TP), bf16),
        pltpu.VMEM((2, d, TP), bf16), pltpu.VMEM((2 * TP, d), bf16), pltpu.VMEM((2, TP, 128), bf16),
        pltpu.VMEM((KP, 8), f32),
    ]
    work = [pltpu.VMEM((2 * d, d), bf16), pltpu.VMEM((d, d), bf16), pltpu.VMEM((d, d), bf16)] + slot + slot

    def first_call(which, outs):
        n = len(plan.first_b if which else plan.first_a)
        return call(
            functools.partial(first_kernel, plan, which), [VMEM] * 7, outs,
            [pltpu.VMEM((window_count, KP), f32)] + work + [pltpu.VMEM((plan.c + 1, SENT, d), bf16)], {},
            n * per_window, LIMIT, VMEM,
        )(brought, land_bits, ocean_list, *weights)

    counts = (len(plan.to_above), max(len(plan.to_below), 1))
    halves = [shape(n, SENT, d) for n in (counts[:1] if plan.joined else counts) + (1,)]
    first_a, left, *bands, diag = first_call(0, [shape(len(plan.first_a), REC, d), shape(ROWS, REC, d)] + halves)
    right = beside(left, 0, -1)
    bands[0] = ring(bands[0], ("lat",), (-1,))
    if plan.up and not plan.joined:
        bands[1] = ring(bands[1], ("lat",), (1,))
    from_diag = beside(diag, 1 if plan.up else -1, -1)
    firsts = (first_a,)
    if plan.first_b:
        firsts += tuple(first_call(1, [shape(len(plan.first_b), REC, d)]))

    def second_call(which, ins, outs):
        scratch = [pltpu.VMEM((6, T, d), bf16), pltpu.VMEM((T, 128), bf16)] + work
        return call(
            functools.partial(second_kernel, plan, which, d), [VMEM] * len(ins), outs, scratch,
            {}, outs[0].shape[0] * per_window, LIMIT, VMEM,
        )(*ins)

    rim = len(plan.some) + len(plan.lower) + len(plan.upper)
    counts = (len(plan.lower), max(len(plan.upper), 1))
    backs = [shape(counts[0], HALF, d)] if plan.joined else [shape(counts[0], HALF, d), shape(counts[1], T - LOW, d)]
    raw_c, to_right, *backs = second_call(
        0,
        firsts + weights + (right, *bands, from_diag),
        [
            shape(rim, T, d), shape(ROWS, T, d), *backs, shape(1, T - LOW if plan.up else HALF, d),
        ] + ([shape(plan.c, HALF, d)] if plan.joined else []),
    )
    edge = (backs.pop(),) if plan.joined else ()
    to_diag = backs.pop()
    lefts = beside(to_right, 0, 1)
    backs[0] = ring(backs[0], ("lat",), (1,))
    if plan.up and not plan.joined:
        backs[1] = ring(backs[1], ("lat",), (-1,))
    corner = beside(to_diag, -1 if plan.up else 1, 1)
    other_c = ring(raw_c, ("sub",), (1,))
    other_edge = (ring(edge[0], ("sub",), (1,)),) if plan.joined else ()
    raw_d = raw_c
    if plan.rest:
        raw_d = second_call(1, firsts + weights + (to_diag,), [shape(len(plan.rest), T, d)])[0]
    other_d = ring(raw_d, ("sub",), (1,)) if plan.rest else other_c
    here = (lefts, *backs, corner)
    there = ring(here, ("sub",), (1,))

    def place_call(which, *ins):
        return call(
            functools.partial(place_kernel, plan, which, d), [VMEM] * (len(ins) - which) + [HBM] * which,
            [shape(window_count, T, d)],
            [pltpu.VMEM((mine, T, d), bf16), pltpu.VMEM((T, 128), bf16), pltpu.SemaphoreType.DMA((mine,))],
            {len(ins) - 1: 0} if which else {}, 100_000_000, LIMIT, HBM,
        )(*ins)[0]

    out = place_call(0, raw_c, raw_d, *here, *edge)
    return place_call(1, other_c, other_d, *there, *other_edge, out)


def solution(mesh):
    placed = (
        P(("groups", "lat", "lon"), None, None),
        P(("groups", "lat", "lon"), None),
        P(("groups", "lat"), None),
        P(None, None, None, "sub"),
        P(None, "sub", None),
    )
    return jax.shard_map(
        shards,
        mesh=mesh,
        in_specs=placed,
        out_specs=P(("groups", "lat", "lon"), None, None),
        check_vma=False,
    )
```

```python
import functools

import jax
import jax.numpy as jnp
import numpy as np
from jax import lax
from jax.experimental import pallas as pl
from jax.experimental.pallas import tpu as pltpu
from jax.sharding import PartitionSpec as P


HD = 32
WH = 10
WW = 20
T = WH * WW
ROWS = 4
TP = 208
KP = 256
LIMIT = 20
BRING = 48
REC = 224
HALF = 112
SENT = HALF + 16
NEG = -1e30
SCALE = HD**-0.5 * 1.4426950408889634
f32 = jnp.float32
bf16 = jnp.bfloat16
NT = (((1,), (1,)), ((), ()))
HBM = pl.BlockSpec(memory_space=pltpu.HBM)
ANY = pl.BlockSpec(memory_space=pl.ANY)
VMEM = pl.BlockSpec(memory_space=pltpu.VMEM)


def normed(x):
    centred = x - jnp.mean(x, axis=-1, keepdims=True)
    variance = jnp.mean(centred * centred, axis=-1, keepdims=True)
    return (centred * lax.rsqrt(variance + 1e-05)).astype(bf16)


def blocks(pairs, load, again, land_rows, keeps, put, weights, slots, heads=4, ahead=1):
    wqk, wv, wout = weights
    d = wv.shape[0]
    lane = lax.broadcasted_iota(jnp.int32, (1, 128), 1)
    masks = [jnp.where((lane >= HD * j) & (lane < HD * j + HD), 1.0, 0.0).astype(bf16) for j in range(4)]
    unit = jnp.broadcast_to(jnp.where(lane == 0, 1.0, 0.0), (TP, 128)).astype(bf16)
    ones = jnp.ones((16, TP), bf16)
    total = len(pairs)

    def before(t):
        norm, qk, values, _, _, bias, land = slots[t % 2]

        def normal(i):
            norm[i * TP : i * TP + T, :] = normed(load(t, i))

        def mask():
            rows = land_rows(t)
            land[...] = jnp.transpose(jnp.concatenate(rows + [rows[0]] * 6, axis=0))
            for i in range(2):
                bias[i] = jnp.where(lane == 0, land[:TP, i : i + 1] * NEG, 0.0).astype(bf16)

        def project(at):
            wide = lax.broadcasted_iota(jnp.int32, (1, 256), 1) + at
            got = lax.dot_general(norm[...], wqk[at : at + 256], NT, preferred_element_type=f32)
            qk[:, at : at + 256] = (got * jnp.where(wide < d, SCALE, 1.0)).astype(bf16)

        def value(i):
            got = lax.dot_general(wv[...], norm[i * TP : i * TP + TP], NT, preferred_element_type=f32)
            values[i] = got.astype(bf16)

        return (
            [functools.partial(normal, i) for i in range(2)] + [mask]
            + [functools.partial(project, at) for at in range(0, 2 * d, 256)]
            + [functools.partial(value, i) for i in range(2)]
        )

    def after(t):
        _, _, _, mixed, joined, _, land = slots[t % 2]
        held = {}

        def turn(i):
            joined[i * TP : i * TP + TP] = jnp.transpose(mixed[i])

        def out():
            held["update"] = jnp.dot(joined[...], wout[...], preferred_element_type=f32)

        def add(i):
            keep = (1.0 - land[:T, i : i + 1]) * keeps(t, i)
            put(t, i, (again(t, i) + held["update"][i * TP : i * TP + T] * keep).astype(bf16))

        return [functools.partial(turn, i) for i in range(2)] + [out] + [functools.partial(add, i) for i in range(2)]

    units = [
        (t, i, g, tuple(range(a, a + heads)))
        for t in range(total) for i in range(2) for g in range(d // 128) for a in range(0, 4, heads)
    ]
    per = len(units) // total
    scores, probs = {}, {}

    def score(u):
        t, i, g, hs = units[u]
        qk, bias = slots[t % 2][1], slots[t % 2][5]
        k = qk[i * TP : i * TP + TP, d + 128 * g : d + 128 * g + 128]
        q = jnp.concatenate([qk[i * TP : i * TP + TP, 128 * g : 128 * g + 128], unit], axis=1)
        b = bias[i]
        keyed = jnp.concatenate([jnp.concatenate([k * masks[j], b], axis=1) for j in hs], axis=0)
        got = lax.dot_general(keyed, q, NT, preferred_element_type=f32)
        scores[u] = [got[n * TP : n * TP + TP] for n in range(len(hs))]

    def soften(u):
        probs[u] = [
            jnp.exp2((s - jnp.max(s, axis=0, keepdims=True)).astype(bf16)) for s in scores.pop(u)
        ]

    def mix(u):
        t, i, g, hs = units[u]
        values, mixed = slots[t % 2][2], slots[t % 2][3]
        for j, p in zip(hs, probs.pop(u)):
            at = 128 * g + HD * j
            both = jnp.dot(
                jnp.concatenate([values[i, at : at + HD], ones], axis=0), p, preferred_element_type=f32
            )
            mixed[i, at : at + HD] = (both[:HD] * (1.0 / both[HD : HD + 1])).astype(bf16)

    for piece in before(0):
        piece()
    pieces, step, place = [], 1.0, 1
    for k in range(len(units) + 2 * ahead):
        t, at = k // per, k % per
        if at == 2 * ahead:
            pieces = (after(t - 1) if t else []) + (before(t + 1) if t + 1 < total else [])
            step, place = (per - 2 * ahead) / (len(pieces) + 1), 1
        if k < len(units):
            score(k)
        if 0 <= k - ahead < len(units):
            soften(k - ahead)
        if 0 <= k - 2 * ahead:
            mix(k - 2 * ahead)
        while pieces and (at == per - 1 or at - 2 * ahead + 1 >= place * step):
            pieces.pop(0)()
            place += 1
    for piece in pieces + after(total - 1):
        piece()


def paired(windows):
    padded = list(windows) + [windows[-1]] * (len(windows) % 2)
    return [padded[n : n + 2] for n in range(0, len(padded), 2)]


def join_weights(block, sources, weights):
    wqk, wv, wout = weights
    for n in range(2):
        qkv, out = sources[2 * n : 2 * n + 2]
        half = out.shape[1]
        rows = slice(n * half, n * half + half)
        for part in range(2):
            wqk[part * 2 * half + n * half : part * 2 * half + n * half + half] = qkv[block, part]
        wv[rows] = qkv[block, 2]
        wout[rows] = out[block]


def clear_pads(slots):
    for slot in slots:
        for i in range(2):
            slot[0][i * TP + TP - 16 : i * TP + TP, :] = jnp.zeros((16, slot[0].shape[1]), bf16)


LOW = T - HALF + 8
MID = T // 2 // 16 * 16


def side_masks(left):
    token = lax.broadcasted_iota(jnp.int32, left.shape, 0)
    left[...] = jnp.where(token % WW < WW // 2, 1.0, 0.0).astype(bf16)


def merged(at, left, d):
    def pick(below, lo, hi):
        side = jnp.concatenate([left[lo:hi]] * (d // 128), axis=1) > 0.5
        return jnp.where(side, at(1, below, slice(lo, hi)), at(0, below, slice(lo, hi)))

    row = lax.broadcasted_iota(jnp.int32, (HALF - MID, d), 0) + MID
    middle = jnp.where(row < T // 2, pick(1, MID, HALF).astype(f32), pick(0, MID, HALF).astype(f32)).astype(bf16)
    return jnp.concatenate([pick(1, 0, MID), middle, pick(0, HALF, T)], axis=0)


class Plan:
    def __init__(self, columns, bands):
        self.c = c = columns
        self.low = low = (c + 1) // 2
        self.up = c > low
        last = ROWS - 1
        sent = [(0, r) for r in range(ROWS)]
        sent += [(x, 0) for x in range(1, min(low, c - 1) + 1)]
        sent += [(x, last) for x in range(max(low, 1), c)]
        self.first_a = sent
        self.first_b = [(x, r) for x in range(c) for r in range(ROWS) if (x, r) not in sent]
        self.to_left = [(0, r) for r in range(ROWS)]
        self.to_above = [(x, 0) for x in range(min(low, c - 1) + 1)]
        self.to_below = [(x, last) for x in range(low, c)]
        self.to_diag = (0, last) if self.up else (0, 0)
        self.rim = [(c - 1, r) for r in range(last)]
        self.lower = [(x, last) for x in range(low)]
        self.upper = [(x, -1) for x in range(low, c)]
        self.inner = [(x, r) for x in range(c - 1) for r in range(last)]
        self.extra = len(self.rim) % 2 if self.inner else 0
        self.some = self.rim + self.inner[: self.extra]
        self.rest = self.inner[self.extra :]
        self.joined = self.up and bands == 2
        self.back_right = [(c - 1, r) for r in (range(-1, last) if self.up else range(ROWS))]

    def index(self, window):
        return window[0] * ROWS + window[1]


def bring_kernel(plan, tokens, mine, sem):
    start = lax.axis_index("sub") * (plan.c * ROWS)
    copy = pltpu.make_async_copy(tokens.at[pl.ds(start, plan.c * ROWS)], mine, sem)
    copy.start()
    copy.wait()


def first_kernel(plan, which, *refs):
    windows = plan.first_b if which else plan.first_a
    tokens, land, ocean = refs[:3]
    sources, refs = refs[3:7], refs[7:]
    out, refs = refs[0], refs[1:]
    if which == 0 and plan.joined:
        (left, across, diag), refs = refs[:3], refs[3:]
        above = below = refs[18]
    elif which == 0:
        (left, above, below, diag), refs = refs[:4], refs[4:]
    bits, weights, slots = refs[0], refs[1:4], (refs[4:11], refs[11:18])
    pairs = paired(list(range(len(windows))))
    start = lax.axis_index("sub") * (plan.c * ROWS)
    clear_pads(slots)
    bits[...] = jnp.ones(bits.shape, f32)
    bits[:, :T] = land[...].astype(f32)
    join_weights(0, sources, weights)

    def row(j):
        return bits[pl.ds(start + plan.index(windows[j]), 1), :]

    def listed(j):
        ident = lax.axis_index("lon") * (plan.c * ROWS * lax.axis_size("sub")) + start + plan.index(windows[j])
        return jnp.max(jnp.where(ocean[...] == ident, 1.0, 0.0), axis=1, keepdims=True)

    def put(t, i, value):
        j = pairs[t][i]
        w = windows[j]
        bottom = jnp.broadcast_to(row(j).astype(bf16), (REC - TP, KP))
        ends = [(out, j, 0)]
        if which == 0:
            ends += [(left, k, 0) for k, v in enumerate(plan.to_left) if v == w]
        for to, k, _ in ends:
            to[k, :T, :] = value
            to[k, TP:, :KP] = bottom
        if which == 0:
            halves = [(above, k, 0) for k, v in enumerate(plan.to_above) if v == w]
            skip = len(plan.to_above) if plan.joined else 0
            halves += [(below, skip + k, LOW) for k, v in enumerate(plan.to_below) if v == w]
            if w == plan.to_diag:
                halves.append((diag, 0, LOW if plan.up else 0))
            for to, k, at in halves:
                end = min(at + HALF, T)
                to[k, : end - at, :] = value[at:end]
                to[k, HALF:, :KP] = bottom[: SENT - HALF]

    def load(t, i):
        return tokens[plan.index(windows[pairs[t][i]])].astype(f32)

    blocks(
        pairs, load, load, lambda t: [row(j) for j in pairs[t]], lambda t, i: listed(pairs[t][i]), put, weights, slots
    )
    if which == 0 and plan.joined:
        for k in range(len(plan.to_above)):
            down = above[len(plan.to_above) + min(k, len(plan.to_below) - 1)].astype(f32)
            across[k] = jnp.where(lax.axis_index("lat") == 0, down, above[k].astype(f32)).astype(bf16)


def second_kernel(plan, which, d, *refs):
    firsts = refs[: 2 if plan.first_b else 1]
    refs = refs[len(firsts) :]
    sources, refs = refs[:4], refs[4 + which :]
    if which == 0 and plan.joined:
        (right, above, diag), refs = refs[:3], refs[3:]
        below = above
    elif which == 0:
        (right, above, below, diag), refs = refs[:4], refs[4:]
    out, refs = refs[0], refs[1:]
    if which == 0 and plan.joined:
        (to_right, across, to_diag, edge), refs = refs[:4], refs[4:]
    elif which == 0:
        (to_right, to_below, to_above, to_diag), refs = refs[:4], refs[4:]
    kept, left = refs[:2]
    weights, slots = refs[2:5], (refs[5:12], refs[12:19])
    side_masks(left)
    clear_pads(slots)
    join_weights(1, sources, weights)
    c = plan.c
    windows = plan.rest if which else plan.some
    all_windows = list(windows) if which else windows + plan.lower + plan.upper

    def record(x, r):
        if r == ROWS:
            return (above, x, 0, HALF) if x < len(plan.to_above) else (diag, 0, 0, HALF)
        if r < 0:
            return (below, x - plan.low, LOW, HALF) if x < c else (diag, 0, LOW, HALF)
        if x == c:
            return right, r, 0, TP
        if (x, r) in plan.first_a:
            return firsts[0], plan.first_a.index((x, r)), 0, TP
        return firsts[1], plan.first_b.index((x, r)), 0, TP

    token = lax.broadcasted_iota(jnp.int32, (1, KP), 1)
    left_row, top_row = token % WW < WW // 2, token < T // 2

    def gathered(x, r):
        def at(i, j, rows):
            ref, k, base, _ = record(x + i, r + j)
            return ref[k, rows.start - base : rows.stop - base, :]

        return merged(at, left, d)

    def land_of(x, r):
        a, b, e, f = [
            ref[k, at : at + 16, :KP].astype(f32)[:1]
            for ref, k, _, at in (record(x + i, r + j) for j in (0, 1) for i in (0, 1))
        ]
        return jnp.where(
            token < T, jnp.where(top_row, jnp.where(left_row, f, e), jnp.where(left_row, b, a)), 1.0
        )

    def store(n, value):
        out[n] = value
        if which:
            return
        w = all_windows[n]
        if w in plan.back_right:
            to_right[plan.back_right.index(w)] = value
        if w in plan.lower and not plan.joined:
            to_below[plan.lower.index(w)] = value[:HALF]
        if w in plan.upper and not plan.joined:
            to_above[plan.upper.index(w)] = value[LOW:]
        if w == (plan.back_right[0] if plan.up else plan.back_right[-1]):
            to_diag[0] = value[LOW:] if plan.up else value[:HALF]

    band, bands = lax.axis_index("lat"), lax.axis_size("lat")
    base = len(windows)
    lower_set = band < bands - 1 if plan.up else band >= 0
    on = jnp.where(lower_set, band < bands - 1, band > 0).astype(f32)

    def either(a, b):
        return jnp.where(lower_set, a.astype(f32), b.astype(f32)).astype(a.dtype)

    def window(place):
        if place[0] != "set":
            return gathered(*place)
        j = place[1]
        low = gathered(*plan.lower[j])
        return either(low, gathered(*plan.upper[min(j, len(plan.upper) - 1)])) if plan.up else low

    def land(place):
        if place[0] != "set":
            return land_of(*place)
        j = place[1]
        low = land_of(*plan.lower[j])
        return either(low, land_of(*plan.upper[min(j, len(plan.upper) - 1)])) if plan.up else low

    def finish(place, value):
        if place[0] != "set":
            return store(all_windows.index(place), value)
        j = place[1]
        if not plan.up:
            return store(base + j, value)
        if plan.joined:
            across[j, : T - LOW] = either(value[: T - LOW], value[LOW:])
            across[j, T - LOW :] = value[T - LOW : HALF]
        store(base + j, either(value, gathered(*plan.lower[j])))
        if j < len(plan.upper):
            store(base + len(plan.lower) + j, either(gathered(*plan.upper[j]), value))

    def run(places, keep):
        pairs = paired(places)

        def load(t, i):
            value = window(pairs[t][i])
            kept[2 * (t % 3) + i] = value
            return value.astype(f32)

        def again(t, i):
            return kept[2 * (t % 3) + i].astype(f32)

        blocks(
            pairs, load, again, lambda t: [land(p) for p in pairs[t]], lambda t, i: keep(pairs[t][i]),
            lambda t, i, value: finish(pairs[t][i], value), weights, slots,
        )

    if which == 0 and plan.joined:
        for x in range(c):
            (a, i, _, _), (b, j, _, _) = record(x, 0), record(x, ROWS - 1)
            edge[x] = either(a[i, :HALF, :], b[j, LOW : LOW + HALF, :])

    moving = [] if which else [("set", j) for j in range(len(plan.lower))]
    run(list(windows) + moving, lambda place: on if place[0] == "set" else 1.0)
    if which == 0 and plan.up and bands > 2:

        @pl.when((band > 0) & (band < bands - 1))
        def _():
            run(plan.upper, lambda place: 1.0)


def place_kernel(plan, which, d, *refs):
    (raw_c, raw_d, lefts, aboves), refs = refs[:4], refs[4:]
    (belows, refs) = (aboves, refs) if plan.joined else (refs[0], refs[1:])
    corner, refs = refs[0], refs[1:]
    if plan.joined:
        edge, refs = refs[0], refs[1:]
    out, fin, left, sem_out = refs[which:]
    c = plan.c
    side_masks(left)
    where = {}
    for j, w in enumerate(plan.some + plan.lower + plan.upper):
        where[w] = (raw_c, j, 0)
    for j, w in enumerate(plan.rest):
        where[w] = (raw_d, j, 0)
    for k, (_, r) in enumerate(plan.back_right):
        where[-1, r] = (lefts, k, 0)
    for k, (x, _) in enumerate(plan.lower):
        where[x, -1] = (aboves, k, 0)
    for k, (x, _) in enumerate(plan.upper):
        where[x, ROWS - 1] = (belows, k, LOW)
    where[(-1, ROWS - 1) if plan.up else (-1, -1)] = (corner, 0, LOW if plan.up else 0)
    me = lax.axis_index("sub")
    start = (1 - me if which else me) * (c * ROWS)
    copies = []

    def keep_edge(w, x, first, band):
        low = LOW if first else 0
        rows = slice(low, min(low + HALF, T))
        token = lax.broadcasted_iota(jnp.int32, (rows.stop - low, d), 0) + low
        own = (lax.axis_index("lat") == band) & (token >= first) & (token < first + T // 2)
        value = jnp.where(own, edge[x, : rows.stop - low].astype(f32), fin[w, rows].astype(f32))
        fin[w, rows] = value.astype(bf16)

    for x in range(c):
        for r in range(ROWS):
            w = x * ROWS + r

            def at(i, j, rows, x=x, r=r):
                ref, k, base = where[x - i, r - j]
                return ref[k, rows.start - base : rows.stop - base, :]

            fin[w] = merged(at, left, d)
            if plan.joined and r == 0:
                keep_edge(w, x, 0, 0)
            if plan.joined and r == ROWS - 1:
                keep_edge(w, x, T // 2, 1)
            copies.append(pltpu.make_async_copy(fin.at[w], out.at[start + w], sem_out.at[w]))
            copies[-1].start()
    for copy in copies:
        copy.wait()


def ring(value, axes, by):
    sizes = [lax.axis_size(a) for a in axes]
    total = int(np.prod(sizes))
    grid = np.arange(total).reshape(sizes)
    moved = grid
    for dim, step in enumerate(by):
        moved = np.roll(moved, -step, axis=dim)
    pairs = list(zip(grid.ravel().tolist(), moved.ravel().tolist()))
    return lax.ppermute(value, tuple(axes), pairs)


def beside(value, lat, step):
    lon, sub, lats = lax.axis_size("lon"), lax.axis_size("sub"), lax.axis_size("lat")
    ident = np.arange(lon * lats * sub).reshape(lon, lats, sub)
    line = np.transpose(ident, (1, 0, 2)).reshape(lats, lon * sub)
    axes = ("lon", "lat", "sub")
    if not lat:
        line, axes = np.arange(lon * sub)[None], ("lon", "sub")
    moved = np.roll(line, (-lat, -step), axis=(0, 1))
    return lax.ppermute(value, axes, list(zip(line.ravel().tolist(), moved.ravel().tolist())))


def call(body, ins, outs, scratch, alias, flops, limit, where):
    total = sum(int(np.prod(o.shape)) * 2 for o in outs)
    return pl.pallas_call(
        body, in_specs=ins, out_specs=[where] * len(outs), out_shape=outs, scratch_shapes=scratch,
        input_output_aliases=alias,
        compiler_params=pltpu.CompilerParams(vmem_limit_bytes=limit * 2**20),
        cost_estimate=pl.CostEstimate(flops=flops, bytes_accessed=2 * total, transcendentals=0),
    )


def shards(tokens, land_bits, ocean_list, w_qkv, w_out):
    window_count, _, d = tokens.shape
    mine = window_count // lax.axis_size("sub")
    plan = Plan(mine // ROWS, lax.axis_size("lat"))
    turned = jnp.swapaxes(w_qkv, 2, 3)
    other_qkv, other_out = ring((turned, w_out), ("sub",), (1,))
    per_window = 12_000_000_000

    def shape(*s):
        return jax.ShapeDtypeStruct(s, bf16)

    brought = call(
        functools.partial(bring_kernel, plan), [HBM], [shape(mine, T, d)],
        [pltpu.SemaphoreType.DMA], {}, 1_000_000, BRING, VMEM,
    )(tokens)[0]
    weights = (turned, w_out, other_qkv, other_out)
    slot = [
        pltpu.VMEM((2 * TP, d), bf16), pltpu.VMEM((2 * TP, 2 * d), bf16), pltpu.VMEM((2, d, TP), bf16),
        pltpu.VMEM((2, d, TP), bf16), pltpu.VMEM((2 * TP, d), bf16), pltpu.VMEM((2, TP, 128), bf16),
        pltpu.VMEM((KP, 8), f32),
    ]
    work = [pltpu.VMEM((2 * d, d), bf16), pltpu.VMEM((d, d), bf16), pltpu.VMEM((d, d), bf16)] + slot + slot

    def first_call(which, outs):
        n = len(plan.first_b if which else plan.first_a)
        return call(
            functools.partial(first_kernel, plan, which), [VMEM] * 7, outs,
            [pltpu.VMEM((window_count, KP), f32)] + work + [pltpu.VMEM((plan.c + 1, SENT, d), bf16)], {},
            n * per_window, LIMIT, VMEM,
        )(brought, land_bits, ocean_list, *weights)

    counts = (len(plan.to_above), max(len(plan.to_below), 1))
    halves = [shape(n, SENT, d) for n in (counts[:1] if plan.joined else counts) + (1,)]
    first_a, left, *bands, diag = first_call(0, [shape(len(plan.first_a), REC, d), shape(ROWS, REC, d)] + halves)
    right = beside(left, 0, -1)
    bands[0] = ring(bands[0], ("lat",), (-1,))
    if plan.up and not plan.joined:
        bands[1] = ring(bands[1], ("lat",), (1,))
    from_diag = beside(diag, 1 if plan.up else -1, -1)
    firsts = (first_a,)
    if plan.first_b:
        firsts += tuple(first_call(1, [shape(len(plan.first_b), REC, d)]))

    def second_call(which, ins, outs):
        scratch = [pltpu.VMEM((6, T, d), bf16), pltpu.VMEM((T, 128), bf16)] + work
        return call(
            functools.partial(second_kernel, plan, which, d), [VMEM] * len(ins), outs, scratch,
            {}, outs[0].shape[0] * per_window, LIMIT, VMEM,
        )(*ins)

    rim = len(plan.some) + len(plan.lower) + len(plan.upper)
    counts = (len(plan.lower), max(len(plan.upper), 1))
    backs = [shape(counts[0], HALF, d)] if plan.joined else [shape(counts[0], HALF, d), shape(counts[1], T - LOW, d)]
    raw_c, to_right, *backs = second_call(
        0,
        firsts + weights + (right, *bands, from_diag),
        [
            shape(rim, T, d), shape(ROWS, T, d), *backs, shape(1, T - LOW if plan.up else HALF, d),
        ] + ([shape(plan.c, HALF, d)] if plan.joined else []),
    )
    edge = (backs.pop(),) if plan.joined else ()
    to_diag = backs.pop()
    lefts = beside(to_right, 0, 1)
    backs[0] = ring(backs[0], ("lat",), (1,))
    if plan.up and not plan.joined:
        backs[1] = ring(backs[1], ("lat",), (-1,))
    corner = beside(to_diag, -1 if plan.up else 1, 1)
    other_c = ring(raw_c, ("sub",), (1,))
    other_edge = (ring(edge[0], ("sub",), (1,)),) if plan.joined else ()
    raw_d = raw_c
    if plan.rest:
        raw_d = second_call(1, firsts + weights + (to_diag,), [shape(len(plan.rest), T, d)])[0]
    other_d = ring(raw_d, ("sub",), (1,)) if plan.rest else other_c
    here = (lefts, *backs, corner)
    there = ring(here, ("sub",), (1,))

    def place_call(which, *ins):
        return call(
            functools.partial(place_kernel, plan, which, d), [VMEM] * (len(ins) - which) + [HBM] * which,
            [shape(window_count, T, d)],
            [pltpu.VMEM((mine, T, d), bf16), pltpu.VMEM((T, 128), bf16), pltpu.SemaphoreType.DMA((mine,))],
            {len(ins) - 1: 0} if which else {}, 100_000_000, LIMIT, HBM,
        )(*ins)[0]

    out = place_call(0, raw_c, raw_d, *here, *edge)
    return place_call(1, other_c, other_d, *there, *other_edge, out)


def solution(mesh):
    placed = (
        P(("groups", "lat", "lon"), None, None),
        P(("groups", "lat", "lon"), None),
        P(("groups", "lat"), None),
        P(None, None, None, "sub"),
        P(None, "sub", None),
    )
    return jax.shard_map(
        shards,
        mesh=mesh,
        in_specs=placed,
        out_specs=P(("groups", "lat", "lon"), None, None),
        check_vma=False,
    )
```
